32 devices in a mesh: dp: 32 (over z, y, x, core).
Axes of the slice: x: 2, y: 2, z: 4, core: 2. Of those that a mesh axis runs over, the one named last changes fastest.
Arguments:
- tokens: bfloat16 [128, 512, 576], P('dp'), may hold values from -6 to 6
- doc_starts: int32 [128, 512], P('dp'), may hold values from 0 to 512, as said below
- cotangent: bfloat16 [128, 512, 576], P('dp'), may hold values from -6 to 6
- master: float32 [3543040], P('dp'), may hold values from -2 to 2
- moment_one: float32 [3543040], P('dp'), may hold values from -0.0003 to 0.0003
- moment_two: float32 [3543040], P('dp'), may hold values from 3e-11 to 3e-09
Outputs:
- layer_out: bfloat16 [128, 512, 576], P('dp')
- input_grad: float32 [128, 512, 576], P('dp')
- grad_params: float32 [3543040], P('dp')
- grad_norm: float32 [], replicated
- new_master: float32 [3543040], P('dp')
- new_one: float32 [3543040], P('dp')
- new_two: float32 [3543040], P('dp')
The draws below stay inside these ranges and needn't reach their ends.
Inputs may be any that keep to these rules, and one draw needn't show every extreme that they name: `doc_starts`: each buffer holds whole documents from its first slot on, then padding in whole tiles of 128 slots; a device's last buffer may be all padding, every other buffer is at least half live; buffer 0 is one document of 512 tokens and buffer 128 - 1 is half padding.
All inputs are finite; a program needn't handle non-finite values.
Results may differ from the reference program's by a relative error of at most 0.012.
The reference program's roundings to bfloat16 on the way count: a program that leaves them out, or rounds other values in their place, can miss the bound.
Values may be sent and summed in bfloat16 or wider, within the bound.
No kernel may reach another device: no remote copies, remote signals or barrier semaphores. Data moves between devices by JAX's collectives and lax.ppermute only.
A program may use at most 256 MiB of HBM per device.

```python
import math
import jax
import jax.numpy as jnp
from jax import lax

MODEL_WIDTH = 576
QUERY_HEADS = 9
KEY_VALUE_HEADS = 3
HEAD_SIZE = 64
FEEDFWD_UNITS = 1536
MB = 4
CAP = 512
TILE = 128
STEP = 8
BUFFERS = 128
PARAMS = 3540096
FLAT = 3543040


def draw_doc_starts(key, part):
    tile_count = CAP // TILE
    key_live, key_fourth, key_cut = jax.random.split(jax.random.fold_in(key, 11), 3)
    live_tiles = jax.random.randint(key_live, (BUFFERS,), tile_count // 2, tile_count + 1)
    has_fourth = jax.random.randint(key_fourth, (BUFFERS // MB,), 0, 2)
    buffer_index = jnp.arange(BUFFERS)
    device_fourth = jnp.repeat(has_fourth, MB)
    live_tiles = jnp.where(buffer_index % MB == MB - 1, live_tiles * device_fourth, live_tiles)
    live_tiles = live_tiles.at[0].set(tile_count).at[BUFFERS - 1].set(tile_count // 2)
    token_index = jnp.arange(CAP)
    cuts = jax.random.randint(key_cut, (BUFFERS, CAP), 0, CAP // 4) == 0
    cuts = cuts | (token_index[None, :] == 0)
    cuts = cuts.at[0].set(token_index == 0)
    starts = lax.cummax(jnp.where(cuts, token_index[None, :], 0), axis=1)
    live_rows = token_index[None, :] < live_tiles[:, None] * TILE
    return jnp.where(live_rows, starts, CAP).astype(jnp.int32)


def draw_master(key, part):
    query_width = QUERY_HEADS * HEAD_SIZE
    value_total_width = KEY_VALUE_HEADS * HEAD_SIZE
    segments = [(MODEL_WIDTH * query_width, MODEL_WIDTH ** (-0.5)), (MODEL_WIDTH * value_total_width, MODEL_WIDTH ** (-0.5)), (MODEL_WIDTH * value_total_width, MODEL_WIDTH ** (-0.5)), (query_width * MODEL_WIDTH, 4.0 * query_width ** (-0.5)), (MODEL_WIDTH * FEEDFWD_UNITS, MODEL_WIDTH ** (-0.5)), (MODEL_WIDTH * FEEDFWD_UNITS, MODEL_WIDTH ** (-0.5)), (FEEDFWD_UNITS * MODEL_WIDTH, FEEDFWD_UNITS ** (-0.5))]
    subkeys = jax.random.split(jax.random.fold_in(key, 5), len(segments) + 2)
    pieces = []
    for number, (entries, spread) in enumerate(segments):
        drawn_raw = jnp.clip(jax.random.normal(subkeys[number], (entries,), jnp.float32), -4.0, 4.0)
        pieces.append(drawn_raw * spread)
    pieces.append(1.0 + 0.2 * jax.random.uniform(subkeys[-2], (2 * MODEL_WIDTH,), jnp.float32, -1.0, 1.0))
    pieces.append(0.02 * jnp.clip(jax.random.normal(subkeys[-1], (FLAT - PARAMS,), jnp.float32), -4.0, 4.0))
    return jnp.concatenate(pieces)


def block_scale(rng, extent, cuts, least, largest):
    def one(dim, blocks):
        steps = jax.random.uniform(jax.random.fold_in(jax.random.fold_in(rng, 6), dim), (blocks,), jnp.float32, least / len(cuts), largest / len(cuts))
        return jnp.repeat(jnp.exp(steps), extent[dim] // blocks).reshape((-1,) + (1,) * (len(extent) - dim - 1))

    factor_of = one(*cuts[0])
    for cut in cuts[1:]:
        factor_of = factor_of * one(*cut)
    return factor_of


def normal_values(stream_key, dims, width, reach, cuts=(), held_as=jnp.bfloat16):
    array = width * jax.random.normal(stream_key, dims, jnp.float32)
    if cuts:
        array = array * block_scale(stream_key, dims, cuts, -0.22, 0.18)
    return jnp.clip(array, -reach, reach).astype(held_as)


def setup_inputs(seed: int = 0) -> dict:
    key_list = jax.random.split(jax.random.key(seed), 7)
    tokens = normal_values(key_list[0], (BUFFERS, CAP, MODEL_WIDTH), 1.0, 6.0, ((0, 32),))
    doc_starts = draw_doc_starts(jax.random.fold_in(key_list[6], 71), 0)
    cotangent = normal_values(key_list[2], (BUFFERS, CAP, MODEL_WIDTH), 1.0, 6.0, ((0, 32),))
    master = draw_master(jax.random.fold_in(key_list[6], 71), 0)
    moment_one = normal_values(key_list[4], (FLAT,), 0.00005, 0.0003, ((0, 32),), jnp.float32)
    moment_two = jnp.clip(jnp.exp(math.log(3.000000026176508e-09) - 4.6051702 * jax.random.uniform(key_list[5], (FLAT,), jnp.float32) ** block_scale(key_list[5], (FLAT,), ((0, 32),), -0.2, 0.2)), 2.999999901276418e-11, 3.000000026176508e-09)
    return dict(tokens=tokens, doc_starts=doc_starts, cotangent=cotangent, master=master, moment_one=moment_one, moment_two=moment_two)


@jax.custom_vjp
def lower_precision(v):
    return lax.optimization_barrier(v.astype(jnp.bfloat16)).astype(jnp.float32)

@jax.custom_vjp
def lower_backward(v):
    return v

def low_keep(v):
    return (lower_precision(v), None)

def low_pass(kept, grad):
    return (grad,)

def back_keep(v):
    return (v, None)

def back_low(kept, grad):
    return (lower_precision(grad),)
lower_precision.defvjp(low_keep, low_pass)
lower_backward.defvjp(back_keep, back_low)
rms_eps = 1e-05
rope_base = 100000.0
learn_rate = 0.02
decay_one = 0.9
decay_two = 0.999
adam_eps = 1e-08
weight_decay = 0.1
clip_norm = 1.0
mask_fill = -1000000000.0

def highest_precision(form, former, latter):
    return jnp.einsum(form, former, latter, precision=lax.Precision.HIGHEST)

def unpack(flat_params):
    query_width = QUERY_HEADS * HEAD_SIZE
    value_total_width = KEY_VALUE_HEADS * HEAD_SIZE
    layout = [(MODEL_WIDTH, query_width), (MODEL_WIDTH, value_total_width), (MODEL_WIDTH, value_total_width), (query_width, MODEL_WIDTH), (MODEL_WIDTH, FEEDFWD_UNITS), (MODEL_WIDTH, FEEDFWD_UNITS), (FEEDFWD_UNITS, MODEL_WIDTH), (2, MODEL_WIDTH)]
    pieces = []
    offset = 0
    for height, breadth in layout:
        pieces.append(flat_params[offset:offset + height * breadth].reshape(height, breadth))
        offset = offset + height * breadth
    return pieces

def rope_tables(positions):
    half_dim = HEAD_SIZE // 2
    frequency = rope_base ** (-(jnp.arange(half_dim, dtype=jnp.float32) * 2.0 / HEAD_SIZE))
    angles = positions.astype(jnp.float32)[:, None] * frequency[None, :]
    angles = jnp.concatenate([angles, angles], axis=1)
    return (jnp.cos(angles), jnp.sin(angles))

def apply_rotary(heads_in, cosine_lookup, sine_lookup):
    half_dim = HEAD_SIZE // 2
    turned = jnp.concatenate([-heads_in[..., half_dim:], heads_in[..., :half_dim]], axis=-1)
    return heads_in * cosine_lookup[:, None, :] + turned * sine_lookup[:, None, :]

def rms_norm(values, gain_row):
    inverse = lax.rsqrt(lax.optimization_barrier(jnp.mean(values * values, axis=-1, keepdims=True)) + rms_eps)
    return values * inverse * gain_row

def buffer_forward(weights, values_in, starts):
    query_weight, key_matrix, value_matrix, output_weight, gate_weight, up_weight, down_weight, norm_gains = weights
    sequence_length = values_in.shape[0]
    token_index = jnp.arange(sequence_length, dtype=jnp.int32)
    live_rows = (starts < sequence_length).astype(values_in.dtype)[:, None]
    positions = jnp.where(starts < sequence_length, token_index - starts, 0).astype(jnp.int32)
    cosine_lookup, sine_lookup = rope_tables(positions)
    first_normalized = lower_precision(rms_norm(values_in, norm_gains[0]))
    rotated_query = lower_precision(apply_rotary(lower_backward(highest_precision('kz,zu->ku', first_normalized, query_weight)).reshape(sequence_length, QUERY_HEADS, HEAD_SIZE), cosine_lookup, sine_lookup))
    rotated_key = lower_precision(apply_rotary(lower_backward(highest_precision('kz,zu->ku', first_normalized, key_matrix)).reshape(sequence_length, KEY_VALUE_HEADS, HEAD_SIZE), cosine_lookup, sine_lookup))
    value_lower = lower_precision(lower_backward(highest_precision('kz,zu->ku', first_normalized, value_matrix)).reshape(sequence_length, KEY_VALUE_HEADS, HEAD_SIZE))
    grouped_heads = rotated_query.reshape(sequence_length, KEY_VALUE_HEADS, QUERY_HEADS // KEY_VALUE_HEADS, HEAD_SIZE)
    scores = highest_precision('qgcd,kgd->gcqk', grouped_heads, rotated_key) * HEAD_SIZE ** (-0.5)
    allowed = (starts[:, None] == starts[None, :]) & (token_index[:, None] >= token_index[None, :])
    scores = lower_backward(jnp.where(allowed[None, None], scores, mask_fill))
    prob_low = lower_precision(jnp.exp(scores - jax.nn.logsumexp(scores, axis=-1, keepdims=True)))
    mixed = highest_precision('gcqk,kgd->qgcd', prob_low, value_lower).reshape(sequence_length, QUERY_HEADS * HEAD_SIZE)
    mixed_low = lower_precision(lower_backward(mixed))
    hidden = values_in + lower_backward(highest_precision('te,ed->td', mixed_low, output_weight))
    normed_two = lower_precision(rms_norm(hidden, norm_gains[1]))
    gate_pre = lower_backward(highest_precision('td,df->tf', normed_two, gate_weight))
    up_pre = lower_backward(highest_precision('td,df->tf', normed_two, up_weight))
    activated = lower_precision(jax.nn.silu(gate_pre) * up_pre)
    result = hidden + lower_backward(highest_precision('tf,fd->td', activated, down_weight))
    return result * live_rows

def forward_all(values_all, flat_params, doc_starts):
    weights = unpack(lower_precision(flat_params))
    checked = jax.checkpoint(lambda values_in, starts: buffer_forward(weights, values_in, starts))

    def scan_body(scan_carry, scan_pair):
        return (scan_carry, checked(scan_pair[0], scan_pair[1]))
    unused, result = lax.scan(scan_body, None, (values_all, doc_starts))
    return result

def reference(tokens, doc_starts, cotangent, master, moment_one, moment_two):
    values_all = tokens.astype(jnp.float32)
    result, pullback = jax.vjp(lambda values, flat_params: forward_all(values, flat_params, doc_starts), values_all, master)
    input_grad, grad_params = pullback(cotangent.astype(jnp.float32))
    grad_norm = jnp.sqrt(jnp.sum(grad_params * grad_params))
    clipped = grad_params * (clip_norm / jnp.maximum(grad_norm, clip_norm))
    new_one = decay_one * moment_one + (1.0 - decay_one) * clipped
    new_two = decay_two * moment_two + (1.0 - decay_two) * clipped * clipped
    corrected_one = new_one / (1.0 - decay_one ** STEP)
    corrected_two = new_two / (1.0 - decay_two ** STEP)
    new_master = master - learn_rate * (corrected_one / (jnp.sqrt(corrected_two) + adam_eps) + weight_decay * master)
    return (result.astype(jnp.bfloat16), input_grad, grad_params, grad_norm, new_master, new_one, new_two)
```

```python
import functools

import jax
import jax.numpy as jnp
from jax import lax
from jax.experimental import pallas as pl
from jax.experimental.pallas import tpu as pltpu
from jax.sharding import PartitionSpec as P

MODEL_WIDTH = 576
QUERY_HEADS = 9
KEY_VALUE_HEADS = 3
HEAD_SIZE = 64
FEEDFWD_UNITS = 1536
TILE = 128
STEP = 8
GROUP = QUERY_HEADS // KEY_VALUE_HEADS
HALF = HEAD_SIZE // 2
KV_WIDTH = KEY_VALUE_HEADS * HEAD_SIZE
QKV_WIDTH = MODEL_WIDTH + 2 * KV_WIDTH
CHUNK = 512

rms_eps = 1e-05
rope_base = 100000.0
learn_rate = 0.02
decay_one = 0.9
decay_two = 0.999
adam_eps = 1e-08
weight_decay = 0.1
clip_norm = 1.0
mask_fill = -1000000000.0

bf16 = jnp.bfloat16
f32 = jnp.float32


def mm(a, b):
    return jnp.dot(a, b, preferred_element_type=f32)


def inverse_rms(x):
    return lax.rsqrt(jnp.mean(x * x, axis=-1, keepdims=True) + rms_eps)


def fill_bias(bias, starts_col, starts_row):
    rows = starts_col.shape[0]
    key_at = lax.broadcasted_iota(jnp.int32, (rows, TILE), 0)
    for i in range(rows // TILE):
        width = (i + 1) * TILE
        query_at = lax.broadcasted_iota(jnp.int32, (rows, TILE), 1) + i * TILE
        allowed = (starts_col == starts_row[:, i * TILE : width]) & (key_at <= query_at)
        bias[:, i * TILE : width] = jnp.where(allowed, 0.0, mask_fill)


def head_rows(ref, g, columns):
    return jnp.concatenate(
        [ref[0, pl.ds((g * GROUP + h) * HEAD_SIZE, HEAD_SIZE), columns] for h in range(GROUP)], axis=1
    )


def attention_forward(
    live, tok, st_row, st_col, cos, sin, wq, wk, wv, wo, gain, qk_t, kv, mix_t, hidden, lse, w_t, v_t, bias
):
    b = pl.program_id(0)
    rows = tok.shape[1]

    @pl.when(b == 0)
    def _():
        w_t[0:MODEL_WIDTH] = wq[...].T
        w_t[MODEL_WIDTH : MODEL_WIDTH + KV_WIDTH] = wk[...].T
        w_t[MODEL_WIDTH + KV_WIDTH : QKV_WIDTH] = wv[...].T

    @pl.when(live[b] > 0)
    def _():
        x = tok[0].astype(f32)
        n1_t = (x * inverse_rms(x) * gain[...]).astype(bf16).T
        c, s = cos[0], sin[0]
        for h in range(QUERY_HEADS + KEY_VALUE_HEADS):
            at = h * HEAD_SIZE
            u = mm(w_t[at : at + HEAD_SIZE], n1_t)
            u1, u2 = u[:HALF], u[HALF:]
            r = jnp.concatenate([u1 * c - u2 * s, u2 * c + u1 * s], axis=0)
            if h < QUERY_HEADS:
                r = r * HEAD_SIZE ** (-0.5)
            r = r.astype(bf16)
            qk_t[0, at : at + HEAD_SIZE] = r
            if h >= QUERY_HEADS:
                kv[0, h - QUERY_HEADS] = r.T
        for g in range(KEY_VALUE_HEADS):
            at = MODEL_WIDTH + KV_WIDTH + g * HEAD_SIZE
            v = mm(w_t[at : at + HEAD_SIZE], n1_t).astype(bf16)
            v_t[g] = v
            kv[0, KEY_VALUE_HEADS + g] = v.T
        fill_bias(bias, st_col[0], st_row[0])
        mix_t[...] = jnp.zeros_like(mix_t)

        def group(g, carry):
            for i in range(rows // TILE):

                @pl.when(i < live[b])
                def _():
                    width = (i + 1) * TILE
                    cols = slice(i * TILE, width)
                    q_t = head_rows(qk_t, g, cols)
                    mask = bias[:width, cols]
                    scores = mm(kv[0, g, :width], q_t) + jnp.concatenate([mask] * GROUP, axis=1)
                    peak = jnp.max(scores, axis=0, keepdims=True)
                    e = jnp.exp(scores - peak)
                    total = jnp.sum(e, axis=0, keepdims=True)
                    prob = (e * (1.0 / total)).astype(bf16)
                    lse[0, g * (rows // TILE) + i] = peak + jnp.log(total)
                    out = mm(v_t[g, :, :width], prob).astype(bf16)
                    for h in range(GROUP):
                        mix_t[0, pl.ds((g * GROUP + h) * HEAD_SIZE, HEAD_SIZE), cols] = out[
                            :, h * TILE : (h + 1) * TILE
                        ]

            return carry

        lax.fori_loop(0, KEY_VALUE_HEADS, group, 0)
        hidden[0] = x + mm(mix_t[0].T, wo[...])


def mlp(
    live, hidden, cot, st_col, wg, wu, wd, gain, layer, hgrad, dwg, dwu, dwd_t, dgain,
    wg_t, wu_t, wd_t, n2, n2_t, rl, rl_t, n2g, res
):
    b = pl.program_id(0)
    rows = hidden.shape[1]

    @pl.when(b == 0)
    def _():
        wg_t[...] = wg[...].T
        wu_t[...] = wu[...].T
        wd_t[...] = wd[...].T
        dwg[...] = jnp.zeros_like(dwg)
        dwu[...] = jnp.zeros_like(dwu)
        dwd_t[...] = jnp.zeros_like(dwd_t)
        dgain[...] = jnp.zeros_like(dgain)

    @pl.when(live[b] == 0)
    def _():
        layer[...] = jnp.zeros_like(layer)
        hgrad[...] = jnp.zeros_like(hgrad)

    @pl.when(live[b] > 0)
    def _():
        x = hidden[0]
        inverse = inverse_rms(x)
        alive = st_col[0] < rows
        normed = (x * inverse * gain[...]).astype(bf16)
        n2[...] = normed
        n2_t[...] = normed.T
        grad = jnp.where(alive, cot[0].astype(f32), 0.0).astype(bf16)
        rl[...] = grad
        rl_t[...] = grad.T
        res[...] = jnp.zeros_like(res)
        n2g[...] = jnp.zeros_like(n2g)

        def chunk(k, carry):
            at = pl.ds(pl.multiple_of(k * CHUNK, CHUNK), CHUNK)
            pre = mm(n2[...], wg[:, at])
            up = mm(n2[...], wu[:, at])
            ag = mm(rl[...], wd_t[:, at])
            s = jax.nn.sigmoid(pre)
            silu = pre * s
            act = (silu * up).astype(bf16)
            gl = (ag * up * s * (1.0 + pre * (1.0 - s))).astype(bf16)
            ul = (ag * silu).astype(bf16)
            res[...] += mm(act, wd[at, :])
            n2g[...] += mm(gl, wg_t[at, :]) + mm(ul, wu_t[at, :])
            dwd_t[:, at] += mm(rl_t[...], act)
            dwg[:, at] += mm(n2_t[...], gl)
            dwu[:, at] += mm(n2_t[...], ul)
            return carry

        lax.fori_loop(0, FEEDFWD_UNITS // CHUNK, chunk, 0)
        x = hidden[0]
        layer[0] = jnp.where(alive, x + res[...], 0.0).astype(bf16)
        ng = n2g[...]
        dgain[...] += jnp.sum(ng * x * inverse, axis=0, keepdims=True)
        e = ng * gain[...]
        hgrad[0] = (
            rl[...].astype(f32)
            + inverse * e
            - x * (inverse * inverse * inverse) * jnp.mean(e * x, axis=-1, keepdims=True)
        )


def attention_backward(
    live, hgrad, tok, qk_t, kv, mix_t, lse, st_row, st_col, cos, sin, wq, wk, wv, wo, gain,
    igrad, dw_t, dwo, dgain, w, bias, mg_t, mg, q, dq, dk, dv, low_t
):
    b = pl.program_id(0)
    rows = tok.shape[1]
    tiles = rows // TILE
    scale = HEAD_SIZE ** (-0.5)

    @pl.when(b == 0)
    def _():
        w[:, 0:MODEL_WIDTH] = wq[...]
        w[:, MODEL_WIDTH : MODEL_WIDTH + KV_WIDTH] = wk[...]
        w[:, MODEL_WIDTH + KV_WIDTH : QKV_WIDTH] = wv[...]
        dw_t[...] = jnp.zeros_like(dw_t)
        dwo[...] = jnp.zeros_like(dwo)
        dgain[...] = jnp.zeros_like(dgain)

    @pl.when(live[b] == 0)
    def _():
        igrad[...] = jnp.zeros_like(igrad)

    @pl.when(live[b] > 0)
    def _():
        hl = hgrad[0].astype(bf16)
        dwo[...] += mm(mix_t[0], hl)
        mg_t[0] = mm(wo[...], hl.T).astype(bf16)
        for h in range(QUERY_HEADS):
            at = slice(h * HEAD_SIZE, (h + 1) * HEAD_SIZE)
            mg[h] = mg_t[0, at].T
            q[h] = qk_t[0, at].T
        fill_bias(bias, st_col[0], st_row[0])
        dq[...] = jnp.zeros_like(dq)
        dk[...] = jnp.zeros_like(dk)
        dv[...] = jnp.zeros_like(dv)

        def group(g, carry):
            for i in range(tiles):

                @pl.when(i < live[b])
                def _():
                    width = (i + 1) * TILE
                    cols = slice(i * TILE, width)
                    q_t = head_rows(qk_t, g, cols)
                    mask = bias[:width, cols]
                    scores = mm(kv[0, g, :width], q_t) + jnp.concatenate([mask] * GROUP, axis=1)
                    prob = jnp.exp(scores - lse[0, g * tiles + i])
                    dp = mm(kv[0, KEY_VALUE_HEADS + g, :width], head_rows(mg_t, g, cols))
                    delta = jnp.sum(prob * dp, axis=0, keepdims=True)
                    ds = (prob * (dp - delta)).astype(bf16)
                    low = prob.astype(bf16)
                    k_t = qk_t[0, pl.ds(MODEL_WIDTH + g * HEAD_SIZE, HEAD_SIZE), :width]
                    dq_i = mm(k_t, ds) * scale
                    for h in range(GROUP):
                        dq[pl.ds((g * GROUP + h) * HEAD_SIZE, HEAD_SIZE), cols] = dq_i[
                            :, h * TILE : (h + 1) * TILE
                        ]
                    q_i = jnp.concatenate([q[g * GROUP + h, cols] for h in range(GROUP)], axis=0)
                    mg_i = jnp.concatenate([mg[g * GROUP + h, cols] for h in range(GROUP)], axis=0)
                    dk[g, :width] += mm(ds, q_i)
                    dv[g, :width] += mm(low, mg_i)

            return carry

        lax.fori_loop(0, KEY_VALUE_HEADS, group, 0)
        c, s = cos[0], sin[0]
        for h in range(QUERY_HEADS + KEY_VALUE_HEADS):
            at = h * HEAD_SIZE
            u = dq[at : at + HEAD_SIZE] if h < QUERY_HEADS else dk[h - QUERY_HEADS].T
            u1, u2 = u[:HALF], u[HALF:]
            r = jnp.concatenate([u1 * c + u2 * s, u2 * c - u1 * s], axis=0)
            low_t[at : at + HEAD_SIZE] = r.astype(bf16)
        for g in range(KEY_VALUE_HEADS):
            at = MODEL_WIDTH + KV_WIDTH + g * HEAD_SIZE
            low_t[at : at + HEAD_SIZE] = dv[g].T.astype(bf16)
        x = tok[0].astype(f32)
        inverse = inverse_rms(x)
        n1 = (x * inverse * gain[...]).astype(bf16)
        dw_t[...] += mm(low_t[...], n1)
        ng = mm(w[...], low_t[...]).T
        dgain[...] += jnp.sum(ng * x * inverse, axis=0, keepdims=True)
        e = ng * gain[...]
        igrad[0] = (
            hgrad[0]
            + inverse * e
            - x * (inverse * inverse * inverse) * jnp.mean(e * x, axis=-1, keepdims=True)
        )


def by_buffer(*shape):
    zeros = (0,) * len(shape)
    return pl.BlockSpec((1,) + shape, lambda b, live: (b,) + zeros)


def whole(*shape):
    zeros = (0,) * len(shape)
    return pl.BlockSpec(shape, lambda b, live: zeros, pipeline_mode=pl.Buffered(1))


def call(kernel, name, buffers, in_specs, out_specs, outs, scratch, flops, moved, args):
    return pl.pallas_call(
        kernel,
        name=name,
        out_shape=[jax.ShapeDtypeStruct(shape, dtype) for shape, dtype in outs],
        grid_spec=pltpu.PrefetchScalarGridSpec(
            num_scalar_prefetch=1,
            grid=(buffers,),
            in_specs=in_specs,
            out_specs=out_specs,
            scratch_shapes=[pltpu.VMEM(shape, dtype) for shape, dtype in scratch],
        ),
        compiler_params=pltpu.CompilerParams(
            dimension_semantics=("arbitrary",), vmem_limit_bytes=60 * 1024 * 1024
        ),
        cost_estimate=pl.CostEstimate(flops=flops, bytes_accessed=moved, transcendentals=0),
    )(*args)


def run_attention_forward(live, tokens, st_row, st_col, cos, sin, wq, wk, wv, wo, gain):
    n, t, d = tokens.shape
    tiles = t // TILE
    return call(
        attention_forward, "attention_forward", n,
        [by_buffer(t, d), by_buffer(1, t), by_buffer(t, 1), by_buffer(HALF, t), by_buffer(HALF, t),
         whole(d, d), whole(d, KV_WIDTH), whole(d, KV_WIDTH), whole(d, d), whole(1, d)],
        [by_buffer(d + KV_WIDTH, t), by_buffer(2 * KEY_VALUE_HEADS, t, HEAD_SIZE), by_buffer(d, t), by_buffer(t, d),
         by_buffer(KEY_VALUE_HEADS * tiles, 1, GROUP * TILE)],
        [((n, d + KV_WIDTH, t), bf16), ((n, 2 * KEY_VALUE_HEADS, t, HEAD_SIZE), bf16), ((n, d, t), bf16), ((n, t, d), f32),
         ((n, KEY_VALUE_HEADS * tiles, 1, GROUP * TILE), f32)],
        [((QKV_WIDTH, d), bf16), ((KEY_VALUE_HEADS, HEAD_SIZE, t), bf16), ((t, t), f32)],
        8 * 10**9, 20 * 10**6,
        (live, tokens, st_row, st_col, cos, sin, wq, wk, wv, wo, gain),
    )


def run_mlp(live, hidden, cot, st_col, wg, wu, wd, gain):
    n, t, d = hidden.shape
    f = FEEDFWD_UNITS
    return call(
        mlp, "mlp", n,
        [by_buffer(t, d), by_buffer(t, d), by_buffer(t, 1), whole(d, f), whole(d, f), whole(f, d), whole(1, d)],
        [by_buffer(t, d), by_buffer(t, d), whole(d, f), whole(d, f), whole(d, f), whole(1, d)],
        [((n, t, d), bf16), ((n, t, d), f32), ((d, f), f32), ((d, f), f32), ((d, f), f32), ((1, d), f32)],
        [((f, d), bf16), ((f, d), bf16), ((d, f), bf16), ((t, d), bf16), ((d, t), bf16), ((t, d), bf16), ((d, t), bf16),
         ((t, d), f32), ((t, d), f32)],
        33 * 10**9, 30 * 10**6,
        (live, hidden, cot, st_col, wg, wu, wd, gain),
    )


def run_attention_backward(live, hgrad, tokens, qk_t, kv, mix_t, lse, st_row, st_col, cos, sin, wq, wk, wv, wo, gain):
    n, t, d = tokens.shape
    tiles = t // TILE
    return call(
        attention_backward, "attention_backward", n,
        [by_buffer(t, d), by_buffer(t, d), by_buffer(d + KV_WIDTH, t), by_buffer(2 * KEY_VALUE_HEADS, t, HEAD_SIZE),
         by_buffer(d, t), by_buffer(KEY_VALUE_HEADS * tiles, 1, GROUP * TILE), by_buffer(1, t), by_buffer(t, 1),
         by_buffer(HALF, t), by_buffer(HALF, t),
         whole(d, d), whole(d, KV_WIDTH), whole(d, KV_WIDTH), whole(d, d), whole(1, d)],
        [by_buffer(t, d), whole(QKV_WIDTH, d), whole(d, d), whole(1, d)],
        [((n, t, d), f32), ((QKV_WIDTH, d), f32), ((d, d), f32), ((1, d), f32)],
        [((d, QKV_WIDTH), bf16), ((t, t), f32), ((1, d, t), bf16), ((QUERY_HEADS, t, HEAD_SIZE), bf16),
         ((QUERY_HEADS, t, HEAD_SIZE), bf16), ((d, t), f32), ((KEY_VALUE_HEADS, t, HEAD_SIZE), f32),
         ((KEY_VALUE_HEADS, t, HEAD_SIZE), f32), ((QKV_WIDTH, t), bf16)],
        16 * 10**9, 40 * 10**6,
        (live, hgrad, tokens, qk_t, kv, mix_t, lse, st_row, st_col, cos, sin, wq, wk, wv, wo, gain),
    )


def unpack(flat_params):
    layout = [
        (MODEL_WIDTH, MODEL_WIDTH),
        (MODEL_WIDTH, KV_WIDTH),
        (MODEL_WIDTH, KV_WIDTH),
        (MODEL_WIDTH, MODEL_WIDTH),
        (MODEL_WIDTH, FEEDFWD_UNITS),
        (MODEL_WIDTH, FEEDFWD_UNITS),
        (FEEDFWD_UNITS, MODEL_WIDTH),
        (2, MODEL_WIDTH),
    ]
    pieces = []
    offset = 0
    for height, breadth in layout:
        pieces.append(flat_params[offset : offset + height * breadth].reshape(height, breadth))
        offset = offset + height * breadth
    return pieces


def local(tokens, doc_starts, cotangent, master, moment_one, moment_two):
    rows = tokens.shape[1]
    whole_rows = master.shape[0] * lax.axis_size("dp")
    flat = lax.all_gather(master.astype(bf16), "dp", axis=0, tiled=True)
    wq, wk, wv, wo, wg, wu, wd, gains = unpack(flat)
    gain_one = gains[0:1].astype(f32)
    gain_two = gains[1:2].astype(f32)

    is_live = doc_starts < rows
    live = jnp.sum(is_live.astype(jnp.int32), axis=1) // TILE
    positions = jnp.where(is_live, jnp.arange(rows) - doc_starts, 0).astype(f32)
    frequency = rope_base ** (-(jnp.arange(HALF, dtype=f32) * 2.0 / HEAD_SIZE))
    angles = frequency[None, :, None] * positions[:, None, :]
    cos, sin = jnp.cos(angles), jnp.sin(angles)
    st_row, st_col = doc_starts[:, None, :], doc_starts[:, :, None]

    qk_t, kv, mix_t, hidden, lse = run_attention_forward(
        live, tokens, st_row, st_col, cos, sin, wq, wk, wv, wo, gain_one
    )
    layer, hgrad, dwg, dwu, dwd_t, dgain_two = run_mlp(live, hidden, cotangent, st_col, wg, wu, wd, gain_two)
    igrad, dw_t, dwo, dgain_one = run_attention_backward(
        live, hgrad, tokens, qk_t, kv, mix_t, lse, st_row, st_col, cos, sin, wq, wk, wv, wo, gain_one
    )
    dw = dw_t.T
    pieces = (
        dw[:, :MODEL_WIDTH], dw[:, MODEL_WIDTH : MODEL_WIDTH + KV_WIDTH], dw[:, MODEL_WIDTH + KV_WIDTH :],
        dwo, dwg, dwu, dwd_t.T, dgain_one, dgain_two,
    )
    flat_grads = jnp.concatenate([piece.reshape(-1) for piece in pieces])
    grads = jnp.pad(flat_grads, (0, whole_rows - flat_grads.shape[0]))
    grad_shard = lax.psum_scatter(grads, "dp", scatter_dimension=0, tiled=True)
    square_sum = lax.psum(jnp.sum(grad_shard * grad_shard), "dp")
    grad_norm = jnp.sqrt(square_sum)
    clipped = grad_shard * (clip_norm / jnp.maximum(grad_norm, clip_norm))
    new_one = decay_one * moment_one + (1.0 - decay_one) * clipped
    new_two = decay_two * moment_two + (1.0 - decay_two) * clipped * clipped
    corrected_one = new_one / (1.0 - decay_one**STEP)
    corrected_two = new_two / (1.0 - decay_two**STEP)
    new_master = master - learn_rate * (
        corrected_one / (jnp.sqrt(corrected_two) + adam_eps) + weight_decay * master
    )
    return (layer, igrad, grad_shard, grad_norm, new_master, new_one, new_two)


def solution(mesh):
    flat, cube = P("dp"), P("dp", None, None)
    return jax.shard_map(
        local,
        mesh=mesh,
        in_specs=(cube, P("dp", None), cube, flat, flat, flat),
        out_specs=(cube, cube, flat, P(), flat, flat, flat),
        check_vma=False,
    )
```

```python
import functools

import jax
import jax.numpy as jnp
from jax import lax
from jax.experimental import pallas as pl
from jax.experimental.pallas import tpu as pltpu
from jax.sharding import PartitionSpec as P

MODEL_WIDTH = 576
QUERY_HEADS = 9
KEY_VALUE_HEADS = 3
HEAD_SIZE = 64
FEEDFWD_UNITS = 1536
TILE = 128
STEP = 8
GROUP = QUERY_HEADS // KEY_VALUE_HEADS
HALF = HEAD_SIZE // 2
KV_WIDTH = KEY_VALUE_HEADS * HEAD_SIZE
QKV_WIDTH = MODEL_WIDTH + 2 * KV_WIDTH
CHUNK = 512
LANES = 128
UNIT = MODEL_WIDTH * KV_WIDTH // LANES
GAIN_ROWS = 16
UNITS = 8

rms_eps = 1e-05
rope_base = 100000.0
learn_rate = 0.02
decay_one = 0.9
decay_two = 0.999
adam_eps = 1e-08
weight_decay = 0.1
clip_norm = 1.0
mask_fill = -1000000000.0

bf16 = jnp.bfloat16
f32 = jnp.float32


def mm(a, b):
    return jnp.dot(a, b, preferred_element_type=f32)


def inverse_rms(x):
    return lax.rsqrt(jnp.mean(x * x, axis=-1, keepdims=True) + rms_eps)


def fill_bias(bias, starts_col, starts_row):
    rows = starts_col.shape[0]
    key_at = lax.broadcasted_iota(jnp.int32, (rows, TILE), 0)
    for i in range(rows // TILE):
        width = (i + 1) * TILE
        query_at = lax.broadcasted_iota(jnp.int32, (rows, TILE), 1) + i * TILE
        allowed = (starts_col == starts_row[:, i * TILE : width]) & (key_at <= query_at)
        bias[:, i * TILE : width] = jnp.where(allowed, 0.0, mask_fill)


def half_turn(x):
    return pltpu.roll(x, HEAD_SIZE, 1)


def to_matrix(flat, base, out, pairs, tiles):
    half = tiles // 2
    low = lax.broadcasted_iota(jnp.int32, (pairs, LANES), 1) < HEAD_SIZE
    for t in range(half + 1):
        out[t, pl.ds(0, pairs, stride=2), :] = flat[pl.ds(base + t, pairs, stride=tiles), :]
    turned = half_turn(flat[pl.ds(base + half, pairs, stride=tiles), :])
    for t in range(half):
        following = half_turn(flat[pl.ds(base + half + t + 1, pairs, stride=tiles), :])
        out[t, pl.ds(1, pairs, stride=2), :] = jnp.where(low, turned, following)
        turned = following
    out[half, pl.ds(1, pairs, stride=2), :] = turned


def to_flat(matrix, flat, base, pairs, tiles):
    half = tiles // 2
    low = lax.broadcasted_iota(jnp.int32, (pairs, LANES), 1) < HEAD_SIZE
    for t in range(half):
        flat[pl.ds(base + t, pairs, stride=tiles), :] = matrix[t, pl.ds(0, pairs, stride=2), :]
    before = matrix[half, pl.ds(0, pairs, stride=2), :]
    for t in range(half + 1):
        turned = half_turn(matrix[t, pl.ds(1, pairs, stride=2), :])
        flat[pl.ds(base + half + t, pairs, stride=tiles), :] = jnp.where(low, before, turned)
        before = turned


def columns_of(matrix, rows, width):
    full = width // LANES
    return jnp.concatenate([matrix[t, :rows] for t in range(full)] + [matrix[full, :rows, :HEAD_SIZE]], axis=1)


def put_columns(matrix, value):
    rows, width = value.shape
    full = width // LANES
    for t in range(full):
        matrix[t, :rows] = value[:, t * LANES : (t + 1) * LANES]
    matrix[full, :rows, :HEAD_SIZE] = value[:, full * LANES :]


def head_rows(ref, g, columns):
    return jnp.concatenate(
        [ref[0, pl.ds((g * GROUP + h) * HEAD_SIZE, HEAD_SIZE), columns] for h in range(GROUP)], axis=1
    )


def attention_forward(
    live, own, tok, st_row, st_col, cos, sin, units, gain, qk_t, kv, mix_t, hidden, lse, w, wo, w_t, v_t, bias, flat, square
):
    b = pl.program_id(0)
    rows = tok.shape[1]

    @pl.when(b == 0)
    def _():
        for k in range(UNITS):
            flat[k * UNIT : (k + 1) * UNIT] = units[k ^ own[0]].astype(f32)
        pairs = MODEL_WIDTH // 2
        to_matrix(flat, 5 * UNIT, square, pairs, 9)
        wo[...] = columns_of(square, MODEL_WIDTH, MODEL_WIDTH).astype(bf16)
        to_matrix(flat, 0, square, pairs, 9)
        value = columns_of(square, MODEL_WIDTH, MODEL_WIDTH)
        w[:, 0:MODEL_WIDTH] = value.astype(bf16)
        w_t[0:MODEL_WIDTH] = value.T.astype(bf16)
        for which in range(2):
            at = MODEL_WIDTH + which * KV_WIDTH
            to_matrix(flat, (3 + which) * UNIT, square, pairs, 3)
            value = columns_of(square, MODEL_WIDTH, KV_WIDTH)
            w[:, at : at + KV_WIDTH] = value.astype(bf16)
            w_t[at : at + KV_WIDTH] = value.T.astype(bf16)

    @pl.when(live[b] > 0)
    def _():
        x = tok[0].astype(f32)
        n1_t = (x * inverse_rms(x) * gain[...]).astype(bf16).T
        c, s = cos[0], sin[0]
        for h in range(QUERY_HEADS + KEY_VALUE_HEADS):
            at = h * HEAD_SIZE
            u = mm(w_t[at : at + HEAD_SIZE], n1_t)
            u1, u2 = u[:HALF], u[HALF:]
            r = jnp.concatenate([u1 * c - u2 * s, u2 * c + u1 * s], axis=0)
            if h < QUERY_HEADS:
                r = r * HEAD_SIZE ** (-0.5)
            r = r.astype(bf16)
            qk_t[0, at : at + HEAD_SIZE] = r
            if h >= QUERY_HEADS:
                kv[0, h - QUERY_HEADS] = r.T
        for g in range(KEY_VALUE_HEADS):
            at = MODEL_WIDTH + KV_WIDTH + g * HEAD_SIZE
            v = mm(w_t[at : at + HEAD_SIZE], n1_t).astype(bf16)
            v_t[g] = v
            kv[0, KEY_VALUE_HEADS + g] = v.T
        fill_bias(bias, st_col[0], st_row[0])
        mix_t[...] = jnp.zeros_like(mix_t)

        def group(g, carry):
            for i in range(rows // TILE):

                @pl.when(i < live[b])
                def _():
                    width = (i + 1) * TILE
                    cols = slice(i * TILE, width)
                    q_t = head_rows(qk_t, g, cols)
                    mask = bias[:width, cols]
                    scores = mm(kv[0, g, :width], q_t) + jnp.concatenate([mask] * GROUP, axis=1)
                    peak = jnp.max(scores, axis=0, keepdims=True)
                    e = jnp.exp(scores - peak)
                    total = jnp.sum(e, axis=0, keepdims=True)
                    prob = (e * (1.0 / total)).astype(bf16)
                    lse[0, g * (rows // TILE) + i] = peak + jnp.log(total)
                    out = mm(v_t[g, :, :width], prob).astype(bf16)
                    for h in range(GROUP):
                        mix_t[0, pl.ds((g * GROUP + h) * HEAD_SIZE, HEAD_SIZE), cols] = out[
                            :, h * TILE : (h + 1) * TILE
                        ]

            return carry

        lax.fori_loop(0, KEY_VALUE_HEADS, group, 0)
        hidden[0] = x + mm(mix_t[0].T, wo[...])


def mlp(
    live, own, hidden, cot, st_col, gate_rows, up_rows, down_rows, gain, layer, hgrad, grads, dgain,
    wg, wu, wd, wg_t, wu_t, wd_t, dwg, dwu, dwd_t, n2, n2_t, rl, rl_t, n2g, res, flat, slab
):
    b = pl.program_id(0)
    rows = hidden.shape[1]

    @pl.when(b == 0)
    def _():
        tiles = FEEDFWD_UNITS // LANES
        for rows_in, straight, turned in ((gate_rows, wg, wg_t), (up_rows, wu, wu_t)):
            flat[...] = rows_in[...].astype(f32)
            for j in range(tiles):
                at = slice(j * LANES, (j + 1) * LANES)
                part = flat[pl.ds(j, MODEL_WIDTH, stride=tiles), :]
                straight[:, at] = part.astype(bf16)
                turned[at] = part.T.astype(bf16)
        flat[...] = down_rows[...].astype(f32)
        for j in range(tiles):
            at = slice(j * LANES, (j + 1) * LANES)
            to_matrix(flat, j * MODEL_WIDTH, slab, LANES // 2, 9)
            value = columns_of(slab, LANES, MODEL_WIDTH)
            wd[at] = value.astype(bf16)
            wd_t[:, at] = value.T.astype(bf16)
        dwg[...] = jnp.zeros_like(dwg)
        dwu[...] = jnp.zeros_like(dwu)
        dwd_t[...] = jnp.zeros_like(dwd_t)
        dgain[...] = jnp.zeros_like(dgain)

    @pl.when(live[b] == 0)
    def _():
        layer[...] = jnp.zeros_like(layer)
        hgrad[...] = jnp.zeros_like(hgrad)

    @pl.when(live[b] > 0)
    def _():
        x = hidden[0]
        inverse = inverse_rms(x)
        alive = st_col[0] < rows
        normed = (x * inverse * gain[...]).astype(bf16)
        n2[...] = normed
        n2_t[...] = normed.T
        grad = jnp.where(alive, cot[0].astype(f32), 0.0).astype(bf16)
        rl[...] = grad
        rl_t[...] = grad.T
        res[...] = jnp.zeros_like(res)
        n2g[...] = jnp.zeros_like(n2g)

        def chunk(k, carry):
            at = pl.ds(pl.multiple_of(k * CHUNK, CHUNK), CHUNK)
            pre = mm(n2[...], wg[:, at])
            up = mm(n2[...], wu[:, at])
            ag = mm(rl[...], wd_t[:, at])
            s = jax.nn.sigmoid(pre)
            silu = pre * s
            act = (silu * up).astype(bf16)
            gl = (ag * up * s * (1.0 + pre * (1.0 - s))).astype(bf16)
            ul = (ag * silu).astype(bf16)
            res[...] += mm(act, wd[at, :])
            n2g[...] += mm(gl, wg_t[at, :]) + mm(ul, wu_t[at, :])
            dwd_t[:, at] += mm(rl_t[...], act)
            dwg[:, at] += mm(n2_t[...], gl)
            dwu[:, at] += mm(n2_t[...], ul)
            return carry

        lax.fori_loop(0, FEEDFWD_UNITS // CHUNK, chunk, 0)
        x = hidden[0]
        layer[0] = jnp.where(alive, x + res[...], 0.0).astype(bf16)
        ng = n2g[...]
        dgain[...] += jnp.sum(ng * x * inverse, axis=0, keepdims=True)
        e = ng * gain[...]
        hgrad[0] = (
            rl[...].astype(f32)
            + inverse * e
            - x * (inverse * inverse * inverse) * jnp.mean(e * x, axis=-1, keepdims=True)
        )

    @pl.when(b == pl.num_programs(0) - 1)
    def _():
        tiles = FEEDFWD_UNITS // LANES
        for p in range(3):
            for j in range(tiles):
                at = slice(j * LANES, (j + 1) * LANES)
                if p < 2:
                    flat[pl.ds(j, MODEL_WIDTH, stride=tiles), :] = (dwg, dwu)[p][:, at]
                else:
                    put_columns(slab, dwd_t[:, at].T)
                    to_flat(slab, flat, j * MODEL_WIDTH, LANES // 2, 9)
            for k in range(UNITS):
                grads[k ^ own[0], p] = flat[k * UNIT : (k + 1) * UNIT].astype(bf16)


def attention_backward(
    live, own, hgrad, tok, qk_t, kv, mix_t, lse, st_row, st_col, cos, sin, w, wo, gain, dgain_two,
    igrad, grads, dw_t, dwo, dgain, bias, mg_t, mg, q, dq, dk, dv, low_t, flat, square
):
    b = pl.program_id(0)
    rows = tok.shape[1]
    tiles = rows // TILE
    scale = HEAD_SIZE ** (-0.5)

    @pl.when(b == 0)
    def _():
        dw_t[...] = jnp.zeros_like(dw_t)
        dwo[...] = jnp.zeros_like(dwo)
        dgain[...] = jnp.zeros_like(dgain)

    @pl.when(live[b] == 0)
    def _():
        igrad[...] = jnp.zeros_like(igrad)

    @pl.when(live[b] > 0)
    def _():
        hl = hgrad[0].astype(bf16)
        dwo[...] += mm(mix_t[0], hl)
        mg_t[0] = mm(wo[...], hl.T).astype(bf16)
        for h in range(QUERY_HEADS):
            at = slice(h * HEAD_SIZE, (h + 1) * HEAD_SIZE)
            mg[h] = mg_t[0, at].T
            q[h] = qk_t[0, at].T
        fill_bias(bias, st_col[0], st_row[0])
        dq[...] = jnp.zeros_like(dq)
        dk[...] = jnp.zeros_like(dk)
        dv[...] = jnp.zeros_like(dv)

        def group(g, carry):
            for i in range(tiles):

                @pl.when(i < live[b])
                def _():
                    width = (i + 1) * TILE
                    cols = slice(i * TILE, width)
                    q_t = head_rows(qk_t, g, cols)
                    mask = bias[:width, cols]
                    scores = mm(kv[0, g, :width], q_t) + jnp.concatenate([mask] * GROUP, axis=1)
                    prob = jnp.exp(scores - lse[0, g * tiles + i])
                    dp = mm(kv[0, KEY_VALUE_HEADS + g, :width], head_rows(mg_t, g, cols))
                    delta = jnp.sum(prob * dp, axis=0, keepdims=True)
                    ds = (prob * (dp - delta)).astype(bf16)
                    low = prob.astype(bf16)
                    k_t = qk_t[0, pl.ds(MODEL_WIDTH + g * HEAD_SIZE, HEAD_SIZE), :width]
                    dq_i = mm(k_t, ds) * scale
                    for h in range(GROUP):
                        dq[pl.ds((g * GROUP + h) * HEAD_SIZE, HEAD_SIZE), cols] = dq_i[
                            :, h * TILE : (h + 1) * TILE
                        ]
                    q_i = jnp.concatenate([q[g * GROUP + h, cols] for h in range(GROUP)], axis=0)
                    mg_i = jnp.concatenate([mg[g * GROUP + h, cols] for h in range(GROUP)], axis=0)
                    dk[g, :width] += mm(ds, q_i)
                    dv[g, :width] += mm(low, mg_i)

            return carry

        lax.fori_loop(0, KEY_VALUE_HEADS, group, 0)
        c, s = cos[0], sin[0]
        for h in range(QUERY_HEADS + KEY_VALUE_HEADS):
            at = h * HEAD_SIZE
            u = dq[at : at + HEAD_SIZE] if h < QUERY_HEADS else dk[h - QUERY_HEADS].T
            u1, u2 = u[:HALF], u[HALF:]
            r = jnp.concatenate([u1 * c + u2 * s, u2 * c - u1 * s], axis=0)
            low_t[at : at + HEAD_SIZE] = r.astype(bf16)
        for g in range(KEY_VALUE_HEADS):
            at = MODEL_WIDTH + KV_WIDTH + g * HEAD_SIZE
            low_t[at : at + HEAD_SIZE] = dv[g].T.astype(bf16)
        x = tok[0].astype(f32)
        inverse = inverse_rms(x)
        n1 = (x * inverse * gain[...]).astype(bf16)
        dw_t[...] += mm(low_t[...], n1)
        ng = mm(w[...], low_t[...]).T
        dgain[...] += jnp.sum(ng * x * inverse, axis=0, keepdims=True)
        e = ng * gain[...]
        igrad[0] = (
            hgrad[0]
            + inverse * e
            - x * (inverse * inverse * inverse) * jnp.mean(e * x, axis=-1, keepdims=True)
        )

    @pl.when(b == pl.num_programs(0) - 1)
    def _():
        pairs = MODEL_WIDTH // 2
        put_columns(square, dw_t[0:MODEL_WIDTH].T)
        to_flat(square, flat, 0, pairs, 9)
        for which in range(2):
            at = MODEL_WIDTH + which * KV_WIDTH
            put_columns(square, dw_t[at : at + KV_WIDTH].T)
            to_flat(square, flat, (3 + which) * UNIT, pairs, 3)
        put_columns(square, dwo[...])
        to_flat(square, flat, 5 * UNIT, pairs, 9)
        gains = jnp.concatenate([dgain[...], dgain_two[...]], axis=1)
        gains = jnp.concatenate([gains[:, j * LANES : (j + 1) * LANES] for j in range(9)], axis=0)
        for k in range(UNITS):
            grads[k ^ own[0], 0:UNIT] = flat[k * UNIT : (k + 1) * UNIT].astype(bf16)
            grads[k, UNIT : UNIT + GAIN_ROWS] = jnp.zeros((GAIN_ROWS, LANES), bf16)
        at = (UNITS - 1) ^ own[0]
        grads[at, UNIT : UNIT + GAIN_ROWS] = jnp.concatenate(
            [gains, jnp.zeros((GAIN_ROWS - 9, LANES), f32)], axis=0
        ).astype(bf16)


def by_buffer(*shape):
    zeros = (0,) * len(shape)
    return pl.BlockSpec((1,) + shape, lambda b, live, own: (b,) + zeros)


def whole(*shape):
    zeros = (0,) * len(shape)
    return pl.BlockSpec(shape, lambda b, live, own: zeros, pipeline_mode=pl.Buffered(1))


def quarter(which):
    return pl.BlockSpec((UNITS * UNIT, LANES), lambda b, live, own: (which, 0), pipeline_mode=pl.Buffered(1))


def call(kernel, name, buffers, in_specs, out_specs, outs, scratch, flops, moved, args):
    return pl.pallas_call(
        kernel,
        name=name,
        out_shape=[jax.ShapeDtypeStruct(shape, dtype) for shape, dtype in outs],
        grid_spec=pltpu.PrefetchScalarGridSpec(
            num_scalar_prefetch=2,
            grid=(buffers,),
            in_specs=in_specs,
            out_specs=out_specs,
            scratch_shapes=[pltpu.VMEM(shape, dtype) for shape, dtype in scratch],
        ),
        compiler_params=pltpu.CompilerParams(
            dimension_semantics=("arbitrary",), vmem_limit_bytes=60 * 1024 * 1024
        ),
        cost_estimate=pl.CostEstimate(flops=flops, bytes_accessed=moved, transcendentals=0),
    )(*args)


def run_attention_forward(live, own, tokens, st_row, st_col, cos, sin, units, gain):
    n, t, d = tokens.shape
    tiles = t // TILE
    return call(
        attention_forward, "attention_forward", n,
        [by_buffer(t, d), by_buffer(1, t), by_buffer(t, 1), by_buffer(HALF, t), by_buffer(HALF, t),
         whole(UNITS, UNIT, LANES), whole(1, d)],
        [by_buffer(d + KV_WIDTH, t), by_buffer(2 * KEY_VALUE_HEADS, t, HEAD_SIZE), by_buffer(d, t), by_buffer(t, d),
         by_buffer(KEY_VALUE_HEADS * tiles, 1, GROUP * TILE), whole(d, QKV_WIDTH), whole(d, d)],
        [((n, d + KV_WIDTH, t), bf16), ((n, 2 * KEY_VALUE_HEADS, t, HEAD_SIZE), bf16), ((n, d, t), bf16), ((n, t, d), f32),
         ((n, KEY_VALUE_HEADS * tiles, 1, GROUP * TILE), f32), ((d, QKV_WIDTH), bf16), ((d, d), bf16)],
        [((QKV_WIDTH, d), bf16), ((KEY_VALUE_HEADS, HEAD_SIZE, t), bf16), ((t, t), f32), ((UNITS * UNIT, LANES), f32),
         ((5, d, LANES), f32)],
        8 * 10**9, 20 * 10**6,
        (live, own, tokens, st_row, st_col, cos, sin, units, gain),
    )


def run_mlp(live, own, hidden, cot, st_col, rows, gain):
    n, t, d = hidden.shape
    f = FEEDFWD_UNITS
    return call(
        mlp, "mlp", n,
        [by_buffer(t, d), by_buffer(t, d), by_buffer(t, 1), quarter(1), quarter(2), quarter(3), whole(1, d)],
        [by_buffer(t, d), by_buffer(t, d), whole(UNITS, 3, UNIT, LANES), whole(1, d)],
        [((n, t, d), bf16), ((n, t, d), f32), ((UNITS, 3, UNIT, LANES), bf16), ((1, d), f32)],
        [((d, f), bf16), ((d, f), bf16), ((f, d), bf16), ((f, d), bf16), ((f, d), bf16), ((d, f), bf16),
         ((d, f), f32), ((d, f), f32), ((d, f), f32), ((t, d), bf16), ((d, t), bf16), ((t, d), bf16), ((d, t), bf16),
         ((t, d), f32), ((t, d), f32), ((UNITS * UNIT, LANES), f32), ((5, LANES, LANES), f32)],
        33 * 10**9, 30 * 10**6,
        (live, own, hidden, cot, st_col, rows, rows, rows, gain),
    )


def run_attention_backward(live, own, hgrad, tokens, qk_t, kv, mix_t, lse, st_row, st_col, cos, sin, w, wo, gain, dgain_two):
    n, t, d = tokens.shape
    tiles = t // TILE
    return call(
        attention_backward, "attention_backward", n,
        [by_buffer(t, d), by_buffer(t, d), by_buffer(d + KV_WIDTH, t), by_buffer(2 * KEY_VALUE_HEADS, t, HEAD_SIZE),
         by_buffer(d, t), by_buffer(KEY_VALUE_HEADS * tiles, 1, GROUP * TILE), by_buffer(1, t), by_buffer(t, 1),
         by_buffer(HALF, t), by_buffer(HALF, t), whole(d, QKV_WIDTH), whole(d, d), whole(1, d), whole(1, d)],
        [by_buffer(t, d), whole(UNITS, UNIT + GAIN_ROWS, LANES)],
        [((n, t, d), f32), ((UNITS, UNIT + GAIN_ROWS, LANES), bf16)],
        [((QKV_WIDTH, d), f32), ((d, d), f32), ((1, d), f32), ((t, t), f32), ((1, d, t), bf16),
         ((QUERY_HEADS, t, HEAD_SIZE), bf16), ((QUERY_HEADS, t, HEAD_SIZE), bf16), ((d, t), f32),
         ((KEY_VALUE_HEADS, t, HEAD_SIZE), f32), ((KEY_VALUE_HEADS, t, HEAD_SIZE), f32), ((QKV_WIDTH, t), bf16),
         ((UNITS * UNIT, LANES), f32), ((5, d, LANES), f32)],
        16 * 10**9, 40 * 10**6,
        (live, own, hgrad, tokens, qk_t, kv, mix_t, lse, st_row, st_col, cos, sin, w, wo, gain, dgain_two),
    )


def swap(x, bits):
    size = lax.axis_size("dp")
    return lax.ppermute(x, "dp", [(i, i ^ bits) for i in range(size)])


def plane(i):
    return i // UNITS


def relative_order(unit):
    z = plane(lax.axis_index("dp"))
    first = jnp.where(z == 0, unit, jnp.zeros_like(unit))
    for far in (3, 2, 1):
        first = first + lax.ppermute(unit, "dp", [(k, far * UNITS + k) for k in range(UNITS)])
    even = [first, swap(first, 2), swap(first, 4), swap(first, 6)]
    units = []
    for piece in even:
        units += [piece, swap(piece, 1)]
    return jnp.stack(units)


def spread_last(rows):
    size = lax.axis_size("dp")
    have = [size - 1]
    me = lax.axis_index("dp")
    rows = jnp.where(me == size - 1, rows, jnp.zeros_like(rows))
    bits = 1
    while bits < size:
        rows = rows + lax.ppermute(rows, "dp", [(i, i ^ bits) for i in have])
        have = have + [i ^ bits for i in have]
        bits *= 2
    return rows


def reduce_in_plane(grads):
    other = swap(grads[1::2], 1)
    both = grads[0::2].astype(f32) + other.astype(f32)
    low = both.astype(bf16)
    return ((both[0] + swap(low[1], 2).astype(f32)) + (swap(low[2], 4).astype(f32) + swap(low[3], 6).astype(f32)))


def add_up(value):
    value = value + swap(value, 1)
    value = (value + swap(value, 2)) + (swap(value, 4) + swap(value, 6))
    return (value + swap(value, 8)) + (swap(value, 16) + swap(value, 24))


def local(tokens, doc_starts, cotangent, master, moment_one, moment_two):
    size = lax.axis_size("dp")
    me = lax.axis_index("dp")
    rows = tokens.shape[1]
    shard = master.shape[0] // LANES
    total = 4 * UNITS * UNIT
    by_units = size == 4 * UNITS and shard == UNIT + 1
    own_rows = master.reshape(shard, LANES)
    if by_units:
        own = me % UNITS
        before = lax.ppermute(own_rows[shard - size :], "dp", [(i, i + 1) for i in range(size - 1)])
        unit = lax.dynamic_slice_in_dim(jnp.concatenate([before, own_rows], axis=0), size - me, UNIT).astype(bf16)
        gain_at = total - (size - 1) * shard
        gain_rows = spread_last(own_rows[gain_at : gain_at + GAIN_ROWS].astype(bf16))
        units = relative_order(unit)
        all_rows = lax.all_gather(unit, "dp", axis=0, tiled=True)
    else:
        own = jnp.zeros_like(me)
        all_rows = lax.all_gather(own_rows.astype(bf16), "dp", axis=0, tiled=True)
        gain_rows = all_rows[total : total + GAIN_ROWS]
        units = all_rows[: UNITS * UNIT].reshape(UNITS, UNIT, LANES)
    gains = gain_rows.reshape(-1)[: 2 * MODEL_WIDTH].reshape(2, MODEL_WIDTH).astype(f32)
    gain_one, gain_two = gains[0:1], gains[1:2]
    own = own.astype(jnp.int32).reshape(1)

    is_live = doc_starts < rows
    live = jnp.sum(is_live.astype(jnp.int32), axis=1) // TILE
    positions = jnp.where(is_live, jnp.arange(rows) - doc_starts, 0).astype(f32)
    frequency = rope_base ** (-(jnp.arange(HALF, dtype=f32) * 2.0 / HEAD_SIZE))
    angles = frequency[None, :, None] * positions[:, None, :]
    cos, sin = jnp.cos(angles), jnp.sin(angles)
    st_row, st_col = doc_starts[:, None, :], doc_starts[:, :, None]

    qk_t, kv, mix_t, hidden, lse, w, wo = run_attention_forward(
        live, own, tokens, st_row, st_col, cos, sin, units, gain_one
    )
    layer, hgrad, late, dgain_two = run_mlp(live, own, hidden, cotangent, st_col, all_rows, gain_two)
    igrad, early = run_attention_backward(
        live, own, hgrad, tokens, qk_t, kv, mix_t, lse, st_row, st_col, cos, sin, w, wo, gain_one, dgain_two
    )
    if by_units:
        z = plane(me)
        last = size // UNITS - 1
        late_sum = reduce_in_plane(late)
        mine = lax.dynamic_index_in_dim(late_sum, jnp.maximum(z - 1, 0), 0, keepdims=False)
        for far in (1, 2, 3):
            to = z ^ far
            sent = lax.dynamic_index_in_dim(late_sum, jnp.maximum(to - 1, 0), 0, keepdims=False).astype(bf16)
            pairs = [(i, i ^ (far * UNITS)) for i in range(size) if plane(i ^ (far * UNITS)) > 0]
            mine = mine + lax.ppermute(sent, "dp", pairs).astype(f32)
        early_sum = reduce_in_plane(early)
        early_low = early_sum.astype(bf16)
        first = early_sum[:UNIT]
        gain_grads = early_sum[UNIT:]
        for far in (1, 2, 3):
            sent = lax.ppermute(early_low[:UNIT], "dp", [(far * UNITS + k, k) for k in range(UNITS)])
            first = first + sent.astype(f32)
            top = [((last ^ far) * UNITS + k, last * UNITS + k) for k in range(UNITS)]
            gain_grads = gain_grads + lax.ppermute(early_low[UNIT:], "dp", top).astype(f32)
        unit_grad = jnp.where(z == 0, first, mine)
        gain_grads = jnp.where(me == size - 1, gain_grads, 0.0)
        square_sum = add_up((jnp.sum(unit_grad * unit_grad) + jnp.sum(gain_grads * gain_grads)).reshape(1, 1))[0, 0]
        after = lax.ppermute(unit_grad[:size], "dp", [(i + 1, i) for i in range(size - 1)])
        after = after + jnp.pad(gain_grads, ((0, size - GAIN_ROWS), (0, 0)))
        grad_shard = lax.dynamic_slice_in_dim(jnp.concatenate([unit_grad, after], axis=0), me, shard).reshape(-1)
    else:
        pieces = [early[:, :UNIT].reshape(-1, LANES)] + [late[:, p].reshape(-1, LANES) for p in range(3)]
        grads = jnp.concatenate(pieces + [early[UNITS - 1, UNIT:]], axis=0).astype(f32)
        grads = jnp.pad(grads, ((0, size * shard - grads.shape[0]), (0, 0)))
        grad_shard = lax.psum_scatter(grads.reshape(-1), "dp", scatter_dimension=0, tiled=True)
        square_sum = lax.psum(jnp.sum(grad_shard * grad_shard), "dp")
    grad_norm = jnp.sqrt(square_sum)
    clipped = grad_shard * (clip_norm / jnp.maximum(grad_norm, clip_norm))
    new_one = decay_one * moment_one + (1.0 - decay_one) * clipped
    new_two = decay_two * moment_two + (1.0 - decay_two) * clipped * clipped
    corrected_one = new_one / (1.0 - decay_one**STEP)
    corrected_two = new_two / (1.0 - decay_two**STEP)
    new_master = master - learn_rate * (
        corrected_one / (jnp.sqrt(corrected_two) + adam_eps) + weight_decay * master
    )
    return (layer, igrad, grad_shard, grad_norm, new_master, new_one, new_two)


def solution(mesh):
    flat, cube = P("dp"), P("dp", None, None)
    return jax.shard_map(
        local,
        mesh=mesh,
        in_specs=(cube, P("dp", None), cube, flat, flat, flat),
        out_specs=(cube, cube, flat, P(), flat, flat, flat),
        check_vma=False,
    )
```

```python
import functools

import jax
import jax.numpy as jnp
from jax import lax
from jax.experimental import pallas as pl
from jax.experimental.pallas import tpu as pltpu
from jax.sharding import PartitionSpec as P

MODEL_WIDTH = 576
QUERY_HEADS = 9
KEY_VALUE_HEADS = 3
HEAD_SIZE = 64
FEEDFWD_UNITS = 1536
TILE = 128
STEP = 8
GROUP = QUERY_HEADS // KEY_VALUE_HEADS
HALF = HEAD_SIZE // 2
KV_WIDTH = KEY_VALUE_HEADS * HEAD_SIZE
QKV_WIDTH = MODEL_WIDTH + 2 * KV_WIDTH
CHUNK = 512
LANES = 128
UNIT = MODEL_WIDTH * KV_WIDTH // LANES
GAIN_ROWS = 16
UNITS = 8
FEEDFWD_TILES = FEEDFWD_UNITS // LANES

rms_eps = 1e-05
rope_base = 100000.0
learn_rate = 0.02
decay_one = 0.9
decay_two = 0.999
adam_eps = 1e-08
weight_decay = 0.1
clip_norm = 1.0
mask_fill = -1000000000.0

bf16 = jnp.bfloat16
f32 = jnp.float32


def mm(a, b):
    return jnp.dot(a, b, preferred_element_type=f32)


def inverse_rms(x):
    return lax.rsqrt(jnp.mean(x * x, axis=0, keepdims=True) + rms_eps)


def spread(gain, tokens):
    return jnp.concatenate([gain] * (tokens // LANES), axis=1)


def fold(x):
    return sum(x[:, t : t + LANES] for t in range(0, x.shape[1], LANES))


def norm_back(x, inverse, gain, grad):
    e = grad * gain
    return inverse * e - x * (inverse * inverse * inverse) * jnp.mean(e * x, axis=0, keepdims=True)


def fill_bias(bias, starts_row):
    rows = starts_row.shape[1]
    starts_col = jnp.broadcast_to(starts_row, (TILE, rows)).T
    key_at = lax.broadcasted_iota(jnp.int32, (rows, TILE), 0)
    for i in range(rows // TILE):
        width = (i + 1) * TILE
        query_at = lax.broadcasted_iota(jnp.int32, (rows, TILE), 1) + i * TILE
        allowed = (starts_col == starts_row[:, i * TILE : width]) & (key_at <= query_at)
        bias[:, i * TILE : width] = jnp.where(allowed, 0.0, mask_fill)


def half_turn(x):
    return pltpu.roll(x, HEAD_SIZE, 1)


def to_matrix(flat, base, out, pairs, tiles):
    half = tiles // 2
    low = lax.broadcasted_iota(jnp.int32, (pairs, LANES), 1) < HEAD_SIZE
    for t in range(half + 1):
        out[t, pl.ds(0, pairs, stride=2), :] = flat[pl.ds(base + t, pairs, stride=tiles), :]
    turned = half_turn(flat[pl.ds(base + half, pairs, stride=tiles), :])
    for t in range(half):
        following = half_turn(flat[pl.ds(base + half + t + 1, pairs, stride=tiles), :])
        out[t, pl.ds(1, pairs, stride=2), :] = jnp.where(low, turned, following)
        turned = following
    out[half, pl.ds(1, pairs, stride=2), :] = turned


def to_flat(matrix, flat, base, pairs, tiles):
    half = tiles // 2
    low = lax.broadcasted_iota(jnp.int32, (pairs, LANES), 1) < HEAD_SIZE
    for t in range(half):
        flat[pl.ds(base + t, pairs, stride=tiles), :] = matrix[t, pl.ds(0, pairs, stride=2), :]
    before = matrix[half, pl.ds(0, pairs, stride=2), :]
    for t in range(half + 1):
        turned = half_turn(matrix[t, pl.ds(1, pairs, stride=2), :])
        flat[pl.ds(base + half + t, pairs, stride=tiles), :] = jnp.where(low, before, turned)
        before = turned


def columns_of(matrix, rows, width):
    full = width // LANES
    return jnp.concatenate([matrix[t, :rows] for t in range(full)] + [matrix[full, :rows, :HEAD_SIZE]], axis=1)


def put_columns(matrix, value):
    rows, width = value.shape
    full = width // LANES
    for t in range(full):
        matrix[t, :rows] = value[:, t * LANES : (t + 1) * LANES]
    matrix[full, :rows, :HEAD_SIZE] = value[:, full * LANES :]


def head_rows(ref, g, columns):
    return jnp.concatenate(
        [ref[0, pl.ds((g * GROUP + h) * HEAD_SIZE, HEAD_SIZE), columns] for h in range(GROUP)], axis=1
    )


def attention_forward(
    live, own, tok, st_row, cos, sin, units,
    qk_t, kv, mix_t, hidden, lse, w, wo, gains,
    w_t, wo_t, v_t, bias, flat, square, gain
):
    b = pl.program_id(0)
    rows = tok.shape[2]

    @pl.when(b == 0)
    def _():
        for k in range(UNITS):
            flat[k * UNIT : (k + 1) * UNIT] = units[k ^ own[0], 0:UNIT].astype(f32)
        pairs = MODEL_WIDTH // 2
        to_matrix(flat, 5 * UNIT, square, pairs, 9)
        value = columns_of(square, MODEL_WIDTH, MODEL_WIDTH)
        wo[...] = value.astype(bf16)
        wo_t[...] = value.T.astype(bf16)
        to_matrix(flat, 0, square, pairs, 9)
        value = columns_of(square, MODEL_WIDTH, MODEL_WIDTH)
        w[:, 0:MODEL_WIDTH] = value.astype(bf16)
        w_t[0:MODEL_WIDTH] = value.T.astype(bf16)
        for which in range(2):
            at = MODEL_WIDTH + which * KV_WIDTH
            to_matrix(flat, (3 + which) * UNIT, square, pairs, 3)
            value = columns_of(square, MODEL_WIDTH, KV_WIDTH)
            w[:, at : at + KV_WIDTH] = value.astype(bf16)
            w_t[at : at + KV_WIDTH] = value.T.astype(bf16)
        tail = units[(UNITS - 1) ^ own[0], UNIT : UNIT + GAIN_ROWS].astype(f32)
        line = jnp.concatenate([tail[j : j + 1] for j in range(9)], axis=1)
        for which in range(2):
            one = line[:, which * MODEL_WIDTH : (which + 1) * MODEL_WIDTH]
            gains[which] = jnp.broadcast_to(one, (LANES, MODEL_WIDTH)).T
        gain[...] = gains[0]

    @pl.when(live[b] > 0)
    def _():
        x = tok[0].astype(f32)
        n1_t = (x * inverse_rms(x) * spread(gain[...], rows)).astype(bf16)
        c, s = cos[0], sin[0]
        for h in range(QUERY_HEADS + KEY_VALUE_HEADS):
            at = h * HEAD_SIZE
            u = mm(w_t[at : at + HEAD_SIZE], n1_t)
            u1, u2 = u[:HALF], u[HALF:]
            r = jnp.concatenate([u1 * c - u2 * s, u2 * c + u1 * s], axis=0)
            if h < QUERY_HEADS:
                r = r * HEAD_SIZE ** (-0.5)
            r = r.astype(bf16)
            qk_t[0, at : at + HEAD_SIZE] = r
            if h >= QUERY_HEADS:
                kv[0, h - QUERY_HEADS] = r.T
        for g in range(KEY_VALUE_HEADS):
            at = MODEL_WIDTH + KV_WIDTH + g * HEAD_SIZE
            v = mm(w_t[at : at + HEAD_SIZE], n1_t).astype(bf16)
            v_t[g] = v
            kv[0, KEY_VALUE_HEADS + g] = v.T
        fill_bias(bias, st_row[0])
        mix_t[...] = jnp.zeros_like(mix_t)

        def group(g, carry):
            for i in range(rows // TILE):

                @pl.when(i < live[b])
                def _():
                    width = (i + 1) * TILE
                    cols = slice(i * TILE, width)
                    q_t = head_rows(qk_t, g, cols)
                    mask = bias[:width, cols]
                    scores = mm(kv[0, g, :width], q_t) + jnp.concatenate([mask] * GROUP, axis=1)
                    peak = jnp.max(scores, axis=0, keepdims=True)
                    e = jnp.exp(scores - peak)
                    total = jnp.sum(e, axis=0, keepdims=True)
                    prob = (e * (1.0 / total)).astype(bf16)
                    lse[0, g * (rows // TILE) + i] = peak + jnp.log(total)
                    out = mm(v_t[g, :, :width], prob).astype(bf16)
                    for h in range(GROUP):
                        mix_t[0, pl.ds((g * GROUP + h) * HEAD_SIZE, HEAD_SIZE), cols] = out[
                            :, h * TILE : (h + 1) * TILE
                        ]

            return carry

        lax.fori_loop(0, KEY_VALUE_HEADS, group, 0)
        hidden[0] = tok[0].astype(f32) + mm(wo_t[...], mix_t[0])


def mlp(
    live, own, hidden, cot, st_row, gate_rows, up_rows, down_rows, gains,
    layer, hgrad, keep, send, dgain,
    wg, wu, wd, wg_t, wu_t, wd_t, dwg_t, dwu_t, dwd, n2, n2_t, rl, rl_t, n2g, res, flat, slab
):
    b = pl.program_id(0)
    rows = hidden.shape[2]

    @pl.when(b == 0)
    def _():
        for rows_in, straight, turned in ((gate_rows, wg, wg_t), (up_rows, wu, wu_t)):
            flat[...] = rows_in[...].astype(f32)
            for j in range(FEEDFWD_TILES):
                at = slice(j * LANES, (j + 1) * LANES)
                part = flat[pl.ds(j, MODEL_WIDTH, stride=FEEDFWD_TILES), :]
                straight[:, at] = part.astype(bf16)
                turned[at] = part.T.astype(bf16)
        flat[...] = down_rows[...].astype(f32)
        for j in range(FEEDFWD_TILES):
            at = slice(j * LANES, (j + 1) * LANES)
            to_matrix(flat, j * MODEL_WIDTH, slab, LANES // 2, 9)
            value = columns_of(slab, LANES, MODEL_WIDTH)
            wd[at] = value.astype(bf16)
            wd_t[:, at] = value.T.astype(bf16)
        dwg_t[...] = jnp.zeros_like(dwg_t)
        dwu_t[...] = jnp.zeros_like(dwu_t)
        dwd[...] = jnp.zeros_like(dwd)
        dgain[...] = jnp.zeros_like(dgain)

    @pl.when(live[b] == 0)
    def _():
        layer[...] = jnp.zeros_like(layer)
        hgrad[...] = jnp.zeros_like(hgrad)

    @pl.when(live[b] > 0)
    def _():
        x = hidden[0]
        inverse = inverse_rms(x)
        alive = st_row[0] < rows
        normed = (x * inverse * spread(gains[1], rows)).astype(bf16)
        n2_t[...] = normed
        n2[...] = normed.T
        grad = jnp.where(alive, cot[0].astype(f32), 0.0).astype(bf16)
        rl_t[...] = grad
        rl[...] = grad.T
        res[...] = jnp.zeros_like(res)
        n2g[...] = jnp.zeros_like(n2g)

        def chunk(k, carry):
            at = pl.ds(pl.multiple_of(k * CHUNK, CHUNK), CHUNK)
            pre = mm(wg_t[at, :], n2_t[...])
            up = mm(wu_t[at, :], n2_t[...])
            ag = mm(wd[at, :], rl_t[...])
            s = jax.nn.sigmoid(pre)
            silu = pre * s
            act = (silu * up).astype(bf16)
            gl = (ag * up * s * (1.0 + pre * (1.0 - s))).astype(bf16)
            ul = (ag * silu).astype(bf16)
            res[...] += mm(wd_t[:, at], act)
            n2g[...] += mm(wg[:, at], gl) + mm(wu[:, at], ul)
            dwd[at, :] += mm(act, rl[...])
            dwg_t[at, :] += mm(gl, n2[...])
            dwu_t[at, :] += mm(ul, n2[...])
            return carry

        lax.fori_loop(0, FEEDFWD_UNITS // CHUNK, chunk, 0)
        x = hidden[0]
        layer[0] = jnp.where(alive, x + res[...], 0.0).astype(bf16)
        ng = n2g[...]
        dgain[...] += fold(ng * x * inverse)
        hgrad[0] = rl_t[...].astype(f32) + norm_back(x, inverse, spread(gains[1], rows), ng)

    @pl.when(b == pl.num_programs(0) - 1)
    def _():
        for p in range(3):
            for j in range(FEEDFWD_TILES):
                at = slice(j * LANES, (j + 1) * LANES)
                if p < 2:
                    flat[pl.ds(j, MODEL_WIDTH, stride=FEEDFWD_TILES), :] = (dwg_t, dwu_t)[p][at].T
                else:
                    put_columns(slab, dwd[at])
                    to_flat(slab, flat, j * MODEL_WIDTH, LANES // 2, 9)
            for k in range(UNITS):
                place = k ^ own[0]

                @pl.when(place % 2 == 0)
                def _():
                    keep[place // 2, p] = flat[k * UNIT : (k + 1) * UNIT].astype(bf16)

                @pl.when(place % 2 == 1)
                def _():
                    send[place // 2, p] = flat[k * UNIT : (k + 1) * UNIT].astype(bf16)


def attention_backward(
    lo, final, live, own, hgrad, tok, qk_t, kv, mix_t, lse, st_row, cos, sin, w, wo, gains, *refs
):
    if final:
        dgain_two, dw_in, dwo_in, dgain_in, _, igrad, keep, send = refs[:8]
        bias, mg_t, mg, q, dq, dk, dv, low_t, flat, square, dw_t, dwo, dgain = refs[8:]
    else:
        igrad, dw_t, dwo, dgain = refs[:4]
        bias, mg_t, mg, q, dq, dk, dv, low_t = refs[4:]
    b = pl.program_id(0) + lo
    rows = tok.shape[2]
    tiles = rows // TILE
    scale = HEAD_SIZE ** (-0.5)

    @pl.when(b == lo)
    def _():
        if final:
            dw_t[...] = dw_in[...]
            dwo[...] = dwo_in[...]
            dgain[...] = dgain_in[...]
        else:
            dw_t[...] = jnp.zeros_like(dw_t)
            dwo[...] = jnp.zeros_like(dwo)
            dgain[...] = jnp.zeros_like(dgain)

    @pl.when(live[b] == 0)
    def _():
        igrad[...] = jnp.zeros_like(igrad)

    @pl.when(live[b] > 0)
    def _():
        hl_t = hgrad[0].astype(bf16)
        dwo[...] += mm(mix_t[0], hl_t.T)
        mg_t[0] = mm(wo[...], hl_t).astype(bf16)
        for h in range(QUERY_HEADS):
            at = slice(h * HEAD_SIZE, (h + 1) * HEAD_SIZE)
            mg[h] = mg_t[0, at].T
            q[h] = qk_t[0, at].T
        fill_bias(bias, st_row[0])
        dq[...] = jnp.zeros_like(dq)
        dk[...] = jnp.zeros_like(dk)
        dv[...] = jnp.zeros_like(dv)

        def group(g, carry):
            for i in range(tiles):

                @pl.when(i < live[b])
                def _():
                    width = (i + 1) * TILE
                    cols = slice(i * TILE, width)
                    q_t = head_rows(qk_t, g, cols)
                    mask = bias[:width, cols]
                    scores = mm(kv[0, g, :width], q_t) + jnp.concatenate([mask] * GROUP, axis=1)
                    prob = jnp.exp(scores - lse[0, g * tiles + i])
                    dp = mm(kv[0, KEY_VALUE_HEADS + g, :width], head_rows(mg_t, g, cols))
                    delta = jnp.sum(prob * dp, axis=0, keepdims=True)
                    ds = (prob * (dp - delta)).astype(bf16)
                    low = prob.astype(bf16)
                    k_t = qk_t[0, pl.ds(MODEL_WIDTH + g * HEAD_SIZE, HEAD_SIZE), :width]
                    dq_i = mm(k_t, ds) * scale
                    for h in range(GROUP):
                        dq[pl.ds((g * GROUP + h) * HEAD_SIZE, HEAD_SIZE), cols] = dq_i[
                            :, h * TILE : (h + 1) * TILE
                        ]
                    q_i = jnp.concatenate([q[g * GROUP + h, cols] for h in range(GROUP)], axis=0)
                    mg_i = jnp.concatenate([mg[g * GROUP + h, cols] for h in range(GROUP)], axis=0)
                    dk[g, :width] += mm(ds, q_i)
                    dv[g, :width] += mm(low, mg_i)

            return carry

        lax.fori_loop(0, KEY_VALUE_HEADS, group, 0)
        c, s = cos[0], sin[0]
        for h in range(QUERY_HEADS + KEY_VALUE_HEADS):
            at = h * HEAD_SIZE
            u = dq[at : at + HEAD_SIZE] if h < QUERY_HEADS else dk[h - QUERY_HEADS].T
            u1, u2 = u[:HALF], u[HALF:]
            r = jnp.concatenate([u1 * c + u2 * s, u2 * c - u1 * s], axis=0)
            low_t[at : at + HEAD_SIZE] = r.astype(bf16)
        for g in range(KEY_VALUE_HEADS):
            at = MODEL_WIDTH + KV_WIDTH + g * HEAD_SIZE
            low_t[at : at + HEAD_SIZE] = dv[g].T.astype(bf16)
        x = tok[0].astype(f32)
        inverse = inverse_rms(x)
        gain = spread(gains[0], rows)
        dw_t[...] += mm(low_t[...], (x * inverse * gain).astype(bf16).T)
        ng = mm(w[...], low_t[...])
        dgain[...] += fold(ng * x * inverse)
        igrad[0] = hgrad[0] + norm_back(x, inverse, gain, ng)

    if not final:
        return

    @pl.when(pl.program_id(0) == pl.num_programs(0) - 1)
    def _():
        pairs = MODEL_WIDTH // 2
        put_columns(square, dw_t[0:MODEL_WIDTH].T)
        to_flat(square, flat, 0, pairs, 9)
        for which in range(2):
            at = MODEL_WIDTH + which * KV_WIDTH
            put_columns(square, dw_t[at : at + KV_WIDTH].T)
            to_flat(square, flat, (3 + which) * UNIT, pairs, 3)
        put_columns(square, dwo[...])
        to_flat(square, flat, 5 * UNIT, pairs, 9)
        lines = [jnp.sum(d[...].T, axis=0, keepdims=True) for d in (dgain, dgain_two)]
        line = jnp.concatenate(lines, axis=1)
        tail = [line[:, j * LANES : (j + 1) * LANES] for j in range(9)]
        tail = jnp.concatenate(tail + [jnp.zeros((GAIN_ROWS - 9, LANES), f32)], axis=0).astype(bf16)
        for k in range(UNITS):
            place = k ^ own[0]
            ours = tail if k == UNITS - 1 else jnp.zeros_like(tail)

            @pl.when(place % 2 == 0)
            def _():
                keep[place // 2, 0:UNIT] = flat[k * UNIT : (k + 1) * UNIT].astype(bf16)
                keep[place // 2, UNIT : UNIT + GAIN_ROWS] = ours

            @pl.when(place % 2 == 1)
            def _():
                send[place // 2, 0:UNIT] = flat[k * UNIT : (k + 1) * UNIT].astype(bf16)
                send[place // 2, UNIT : UNIT + GAIN_ROWS] = ours


def by_buffer(*shape, lo=0):
    zeros = (0,) * len(shape)
    return pl.BlockSpec((1,) + shape, lambda b, live, own: (b + lo if lo else b,) + zeros)


def whole(*shape):
    zeros = (0,) * len(shape)
    return pl.BlockSpec(shape, lambda b, live, own: zeros, pipeline_mode=pl.Buffered(1))


def quarter(which):
    return pl.BlockSpec((UNITS * UNIT, LANES), lambda b, live, own: (which, 0), pipeline_mode=pl.Buffered(1))


def call(kernel, name, buffers, in_specs, out_specs, outs, scratch, flops, moved, args, aliases=None):
    return pl.pallas_call(
        kernel,
        name=name,
        out_shape=[jax.ShapeDtypeStruct(shape, dtype) for shape, dtype in outs],
        grid_spec=pltpu.PrefetchScalarGridSpec(
            num_scalar_prefetch=2,
            grid=(buffers,),
            in_specs=in_specs,
            out_specs=out_specs,
            scratch_shapes=[pltpu.VMEM(shape, dtype) for shape, dtype in scratch],
        ),
        input_output_aliases=aliases or {},
        compiler_params=pltpu.CompilerParams(
            dimension_semantics=("arbitrary",), vmem_limit_bytes=60 * 1024 * 1024
        ),
        cost_estimate=pl.CostEstimate(flops=flops, bytes_accessed=moved, transcendentals=0),
    )(*args)


def run_attention_forward(live, own, tokens, st_row, cos, sin, units):
    n, d, t = tokens.shape
    lines = KEY_VALUE_HEADS * (t // TILE)
    return call(
        attention_forward, "attention_forward", n,
        [by_buffer(d, t), by_buffer(1, t), by_buffer(HALF, t), by_buffer(HALF, t), whole(UNITS, UNIT + GAIN_ROWS, LANES)],
        [by_buffer(d + KV_WIDTH, t), by_buffer(2 * KEY_VALUE_HEADS, t, HEAD_SIZE), by_buffer(d, t), by_buffer(d, t),
         by_buffer(lines, 1, GROUP * TILE), whole(d, QKV_WIDTH), whole(d, d), whole(2, d, LANES)],
        [((n, d + KV_WIDTH, t), bf16), ((n, 2 * KEY_VALUE_HEADS, t, HEAD_SIZE), bf16), ((n, d, t), bf16), ((n, d, t), f32),
         ((n, lines, 1, GROUP * TILE), f32), ((d, QKV_WIDTH), bf16), ((d, d), bf16), ((2, d, LANES), f32)],
        [((QKV_WIDTH, d), bf16), ((d, d), bf16), ((KEY_VALUE_HEADS, HEAD_SIZE, t), bf16), ((t, t), f32),
         ((UNITS * UNIT, LANES), f32), ((5, d, LANES), f32), ((d, LANES), f32)],
        8 * 10**9, 20 * 10**6,
        (live, own, tokens, st_row, cos, sin, units),
    )


def run_mlp(live, own, hidden, cot, st_row, rows, gains):
    n, d, t = hidden.shape
    f = FEEDFWD_UNITS
    half = (UNITS // 2, 3, UNIT, LANES)
    return call(
        mlp, "mlp", n,
        [by_buffer(d, t), by_buffer(d, t), by_buffer(1, t), quarter(1), quarter(2), quarter(3), whole(2, d, LANES)],
        [by_buffer(d, t), by_buffer(d, t), whole(*half), whole(*half), whole(d, LANES)],
        [((n, d, t), bf16), ((n, d, t), f32), (half, bf16), (half, bf16), ((d, LANES), f32)],
        [((d, f), bf16), ((d, f), bf16), ((f, d), bf16), ((f, d), bf16), ((f, d), bf16), ((d, f), bf16),
         ((f, d), f32), ((f, d), f32), ((f, d), f32), ((t, d), bf16), ((d, t), bf16), ((t, d), bf16), ((d, t), bf16),
         ((d, t), f32), ((d, t), f32), ((UNITS * UNIT, LANES), f32), ((5, LANES, LANES), f32)],
        33 * 10**9, 30 * 10**6,
        (live, own, hidden, cot, st_row, rows, rows, rows, gains),
    )


def run_attention_backward(lo, hi, live, own, hgrad, tokens, qk_t, kv, mix_t, lse, st_row, cos, sin, w, wo, gains, so_far=None):
    n, d, t = tokens.shape
    lines = KEY_VALUE_HEADS * (t // TILE)
    final = so_far is not None
    sums = [((QKV_WIDTH, d), f32), ((d, d), f32), ((d, LANES), f32)]
    of = functools.partial(by_buffer, lo=lo)
    in_specs = [of(d, t), of(d, t), of(d + KV_WIDTH, t), of(2 * KEY_VALUE_HEADS, t, HEAD_SIZE), of(d, t), of(lines, 1, GROUP * TILE),
                of(1, t), of(HALF, t), of(HALF, t), whole(d, QKV_WIDTH), whole(d, d), whole(2, d, LANES)]
    args = [live, own, hgrad, tokens, qk_t, kv, mix_t, lse, st_row, cos, sin, w, wo, gains]
    out_specs, outs = [of(d, t)], [((n, d, t), f32)]
    scratch = [((t, t), f32), ((1, d, t), bf16), ((QUERY_HEADS, t, HEAD_SIZE), bf16), ((QUERY_HEADS, t, HEAD_SIZE), bf16),
               ((d, t), f32), ((KEY_VALUE_HEADS, t, HEAD_SIZE), f32), ((KEY_VALUE_HEADS, t, HEAD_SIZE), f32), ((QKV_WIDTH, t), bf16)]
    aliases = {}
    if final:
        half = (UNITS // 2, UNIT + GAIN_ROWS, LANES)
        in_specs += [whole(d, LANES)] + [whole(*shape) for shape, _ in sums] + [pl.BlockSpec(memory_space=pl.ANY)]
        args += list(so_far)
        aliases = {len(args) - 1: 0}
        out_specs += [whole(*half)] * 2
        outs += [(half, bf16)] * 2
        scratch += [((UNITS * UNIT, LANES), f32), ((5, d, LANES), f32)] + sums
    else:
        out_specs += [whole(*shape) for shape, _ in sums]
        outs += sums
    return call(
        functools.partial(attention_backward, lo, final), "attention_backward", hi - lo,
        in_specs, out_specs, outs, scratch, 8 * 10**9, 20 * 10**6, args, aliases,
    )


def swap(x, bits):
    size = lax.axis_size("dp")
    return lax.ppermute(x, "dp", [(i, i ^ bits) for i in range(size)])


def plane(i):
    return i // UNITS


def relative_order(rows):
    size = lax.axis_size("dp")
    last = size // UNITS - 1
    first = rows
    for far in (3, 2, 1):
        pairs = [(k, far * UNITS + k) for k in range(UNITS)] + [(size - 1, (last - far) * UNITS + UNITS - 1)]
        first = first + lax.ppermute(rows, "dp", pairs)
    even = [first, swap(first, 2), swap(first, 4), swap(first, 6)]
    units = []
    for piece in even:
        units += [piece, swap(piece, 1)]
    return jnp.stack(units)


def core_sums(keep, send):
    other = swap(send, 1)
    sums = [keep[j].astype(f32) + other[j].astype(f32) for j in range(UNITS // 2)]
    return [sums[0]] + [s.astype(bf16) for s in sums[1:]]


def to_plane(two, four, six):
    return [swap(two, 2), swap(four, 4), swap(six, 6)]


def plane_sums(own, two, four, six):
    return (own + two.astype(f32)) + (four.astype(f32) + six.astype(f32))


def add_up(value):
    bits = 1
    while bits < lax.axis_size("dp"):
        value = value + swap(value, bits)
        bits *= 2
    return value


def local(tokens, doc_starts, cotangent, master, moment_one, moment_two):
    size = lax.axis_size("dp")
    me = lax.axis_index("dp")
    z = plane(me)
    buffers, rows = tokens.shape[:2]
    shard = master.shape[0] // LANES
    total = 4 * UNITS * UNIT
    by_units = size == 4 * UNITS and shard == UNIT + 1
    own_rows = master.reshape(shard, LANES)
    if by_units:
        own = me % UNITS
        before = lax.ppermute(own_rows[shard - size :], "dp", [(i, i + 1) for i in range(size - 1)])
        unit = lax.dynamic_slice_in_dim(jnp.concatenate([before, own_rows], axis=0), size - me, UNIT).astype(bf16)
        gain_at = total - (size - 1) * shard
        gain_rows = own_rows[gain_at : gain_at + GAIN_ROWS].astype(bf16)
        units = relative_order(
            jnp.concatenate(
                [jnp.where(z == 0, unit, jnp.zeros_like(unit)), jnp.where(me == size - 1, gain_rows, jnp.zeros_like(gain_rows))],
                axis=0,
            )
        )
        all_rows = lax.all_gather(unit, "dp", axis=0, tiled=True)
    else:
        own = jnp.zeros_like(me)
        all_rows = lax.all_gather(own_rows.astype(bf16), "dp", axis=0, tiled=True)
        units = all_rows[: UNITS * UNIT].reshape(UNITS, UNIT, LANES)
        gain_rows = jnp.pad(all_rows[None, total : total + GAIN_ROWS], ((UNITS - 1, 0), (0, 0), (0, 0)))
        units = jnp.concatenate([units, gain_rows], axis=1)
    own = own.astype(jnp.int32).reshape(1)

    is_live = doc_starts < rows
    live = jnp.sum(is_live.astype(jnp.int32), axis=1) // TILE
    positions = jnp.where(is_live, jnp.arange(rows) - doc_starts, 0).astype(f32)
    frequency = rope_base ** (-(jnp.arange(HALF, dtype=f32) * 2.0 / HEAD_SIZE))
    angles = frequency[None, :, None] * positions[:, None, :]
    cos, sin = jnp.cos(angles), jnp.sin(angles)
    st_row = doc_starts.astype(f32)[:, None, :]
    tok_t, cot_t = tokens.transpose(0, 2, 1), cotangent.transpose(0, 2, 1)

    qk_t, kv, mix_t, hidden, lse, w, wo, gains = run_attention_forward(live, own, tok_t, st_row, cos, sin, units)
    layer, hgrad, keep, send, dgain_two = run_mlp(live, own, hidden, cot_t, st_row, all_rows, gains)
    shared = (live, own, hgrad, tok_t, qk_t, kv, mix_t, lse, st_row, cos, sin, w, wo, gains)
    igrad, dw_t, dwo, dgain = run_attention_backward(0, buffers // 2, *shared)
    if by_units:
        late = core_sums(keep, send)
        dgain, *late = lax.optimization_barrier((dgain, *late))
        arrived = to_plane(*late[1:])
    igrad, keep_early, send_early = run_attention_backward(
        buffers // 2, buffers, *shared, so_far=(dgain_two, dw_t, dwo, dgain, igrad)
    )
    if by_units:
        last = size // UNITS - 1
        keep_early, send_early, *arrived = lax.optimization_barrier((keep_early, send_early, *arrived))
        late_sum = plane_sums(late[0], *arrived)
        mine = lax.dynamic_index_in_dim(late_sum, jnp.maximum(z - 1, 0), 0, keepdims=False)
        sent = [
            lax.dynamic_index_in_dim(late_sum, jnp.maximum((z ^ far) - 1, 0), 0, keepdims=False).astype(bf16)
            for far in (1, 2, 3)
        ]
        send_early, *sent = lax.optimization_barrier((send_early, *sent))
        for far in (1, 2, 3):
            pairs = [(i, i ^ (far * UNITS)) for i in range(size) if plane(i ^ (far * UNITS)) > 0]
            sent[far - 1] = lax.ppermute(sent[far - 1], "dp", pairs)
        early = core_sums(keep_early, send_early)
        arrived = to_plane(*early[1:])
        sent_and_arrived = lax.optimization_barrier((*sent, *arrived))
        sent, arrived = sent_and_arrived[:3], sent_and_arrived[3:]
        for piece in sent:
            mine = mine + piece.astype(f32)
        early_sum = plane_sums(early[0], *arrived)
        early_low = early_sum.astype(bf16)
        for far in (1, 2, 3):
            pairs = [(far * UNITS + k, k) for k in range(UNITS)]
            pairs += [((last ^ far) * UNITS + UNITS - 1, size - 1)]
            early_sum = early_sum + lax.ppermute(early_low, "dp", pairs).astype(f32)
        unit_grad = jnp.where(z == 0, early_sum[:UNIT], mine)
        gain_grads = jnp.where(me == size - 1, early_sum[UNIT:], 0.0)
        square_sum = add_up((jnp.sum(unit_grad * unit_grad) + jnp.sum(gain_grads * gain_grads)).reshape(1, 1))[0, 0]
        after = lax.ppermute(unit_grad[:size], "dp", [(i + 1, i) for i in range(size - 1)])
        after = after + jnp.pad(gain_grads, ((0, size - GAIN_ROWS), (0, 0)))
        grad_shard = lax.dynamic_slice_in_dim(jnp.concatenate([unit_grad, after], axis=0), me, shard).reshape(-1)
    else:
        early = jnp.stack([keep_early, send_early], axis=1).reshape(UNITS, UNIT + GAIN_ROWS, LANES)
        late = jnp.stack([keep, send], axis=1).reshape(UNITS, 3, UNIT, LANES)
        pieces = [early[:, :UNIT].reshape(-1, LANES)] + [late[:, p].reshape(-1, LANES) for p in range(3)]
        grads = jnp.concatenate(pieces + [early[UNITS - 1, UNIT:]], axis=0).astype(f32)
        grads = jnp.pad(grads, ((0, size * shard - grads.shape[0]), (0, 0)))
        grad_shard = lax.psum_scatter(grads.reshape(-1), "dp", scatter_dimension=0, tiled=True)
        square_sum = lax.psum(jnp.sum(grad_shard * grad_shard), "dp")
    grad_norm = jnp.sqrt(square_sum)
    clipped = grad_shard * (clip_norm / jnp.maximum(grad_norm, clip_norm))
    new_one = decay_one * moment_one + (1.0 - decay_one) * clipped
    new_two = decay_two * moment_two + (1.0 - decay_two) * clipped * clipped
    corrected_one = new_one / (1.0 - decay_one**STEP)
    corrected_two = new_two / (1.0 - decay_two**STEP)
    new_master = master - learn_rate * (
        corrected_one / (jnp.sqrt(corrected_two) + adam_eps) + weight_decay * master
    )
    return (layer.transpose(0, 2, 1), igrad.transpose(0, 2, 1), grad_shard, grad_norm, new_master, new_one, new_two)


def solution(mesh):
    flat, cube = P("dp"), P("dp", None, None)
    return jax.shard_map(
        local,
        mesh=mesh,
        in_specs=(cube, P("dp", None), cube, flat, flat, flat),
        out_specs=(cube, cube, flat, P(), flat, flat, flat),
        check_vma=False,
    )
```

```python
import functools

import jax
import jax.numpy as jnp
from jax import lax
from jax.experimental import pallas as pl
from jax.experimental.pallas import tpu as pltpu
from jax.sharding import PartitionSpec as P

MODEL_WIDTH = 576
QUERY_HEADS = 9
KEY_VALUE_HEADS = 3
HEAD_SIZE = 64
FEEDFWD_UNITS = 1536
TILE = 128
STEP = 8
GROUP = QUERY_HEADS // KEY_VALUE_HEADS
HALF = HEAD_SIZE // 2
KV_WIDTH = KEY_VALUE_HEADS * HEAD_SIZE
QKV_WIDTH = MODEL_WIDTH + 2 * KV_WIDTH
CHUNK = 1536
LANES = 128
UNIT = MODEL_WIDTH * KV_WIDTH // LANES
GAIN_ROWS = 16
UNITS = 8
STRIDE = UNIT + GAIN_ROWS
FEEDFWD_TILES = FEEDFWD_UNITS // LANES

rms_eps = 1e-05
rope_base = 100000.0
learn_rate = 0.02
decay_one = 0.9
decay_two = 0.999
adam_eps = 1e-08
weight_decay = 0.1
clip_norm = 1.0
mask_fill = -1000000000.0

bf16 = jnp.bfloat16
f32 = jnp.float32


def mm(a, b):
    return jnp.dot(a, b, preferred_element_type=f32)


def inverse_rms(x):
    return lax.rsqrt(jnp.mean(x * x, axis=0, keepdims=True) + rms_eps)


def spread(gain, tokens):
    return jnp.concatenate([gain] * (tokens // LANES), axis=1)


def fold(x):
    return sum(x[:, t : t + LANES] for t in range(0, x.shape[1], LANES))


def norm_back(x, inverse, gain, grad):
    e = grad * gain
    return inverse * e - x * (inverse * inverse * inverse) * jnp.mean(e * x, axis=0, keepdims=True)


def fill_bias(bias, starts_row):
    rows = starts_row.shape[1]
    starts_col = jnp.broadcast_to(starts_row, (TILE, rows)).T
    key_at = lax.broadcasted_iota(jnp.int32, (rows, TILE), 0)
    for i in range(rows // TILE):
        width = (i + 1) * TILE
        query_at = lax.broadcasted_iota(jnp.int32, (rows, TILE), 1) + i * TILE
        allowed = (starts_col == starts_row[:, i * TILE : width]) & (key_at <= query_at)
        bias[:, i * TILE : width] = jnp.where(allowed, 0.0, mask_fill)


def half_turn(x):
    return pltpu.roll(x, HEAD_SIZE, 1)


def to_matrix(flat, base, out, pairs, tiles):
    half = tiles // 2
    low = lax.broadcasted_iota(jnp.int32, (pairs, LANES), 1) < HEAD_SIZE
    for t in range(half + 1):
        out[t, pl.ds(0, pairs, stride=2), :] = flat[pl.ds(base + t, pairs, stride=tiles), :]
    turned = half_turn(flat[pl.ds(base + half, pairs, stride=tiles), :])
    for t in range(half):
        following = half_turn(flat[pl.ds(base + half + t + 1, pairs, stride=tiles), :])
        out[t, pl.ds(1, pairs, stride=2), :] = jnp.where(low, turned, following)
        turned = following
    out[half, pl.ds(1, pairs, stride=2), :] = turned


def to_flat(matrix, flat, base, pairs, tiles):
    half = tiles // 2
    low = lax.broadcasted_iota(jnp.int32, (pairs, LANES), 1) < HEAD_SIZE
    for t in range(half):
        flat[pl.ds(base + t, pairs, stride=tiles), :] = matrix[t, pl.ds(0, pairs, stride=2), :]
    before = matrix[half, pl.ds(0, pairs, stride=2), :]
    for t in range(half + 1):
        turned = half_turn(matrix[t, pl.ds(1, pairs, stride=2), :])
        flat[pl.ds(base + half + t, pairs, stride=tiles), :] = jnp.where(low, before, turned)
        before = turned


def columns_of(matrix, rows, width):
    full = width // LANES
    return jnp.concatenate([matrix[t, :rows] for t in range(full)] + [matrix[full, :rows, :HEAD_SIZE]], axis=1)


def put_columns(matrix, value):
    rows, width = value.shape
    full = width // LANES
    for t in range(full):
        matrix[t, :rows] = value[:, t * LANES : (t + 1) * LANES]
    matrix[full, :rows, :HEAD_SIZE] = value[:, full * LANES :]


def head_rows(ref, g, columns):
    return jnp.concatenate(
        [ref[0, pl.ds((g * GROUP + h) * HEAD_SIZE, HEAD_SIZE), columns] for h in range(GROUP)], axis=1
    )


def attention_forward(
    pitch, live, own, tok, st_row, cos, sin, units,
    qk_t, kv, mix_t, hidden, lse, w, wo, gains,
    w_t, wo_t, v_t, bias, flat, square, gain
):
    b = pl.program_id(0)
    rows = tok.shape[2]

    @pl.when(b == 0)
    def _():
        for k in range(UNITS):
            flat[k * pitch : k * pitch + UNIT + 8] = units[k ^ own[0], 0 : UNIT + 8].astype(f32)
        pairs = MODEL_WIDTH // 2
        to_matrix(flat, 5 * UNIT, square, pairs, 9)
        value = columns_of(square, MODEL_WIDTH, MODEL_WIDTH)
        wo[...] = value.astype(bf16)
        wo_t[...] = value.T.astype(bf16)
        to_matrix(flat, 0, square, pairs, 9)
        value = columns_of(square, MODEL_WIDTH, MODEL_WIDTH)
        w[:, 0:MODEL_WIDTH] = value.astype(bf16)
        w_t[0:MODEL_WIDTH] = value.T.astype(bf16)
        for which in range(2):
            at = MODEL_WIDTH + which * KV_WIDTH
            to_matrix(flat, (3 + which) * UNIT, square, pairs, 3)
            value = columns_of(square, MODEL_WIDTH, KV_WIDTH)
            w[:, at : at + KV_WIDTH] = value.astype(bf16)
            w_t[at : at + KV_WIDTH] = value.T.astype(bf16)
        tail = units[(UNITS - 1) ^ own[0], UNIT:STRIDE].astype(f32)
        line = jnp.concatenate([tail[j + 1 : j + 2] for j in range(9)], axis=1)
        for which in range(2):
            one = line[:, which * MODEL_WIDTH : (which + 1) * MODEL_WIDTH]
            gains[which] = jnp.broadcast_to(one, (LANES, MODEL_WIDTH)).T
        gain[...] = gains[0]

    @pl.when(live[b] > 0)
    def _():
        x = tok[0].astype(f32)
        n1_t = (x * inverse_rms(x) * spread(gain[...], rows)).astype(bf16)
        c, s = cos[0], sin[0]
        for h in range(QUERY_HEADS + KEY_VALUE_HEADS):
            at = h * HEAD_SIZE
            u = mm(w_t[at : at + HEAD_SIZE], n1_t)
            u1, u2 = u[:HALF], u[HALF:]
            r = jnp.concatenate([u1 * c - u2 * s, u2 * c + u1 * s], axis=0)
            if h < QUERY_HEADS:
                r = r * HEAD_SIZE ** (-0.5)
            r = r.astype(bf16)
            qk_t[0, at : at + HEAD_SIZE] = r
            if h >= QUERY_HEADS:
                kv[0, h - QUERY_HEADS] = r.T
        for g in range(KEY_VALUE_HEADS):
            at = MODEL_WIDTH + KV_WIDTH + g * HEAD_SIZE
            v = mm(w_t[at : at + HEAD_SIZE], n1_t).astype(bf16)
            v_t[g] = v
            kv[0, KEY_VALUE_HEADS + g] = v.T
        fill_bias(bias, st_row[0])
        mix_t[...] = jnp.zeros_like(mix_t)

        for i in range(rows // TILE):

            @pl.when(i < live[b])
            def _():
                for g in range(KEY_VALUE_HEADS):
                    width = (i + 1) * TILE
                    cols = slice(i * TILE, width)
                    q_t = head_rows(qk_t, g, cols)
                    mask = bias[:width, cols]
                    scores = mm(kv[0, g, :width], q_t) + jnp.concatenate([mask] * GROUP, axis=1)
                    peak = jnp.max(scores, axis=0, keepdims=True)
                    e = jnp.exp(scores - peak)
                    total = jnp.sum(e, axis=0, keepdims=True)
                    prob = (e * (1.0 / total)).astype(bf16)
                    lse[0, g * (rows // TILE) + i] = peak + jnp.log(total)
                    out = mm(v_t[g, :, :width], prob).astype(bf16)
                    for h in range(GROUP):
                        mix_t[0, pl.ds((g * GROUP + h) * HEAD_SIZE, HEAD_SIZE), cols] = out[
                            :, h * TILE : (h + 1) * TILE
                        ]

        hidden[0] = tok[0].astype(f32) + mm(wo_t[...], mix_t[0])


def mlp(
    pitch, live, own, hidden, cot, st_row, all_rows, gains,
    layer, hgrad, keep, send, dgain,
    wg, wu, wd, wg_t, wu_t, wd_t, dwg_t, dwu_t, dwd, n2, n2_t, rl, rl_t, n2g, res, flat, slab, fetched, ready
):
    b = pl.program_id(0)
    rows = hidden.shape[2]

    @pl.when(b == 0)
    def _():
        def pieces(which):
            start = which * UNITS * UNIT
            return start // pitch, (start + UNITS * UNIT - 1) // pitch + 1

        def fetch(which):
            first, end = pieces(which)
            slot = which % 2
            return pltpu.make_async_copy(
                all_rows.at[first * STRIDE : end * STRIDE], fetched.at[slot, 0 : (end - first) * STRIDE], ready.at[slot]
            )

        def spell_out(which):
            fetch(which).wait()
            first, end = pieces(which)
            for k in range(end - first):
                flat[k * pitch : k * pitch + UNIT + 8] = fetched[which % 2, k * STRIDE : k * STRIDE + UNIT + 8].astype(f32)
            return which * UNITS * UNIT - first * pitch

        fetch(1).start()
        fetch(2).start()
        for which, straight, turned in ((1, wg, wg_t), (2, wu, wu_t)):
            base = spell_out(which)
            if which == 1:
                fetch(3).start()
            for j in range(FEEDFWD_TILES):
                at = slice(j * LANES, (j + 1) * LANES)
                part = flat[pl.ds(base + j, MODEL_WIDTH, stride=FEEDFWD_TILES), :]
                straight[:, at] = part.astype(bf16)
                turned[at] = part.T.astype(bf16)
        base = spell_out(3)
        for j in range(FEEDFWD_TILES):
            at = slice(j * LANES, (j + 1) * LANES)
            to_matrix(flat, base + j * MODEL_WIDTH, slab, LANES // 2, 9)
            value = columns_of(slab, LANES, MODEL_WIDTH)
            wd[at] = value.astype(bf16)
            wd_t[:, at] = value.T.astype(bf16)
        dwg_t[...] = jnp.zeros_like(dwg_t)
        dwu_t[...] = jnp.zeros_like(dwu_t)
        dwd[...] = jnp.zeros_like(dwd)
        dgain[...] = jnp.zeros_like(dgain)

    @pl.when(live[b] == 0)
    def _():
        layer[...] = jnp.zeros_like(layer)
        hgrad[...] = jnp.zeros_like(hgrad)

    @pl.when(live[b] > 0)
    def _():
        x = hidden[0]
        inverse = inverse_rms(x)
        alive = st_row[0] < rows
        normed = (x * inverse * spread(gains[1], rows)).astype(bf16)
        n2_t[...] = normed
        n2[...] = normed.T
        grad = jnp.where(alive, cot[0].astype(f32), 0.0).astype(bf16)
        rl_t[...] = grad
        rl[...] = grad.T
        res[...] = jnp.zeros_like(res)
        n2g[...] = jnp.zeros_like(n2g)

        def chunk(k, carry):
            at = pl.ds(pl.multiple_of(k * CHUNK, CHUNK), CHUNK)
            pre = mm(wg_t[at, :], n2_t[...])
            up = mm(wu_t[at, :], n2_t[...])
            ag = mm(wd[at, :], rl_t[...])
            s = jax.nn.sigmoid(pre)
            silu = pre * s
            act = (silu * up).astype(bf16)
            gl = (ag * up * s * (1.0 + pre * (1.0 - s))).astype(bf16)
            ul = (ag * silu).astype(bf16)
            res[...] += mm(wd_t[:, at], act)
            n2g[...] += mm(wg[:, at], gl) + mm(wu[:, at], ul)
            dwd[at, :] += mm(act, rl[...])
            dwg_t[at, :] += mm(gl, n2[...])
            dwu_t[at, :] += mm(ul, n2[...])
            return carry

        lax.fori_loop(0, FEEDFWD_UNITS // CHUNK, chunk, 0)
        x = hidden[0]
        layer[0] = jnp.where(alive, x + res[...], 0.0).astype(bf16)
        ng = n2g[...]
        dgain[...] += fold(ng * x * inverse)
        hgrad[0] = rl_t[...].astype(f32) + norm_back(x, inverse, spread(gains[1], rows), ng)

    @pl.when(b == pl.num_programs(0) - 1)
    def _():
        for p in range(3):
            for j in range(FEEDFWD_TILES):
                at = slice(j * LANES, (j + 1) * LANES)
                if p < 2:
                    flat[pl.ds(j, MODEL_WIDTH, stride=FEEDFWD_TILES), :] = (dwg_t, dwu_t)[p][at].T
                else:
                    put_columns(slab, dwd[at])
                    to_flat(slab, flat, j * MODEL_WIDTH, LANES // 2, 9)
            for k in range(UNITS):
                place = k ^ own[0]

                @pl.when(place % 2 == 0)
                def _():
                    keep[place // 2, p] = flat[k * UNIT : (k + 1) * UNIT].astype(bf16)

                @pl.when(place % 2 == 1)
                def _():
                    send[place // 2, p] = flat[k * UNIT : (k + 1) * UNIT].astype(bf16)


def attention_backward(
    lo, final, live, own, hgrad, tok, qk_t, kv, mix_t, lse, st_row, cos, sin, w, wo, gains, *refs
):
    if lo:
        dw_in, dwo_in, dgain_in, _ = refs[:4]
        refs = refs[4:]
    if final:
        dgain_two, igrad, keep, send = refs[:4]
        bias, mg_t, mg, q, dq, dk, dv, low_t, flat, square, dw_t, dwo, dgain = refs[4:]
    else:
        igrad, dw_t, dwo, dgain = refs[:4]
        bias, mg_t, mg, q, dq, dk, dv, low_t = refs[4:]
    b = pl.program_id(0) + lo
    rows = tok.shape[2]
    tiles = rows // TILE
    scale = HEAD_SIZE ** (-0.5)

    @pl.when(b == lo)
    def _():
        if lo:
            dw_t[...] = dw_in[...]
            dwo[...] = dwo_in[...]
            dgain[...] = dgain_in[...]
        else:
            dw_t[...] = jnp.zeros_like(dw_t)
            dwo[...] = jnp.zeros_like(dwo)
            dgain[...] = jnp.zeros_like(dgain)

    @pl.when(live[b] == 0)
    def _():
        igrad[...] = jnp.zeros_like(igrad)

    @pl.when(live[b] > 0)
    def _():
        hl_t = hgrad[0].astype(bf16)
        dwo[...] += mm(mix_t[0], hl_t.T)
        mg_t[0] = mm(wo[...], hl_t).astype(bf16)
        for h in range(QUERY_HEADS):
            at = slice(h * HEAD_SIZE, (h + 1) * HEAD_SIZE)
            mg[h] = mg_t[0, at].T
            q[h] = qk_t[0, at].T
        fill_bias(bias, st_row[0])
        dq[...] = jnp.zeros_like(dq)
        dk[...] = jnp.zeros_like(dk)
        dv[...] = jnp.zeros_like(dv)

        for i in range(tiles):

            @pl.when(i < live[b])
            def _():
                for g in range(KEY_VALUE_HEADS):
                    width = (i + 1) * TILE
                    cols = slice(i * TILE, width)
                    q_t = head_rows(qk_t, g, cols)
                    mask = bias[:width, cols]
                    scores = mm(kv[0, g, :width], q_t) + jnp.concatenate([mask] * GROUP, axis=1)
                    prob = jnp.exp(scores - lse[0, g * tiles + i])
                    dp = mm(kv[0, KEY_VALUE_HEADS + g, :width], head_rows(mg_t, g, cols))
                    delta = jnp.sum(prob * dp, axis=0, keepdims=True)
                    ds = (prob * (dp - delta)).astype(bf16)
                    low = prob.astype(bf16)
                    k_t = qk_t[0, pl.ds(MODEL_WIDTH + g * HEAD_SIZE, HEAD_SIZE), :width]
                    dq_i = mm(k_t, ds) * scale
                    for h in range(GROUP):
                        dq[pl.ds((g * GROUP + h) * HEAD_SIZE, HEAD_SIZE), cols] = dq_i[
                            :, h * TILE : (h + 1) * TILE
                        ]
                    q_i = jnp.concatenate([q[g * GROUP + h, cols] for h in range(GROUP)], axis=0)
                    mg_i = jnp.concatenate([mg[g * GROUP + h, cols] for h in range(GROUP)], axis=0)
                    dk[g, :width] += mm(ds, q_i)
                    dv[g, :width] += mm(low, mg_i)

        c, s = cos[0], sin[0]
        for h in range(QUERY_HEADS + KEY_VALUE_HEADS):
            at = h * HEAD_SIZE
            u = dq[at : at + HEAD_SIZE] if h < QUERY_HEADS else dk[h - QUERY_HEADS].T
            u1, u2 = u[:HALF], u[HALF:]
            r = jnp.concatenate([u1 * c + u2 * s, u2 * c - u1 * s], axis=0)
            low_t[at : at + HEAD_SIZE] = r.astype(bf16)
        for g in range(KEY_VALUE_HEADS):
            at = MODEL_WIDTH + KV_WIDTH + g * HEAD_SIZE
            low_t[at : at + HEAD_SIZE] = dv[g].T.astype(bf16)
        x = tok[0].astype(f32)
        inverse = inverse_rms(x)
        gain = spread(gains[0], rows)
        dw_t[...] += mm(low_t[...], (x * inverse * gain).astype(bf16).T)
        ng = mm(w[...], low_t[...])
        dgain[...] += fold(ng * x * inverse)
        igrad[0] = hgrad[0] + norm_back(x, inverse, gain, ng)

    if not final:
        return

    @pl.when(pl.program_id(0) == pl.num_programs(0) - 1)
    def _():
        pairs = MODEL_WIDTH // 2
        put_columns(square, dw_t[0:MODEL_WIDTH].T)
        to_flat(square, flat, 0, pairs, 9)
        for which in range(2):
            at = MODEL_WIDTH + which * KV_WIDTH
            put_columns(square, dw_t[at : at + KV_WIDTH].T)
            to_flat(square, flat, (3 + which) * UNIT, pairs, 3)
        put_columns(square, dwo[...])
        to_flat(square, flat, 5 * UNIT, pairs, 9)
        lines = [jnp.sum(d[...].T, axis=0, keepdims=True) for d in (dgain, dgain_two)]
        line = jnp.concatenate(lines, axis=1)
        tail = [line[:, j * LANES : (j + 1) * LANES] for j in range(9)]
        tail = jnp.concatenate(tail + [jnp.zeros((GAIN_ROWS - 9, LANES), f32)], axis=0).astype(bf16)
        for k in range(UNITS):
            place = k ^ own[0]
            ours = tail if k == UNITS - 1 else jnp.zeros_like(tail)

            @pl.when(place % 2 == 0)
            def _():
                keep[place // 2, 0:UNIT] = flat[k * UNIT : (k + 1) * UNIT].astype(bf16)
                keep[place // 2, UNIT : UNIT + GAIN_ROWS] = ours

            @pl.when(place % 2 == 1)
            def _():
                send[place // 2, 0:UNIT] = flat[k * UNIT : (k + 1) * UNIT].astype(bf16)
                send[place // 2, UNIT : UNIT + GAIN_ROWS] = ours


def by_buffer(*shape, lo=0):
    zeros = (0,) * len(shape)
    return pl.BlockSpec((1,) + shape, lambda b, live, own: (b + lo if lo else b,) + zeros)


def whole(*shape):
    zeros = (0,) * len(shape)
    return pl.BlockSpec(shape, lambda b, live, own: zeros, pipeline_mode=pl.Buffered(1))


def call(kernel, name, buffers, in_specs, out_specs, outs, scratch, flops, moved, args, aliases=None):
    return pl.pallas_call(
        kernel,
        name=name,
        out_shape=[jax.ShapeDtypeStruct(shape, dtype) for shape, dtype in outs],
        grid_spec=pltpu.PrefetchScalarGridSpec(
            num_scalar_prefetch=2,
            grid=(buffers,),
            in_specs=in_specs,
            out_specs=out_specs,
            scratch_shapes=[pltpu.VMEM(*kind) if isinstance(kind, tuple) else kind for kind in scratch],
        ),
        input_output_aliases=aliases or {},
        compiler_params=pltpu.CompilerParams(
            dimension_semantics=("arbitrary",), vmem_limit_bytes=60 * 1024 * 1024
        ),
        cost_estimate=pl.CostEstimate(flops=flops, bytes_accessed=moved, transcendentals=0),
    )(*args)


def run_attention_forward(pitch, live, own, tokens, st_row, cos, sin, units):
    n, d, t = tokens.shape
    lines = KEY_VALUE_HEADS * (t // TILE)
    return call(
        functools.partial(attention_forward, pitch), "attention_forward", n,
        [by_buffer(d, t), by_buffer(1, t), by_buffer(HALF, t), by_buffer(HALF, t), whole(UNITS, UNIT + GAIN_ROWS, LANES)],
        [by_buffer(d + KV_WIDTH, t), by_buffer(2 * KEY_VALUE_HEADS, t, HEAD_SIZE), by_buffer(d, t), by_buffer(d, t),
         by_buffer(lines, 1, GROUP * TILE), whole(d, QKV_WIDTH), whole(d, d), whole(2, d, LANES)],
        [((n, d + KV_WIDTH, t), bf16), ((n, 2 * KEY_VALUE_HEADS, t, HEAD_SIZE), bf16), ((n, d, t), bf16), ((n, d, t), f32),
         ((n, lines, 1, GROUP * TILE), f32), ((d, QKV_WIDTH), bf16), ((d, d), bf16), ((2, d, LANES), f32)],
        [((QKV_WIDTH, d), bf16), ((d, d), bf16), ((KEY_VALUE_HEADS, HEAD_SIZE, t), bf16), ((t, t), f32),
         ((UNITS * STRIDE, LANES), f32), ((5, d, LANES), f32), ((d, LANES), f32)],
        8 * 10**9, 20 * 10**6,
        (live, own, tokens, st_row, cos, sin, units),
    )


def run_mlp(pitch, live, own, hidden, cot, st_row, rows, gains):
    n, d, t = hidden.shape
    f = FEEDFWD_UNITS
    half = (UNITS // 2, 3, UNIT, LANES)
    return call(
        functools.partial(mlp, pitch), "mlp", n,
        [by_buffer(d, t), by_buffer(d, t), by_buffer(1, t), pl.BlockSpec(memory_space=pl.ANY), whole(2, d, LANES)],
        [by_buffer(d, t), by_buffer(d, t), whole(*half), whole(*half), whole(d, LANES)],
        [((n, d, t), bf16), ((n, d, t), f32), (half, bf16), (half, bf16), ((d, LANES), f32)],
        [((d, f), bf16), ((d, f), bf16), ((f, d), bf16), ((f, d), bf16), ((f, d), bf16), ((d, f), bf16),
         ((f, d), f32), ((f, d), f32), ((f, d), f32), ((t, d), bf16), ((d, t), bf16), ((t, d), bf16), ((d, t), bf16),
         ((d, t), f32), ((d, t), f32), (((UNITS + 1) * STRIDE, LANES), f32), ((5, LANES, LANES), f32),
         ((2, (UNITS + 1) * STRIDE, LANES), bf16), pltpu.SemaphoreType.DMA((2,))],
        33 * 10**9, 30 * 10**6,
        (live, own, hidden, cot, st_row, rows, gains),
    )


def run_attention_backward(lo, hi, live, own, hgrad, tokens, qk_t, kv, mix_t, lse, st_row, cos, sin, w, wo, gains, so_far=(), dgain_two=None):
    n, d, t = tokens.shape
    lines = KEY_VALUE_HEADS * (t // TILE)
    final = dgain_two is not None
    sums = [((QKV_WIDTH, d), f32), ((d, d), f32), ((d, LANES), f32)]
    of = functools.partial(by_buffer, lo=lo)
    in_specs = [of(d, t), of(d, t), of(d + KV_WIDTH, t), of(2 * KEY_VALUE_HEADS, t, HEAD_SIZE), of(d, t), of(lines, 1, GROUP * TILE),
                of(1, t), of(HALF, t), of(HALF, t), whole(d, QKV_WIDTH), whole(d, d), whole(2, d, LANES)]
    args = [live, own, hgrad, tokens, qk_t, kv, mix_t, lse, st_row, cos, sin, w, wo, gains]
    out_specs, outs = [of(d, t)], [((n, d, t), f32)]
    scratch = [((t, t), f32), ((1, d, t), bf16), ((QUERY_HEADS, t, HEAD_SIZE), bf16), ((QUERY_HEADS, t, HEAD_SIZE), bf16),
               ((d, t), f32), ((KEY_VALUE_HEADS, t, HEAD_SIZE), f32), ((KEY_VALUE_HEADS, t, HEAD_SIZE), f32), ((QKV_WIDTH, t), bf16)]
    aliases = {}
    if so_far:
        in_specs += [whole(*shape) for shape, _ in sums] + [pl.BlockSpec(memory_space=pl.ANY)]
        args += list(so_far)
        aliases = {len(args) - 1: 0}
    if final:
        half = (UNITS // 2, UNIT + GAIN_ROWS, LANES)
        in_specs += [whole(d, LANES)]
        args += [dgain_two]
        out_specs += [whole(*half)] * 2
        outs += [(half, bf16)] * 2
        scratch += [((UNITS * UNIT, LANES), f32), ((5, d, LANES), f32)] + sums
    else:
        out_specs += [whole(*shape) for shape, _ in sums]
        outs += sums
    return call(
        functools.partial(attention_backward, lo, final), "attention_backward", hi - lo,
        in_specs, out_specs, outs, scratch, 8 * 10**9, 20 * 10**6, args, aliases,
    )


def swap(x, bits):
    size = lax.axis_size("dp")
    return lax.ppermute(x, "dp", [(i, i ^ bits) for i in range(size)])


def plane(i):
    return i // UNITS


def relative_order(rows):
    size = lax.axis_size("dp")
    last = size // UNITS - 1
    first = rows
    for far in (3, 2, 1):
        pairs = [(k, far * UNITS + k) for k in range(UNITS)] + [(size - 1, (last - far) * UNITS + UNITS - 1)]
        first = first + lax.ppermute(rows, "dp", pairs)
    even = [first, swap(first, 2), swap(first, 4), swap(first, 6)]
    units = []
    for piece in even:
        units += [piece, swap(piece, 1)]
    return jnp.stack(units)


def core_sums(keep, other):
    sums = [keep[j].astype(f32) + other[j].astype(f32) for j in range(UNITS // 2)]
    return [sums[0]] + [s.astype(bf16) for s in sums[1:]]


def to_plane(two, four, six):
    return [swap(two, 2), swap(four, 4), swap(six, 6)]


def plane_sums(own, two, four, six):
    return (own + two.astype(f32)) + (four.astype(f32) + six.astype(f32))


def add_up(value):
    bits = 1
    while bits < lax.axis_size("dp"):
        value = value + swap(value, bits)
        bits *= 2
    return value


def local(tokens, doc_starts, cotangent, master, moment_one, moment_two):
    size = lax.axis_size("dp")
    me = lax.axis_index("dp")
    z = plane(me)
    buffers, rows = tokens.shape[:2]
    shard = master.shape[0] // LANES
    total = 4 * UNITS * UNIT
    by_units = size == 4 * UNITS and shard == UNIT + 1
    own_rows = master.reshape(shard, LANES)
    if by_units:
        own = me % UNITS
        pitch = shard
        gain_at = total - (size - 1) * shard
        low_rows = own_rows.astype(bf16)
        padded = jnp.pad(low_rows, ((0, STRIDE - shard), (0, 0)))
        all_rows = lax.all_gather(padded, "dp", axis=0, tiled=True)
        gain_rows = jnp.pad(low_rows[gain_at : gain_at + 9], ((shard, STRIDE - shard - 9), (0, 0)))
        nothing = jnp.zeros_like(padded)
        units = relative_order(jnp.where(z == 0, padded, jnp.where(me == size - 1, gain_rows, nothing)))
    else:
        own = jnp.zeros_like(me)
        pitch = UNIT
        all_rows = lax.all_gather(own_rows.astype(bf16), "dp", axis=0, tiled=True)
        gain_rows = jnp.pad(all_rows[None, total : total + 9], ((UNITS - 1, 0), (1, GAIN_ROWS - 10), (0, 0)))
        all_rows = jnp.pad(all_rows[:total].reshape(-1, UNIT, LANES), ((0, 0), (0, GAIN_ROWS), (0, 0)))
        units = all_rows[:UNITS] + jnp.pad(gain_rows, ((0, 0), (UNIT, 0), (0, 0)))
        all_rows = all_rows.reshape(-1, LANES)
    own = own.astype(jnp.int32).reshape(1)

    is_live = doc_starts < rows
    live = jnp.sum(is_live.astype(jnp.int32), axis=1) // TILE
    positions = jnp.where(is_live, jnp.arange(rows) - doc_starts, 0).astype(f32)
    frequency = rope_base ** (-(jnp.arange(HALF, dtype=f32) * 2.0 / HEAD_SIZE))
    angles = frequency[None, :, None] * positions[:, None, :]
    cos, sin = jnp.cos(angles), jnp.sin(angles)
    st_row = doc_starts.astype(f32)[:, None, :]
    tok_t, cot_t = tokens.transpose(0, 2, 1), cotangent.transpose(0, 2, 1)

    qk_t, kv, mix_t, hidden, lse, w, wo, gains = run_attention_forward(pitch, live, own, tok_t, st_row, cos, sin, units)
    layer, hgrad, keep, send, dgain_two = run_mlp(pitch, live, own, hidden, cot_t, st_row, all_rows, gains)
    shared = (live, own, hgrad, tok_t, qk_t, kv, mix_t, lse, st_row, cos, sin, w, wo, gains)
    igrad, dw_t, dwo, dgain = run_attention_backward(0, 1, *shared)
    if by_units:
        late = core_sums(keep, swap(send, 1))
        dgain, *late = lax.optimization_barrier((dgain, *late))
        arrived = to_plane(*late[1:])
    igrad, dw_t, dwo, dgain = run_attention_backward(1, buffers - 1, *shared, so_far=(dw_t, dwo, dgain, igrad))
    if by_units:
        dgain, *arrived = lax.optimization_barrier((dgain, *arrived))
        late_sum = plane_sums(late[0], *arrived)
        mine = lax.dynamic_index_in_dim(late_sum, jnp.maximum(z - 1, 0), 0, keepdims=False)
        sent = [
            lax.dynamic_index_in_dim(late_sum, jnp.maximum((z ^ far) - 1, 0), 0, keepdims=False).astype(bf16)
            for far in (1, 2, 3)
        ]
        dgain, *sent = lax.optimization_barrier((dgain, *sent))
        for far in (1, 2, 3):
            pairs = [(i, i ^ (far * UNITS)) for i in range(size) if plane(i ^ (far * UNITS)) > 0]
            sent[far - 1] = lax.ppermute(sent[far - 1], "dp", pairs)
    igrad, keep_early, send_early = run_attention_backward(
        buffers - 1, buffers, *shared, so_far=(dw_t, dwo, dgain, igrad), dgain_two=dgain_two
    )
    if by_units:
        last = size // UNITS - 1
        keep_early, send_early, *sent = lax.optimization_barrier((keep_early, send_early, *sent))
        early = core_sums(keep_early, swap(send_early, 1))
        arrived = to_plane(*early[1:])
        for piece in sent:
            mine = mine + piece.astype(f32)
        early_sum = plane_sums(early[0], *arrived)
        early_low = early_sum.astype(bf16)
        for far in (1, 2, 3):
            pairs = [(far * UNITS + k, k) for k in range(UNITS)]
            pairs += [((last ^ far) * UNITS + UNITS - 1, size - 1)]
            early_sum = early_sum + lax.ppermute(early_low, "dp", pairs).astype(f32)
        unit_grad = jnp.where(z == 0, early_sum[:UNIT], mine)
        gain_grads = jnp.where(me == size - 1, early_sum[UNIT:], 0.0)
        square_sum = add_up((jnp.sum(unit_grad * unit_grad) + jnp.sum(gain_grads * gain_grads)).reshape(1, 1))[0, 0]
        after = lax.ppermute(unit_grad[:size], "dp", [(i + 1, i) for i in range(size - 1)])
        after = after + jnp.pad(gain_grads, ((0, size - GAIN_ROWS), (0, 0)))
        grad_shard = lax.dynamic_slice_in_dim(jnp.concatenate([unit_grad, after], axis=0), me, shard).reshape(-1)
    else:
        early = jnp.stack([keep_early, send_early], axis=1).reshape(UNITS, UNIT + GAIN_ROWS, LANES)
        late = jnp.stack([keep, send], axis=1).reshape(UNITS, 3, UNIT, LANES)
        pieces = [early[:, :UNIT].reshape(-1, LANES)] + [late[:, p].reshape(-1, LANES) for p in range(3)]
        grads = jnp.concatenate(pieces + [early[UNITS - 1, UNIT:]], axis=0).astype(f32)
        grads = jnp.pad(grads, ((0, size * shard - grads.shape[0]), (0, 0)))
        grad_shard = lax.psum_scatter(grads.reshape(-1), "dp", scatter_dimension=0, tiled=True)
        square_sum = lax.psum(jnp.sum(grad_shard * grad_shard), "dp")
    grad_norm = jnp.sqrt(square_sum)
    clipped = grad_shard * (clip_norm / jnp.maximum(grad_norm, clip_norm))
    new_one = decay_one * moment_one + (1.0 - decay_one) * clipped
    new_two = decay_two * moment_two + (1.0 - decay_two) * clipped * clipped
    corrected_one = new_one / (1.0 - decay_one**STEP)
    corrected_two = new_two / (1.0 - decay_two**STEP)
    new_master = master - learn_rate * (
        corrected_one / (jnp.sqrt(corrected_two) + adam_eps) + weight_decay * master
    )
    return (layer.transpose(0, 2, 1), igrad.transpose(0, 2, 1), grad_shard, grad_norm, new_master, new_one, new_two)


def solution(mesh):
    flat, cube = P("dp"), P("dp", None, None)
    return jax.shard_map(
        local,
        mesh=mesh,
        in_specs=(cube, P("dp", None), cube, flat, flat, flat),
        out_specs=(cube, cube, flat, P(), flat, flat, flat),
        check_vma=False,
    )
```

```python
import functools

import jax
import jax.numpy as jnp
from jax import lax
from jax.experimental import pallas as pl
from jax.experimental.pallas import tpu as pltpu
from jax.sharding import PartitionSpec as P

MODEL_WIDTH = 576
QUERY_HEADS = 9
KEY_VALUE_HEADS = 3
HEAD_SIZE = 64
FEEDFWD_UNITS = 1536
TILE = 128
STEP = 8
GROUP = QUERY_HEADS // KEY_VALUE_HEADS
HALF = HEAD_SIZE // 2
KV_WIDTH = KEY_VALUE_HEADS * HEAD_SIZE
QKV_WIDTH = MODEL_WIDTH + 2 * KV_WIDTH
CHUNK = 1536
LANES = 128
UNIT = MODEL_WIDTH * KV_WIDTH // LANES
GAIN_ROWS = 16
UNITS = 8
FEEDFWD_TILES = FEEDFWD_UNITS // LANES

rms_eps = 1e-05
rope_base = 100000.0
learn_rate = 0.02
decay_one = 0.9
decay_two = 0.999
adam_eps = 1e-08
weight_decay = 0.1
clip_norm = 1.0
mask_fill = -1000000000.0

bf16 = jnp.bfloat16
f32 = jnp.float32


def mm(a, b):
    return jnp.dot(a, b, preferred_element_type=f32)


def inverse_rms(x):
    return lax.rsqrt(jnp.mean(x * x, axis=0, keepdims=True) + rms_eps)


def spread(gain, tokens):
    return jnp.concatenate([gain] * (tokens // LANES), axis=1)


def fold(x):
    return sum(x[:, t : t + LANES] for t in range(0, x.shape[1], LANES))


def norm_back(x, inverse, gain, grad):
    e = grad * gain
    return inverse * e - x * (inverse * inverse * inverse) * jnp.mean(e * x, axis=0, keepdims=True)


def fill_bias(bias, starts_row):
    rows = starts_row.shape[1]
    starts_col = jnp.broadcast_to(starts_row, (TILE, rows)).T
    key_at = lax.broadcasted_iota(jnp.int32, (rows, TILE), 0)
    for i in range(rows // TILE):
        width = (i + 1) * TILE
        query_at = lax.broadcasted_iota(jnp.int32, (rows, TILE), 1) + i * TILE
        allowed = (starts_col == starts_row[:, i * TILE : width]) & (key_at <= query_at)
        bias[:, i * TILE : width] = jnp.where(allowed, 0.0, mask_fill)


def half_turn(x):
    return pltpu.roll(x, HEAD_SIZE, 1)


def to_matrix(flat, base, out, pairs, tiles):
    half = tiles // 2
    low = lax.broadcasted_iota(jnp.int32, (pairs, LANES), 1) < HEAD_SIZE
    for t in range(half + 1):
        out[t, pl.ds(0, pairs, stride=2), :] = flat[pl.ds(base + t, pairs, stride=tiles), :]
    turned = half_turn(flat[pl.ds(base + half, pairs, stride=tiles), :])
    for t in range(half):
        following = half_turn(flat[pl.ds(base + half + t + 1, pairs, stride=tiles), :])
        out[t, pl.ds(1, pairs, stride=2), :] = jnp.where(low, turned, following)
        turned = following
    out[half, pl.ds(1, pairs, stride=2), :] = turned


def to_flat(matrix, flat, base, pairs, tiles):
    half = tiles // 2
    low = lax.broadcasted_iota(jnp.int32, (pairs, LANES), 1) < HEAD_SIZE
    for t in range(half):
        flat[pl.ds(base + t, pairs, stride=tiles), :] = matrix[t, pl.ds(0, pairs, stride=2), :]
    before = matrix[half, pl.ds(0, pairs, stride=2), :]
    for t in range(half + 1):
        turned = half_turn(matrix[t, pl.ds(1, pairs, stride=2), :])
        flat[pl.ds(base + half + t, pairs, stride=tiles), :] = jnp.where(low, before, turned)
        before = turned


def columns_of(matrix, rows, width):
    full = width // LANES
    return jnp.concatenate([matrix[t, :rows] for t in range(full)] + [matrix[full, :rows, :HEAD_SIZE]], axis=1)


def put_columns(matrix, value):
    rows, width = value.shape
    full = width // LANES
    for t in range(full):
        matrix[t, :rows] = value[:, t * LANES : (t + 1) * LANES]
    matrix[full, :rows, :HEAD_SIZE] = value[:, full * LANES :]


def head_rows(ref, g, columns):
    return jnp.concatenate(
        [ref[0, pl.ds((g * GROUP + h) * HEAD_SIZE, HEAD_SIZE), columns] for h in range(GROUP)], axis=1
    )


def attention_forward(
    live, own, tok, st_row, cos, sin, units,
    qk_t, kv, mix_t, hidden, lse, w, wo, gains,
    w_t, wo_t, v_t, bias, flat, square, gain
):
    b = pl.program_id(0)
    rows = tok.shape[2]

    @pl.when(b == 0)
    def _():
        for k in range(UNITS):
            flat[k * UNIT : (k + 1) * UNIT] = units[k ^ own[0], 0:UNIT].astype(f32)
        pairs = MODEL_WIDTH // 2
        to_matrix(flat, 5 * UNIT, square, pairs, 9)
        value = columns_of(square, MODEL_WIDTH, MODEL_WIDTH)
        wo[...] = value.astype(bf16)
        wo_t[...] = value.T.astype(bf16)
        to_matrix(flat, 0, square, pairs, 9)
        value = columns_of(square, MODEL_WIDTH, MODEL_WIDTH)
        w[:, 0:MODEL_WIDTH] = value.astype(bf16)
        w_t[0:MODEL_WIDTH] = value.T.astype(bf16)
        for which in range(2):
            at = MODEL_WIDTH + which * KV_WIDTH
            to_matrix(flat, (3 + which) * UNIT, square, pairs, 3)
            value = columns_of(square, MODEL_WIDTH, KV_WIDTH)
            w[:, at : at + KV_WIDTH] = value.astype(bf16)
            w_t[at : at + KV_WIDTH] = value.T.astype(bf16)
        tail = units[(UNITS - 1) ^ own[0], UNIT : UNIT + GAIN_ROWS].astype(f32)
        line = jnp.concatenate([tail[j : j + 1] for j in range(9)], axis=1)
        for which in range(2):
            one = line[:, which * MODEL_WIDTH : (which + 1) * MODEL_WIDTH]
            gains[which] = jnp.broadcast_to(one, (LANES, MODEL_WIDTH)).T
        gain[...] = gains[0]

    @pl.when(live[b] > 0)
    def _():
        x = tok[0].astype(f32)
        n1_t = (x * inverse_rms(x) * spread(gain[...], rows)).astype(bf16)
        c, s = cos[0], sin[0]
        for h in range(QUERY_HEADS + KEY_VALUE_HEADS):
            at = h * HEAD_SIZE
            u = mm(w_t[at : at + HEAD_SIZE], n1_t)
            u1, u2 = u[:HALF], u[HALF:]
            r = jnp.concatenate([u1 * c - u2 * s, u2 * c + u1 * s], axis=0)
            if h < QUERY_HEADS:
                r = r * HEAD_SIZE ** (-0.5)
            r = r.astype(bf16)
            qk_t[0, at : at + HEAD_SIZE] = r
            if h >= QUERY_HEADS:
                kv[0, h - QUERY_HEADS] = r.T
        for g in range(KEY_VALUE_HEADS):
            at = MODEL_WIDTH + KV_WIDTH + g * HEAD_SIZE
            v = mm(w_t[at : at + HEAD_SIZE], n1_t).astype(bf16)
            v_t[g] = v
            kv[0, KEY_VALUE_HEADS + g] = v.T
        fill_bias(bias, st_row[0])
        mix_t[...] = jnp.zeros_like(mix_t)

        for i in range(rows // TILE):

            @pl.when(i < live[b])
            def _():
                for g in range(KEY_VALUE_HEADS):
                    width = (i + 1) * TILE
                    cols = slice(i * TILE, width)
                    q_t = head_rows(qk_t, g, cols)
                    mask = bias[:width, cols]
                    scores = mm(kv[0, g, :width], q_t) + jnp.concatenate([mask] * GROUP, axis=1)
                    peak = jnp.max(scores, axis=0, keepdims=True)
                    e = jnp.exp(scores - peak)
                    total = jnp.sum(e, axis=0, keepdims=True)
                    prob = (e * (1.0 / total)).astype(bf16)
                    lse[0, g * (rows // TILE) + i] = peak + jnp.log(total)
                    out = mm(v_t[g, :, :width], prob).astype(bf16)
                    for h in range(GROUP):
                        mix_t[0, pl.ds((g * GROUP + h) * HEAD_SIZE, HEAD_SIZE), cols] = out[
                            :, h * TILE : (h + 1) * TILE
                        ]

        hidden[0] = tok[0].astype(f32) + mm(wo_t[...], mix_t[0])


def mlp(
    live, own, hidden, cot, st_row, gains, *refs
):
    units, refs = refs[:UNITS], refs[UNITS:]
    layer, hgrad, keep, send, dgain, *refs = refs
    wg, wu, wd, wg_t, wu_t, wd_t, dwg_t, dwu_t, dwd, n2, n2_t, rl, rl_t, n2g, res, flat, slab = refs
    b = pl.program_id(0)
    rows = hidden.shape[2]

    @pl.when(b == 0)
    def _():
        def spell_out(which):
            half = UNIT // 2
            for m in range(UNITS):

                def place(part, carry):
                    to = pl.multiple_of((own[0] ^ m) * UNIT + part * half, 8)
                    at = pl.multiple_of(part * half, 16)
                    flat[pl.ds(to, half)] = units[m][which, pl.ds(at, half)].astype(f32)
                    return carry

                lax.fori_loop(0, 2, place, 0)

        for which, straight, turned in ((0, wg, wg_t), (1, wu, wu_t)):
            spell_out(which)
            for j in range(FEEDFWD_TILES):
                at = slice(j * LANES, (j + 1) * LANES)
                part = flat[pl.ds(j, MODEL_WIDTH, stride=FEEDFWD_TILES), :]
                straight[:, at] = part.astype(bf16)
                turned[at] = part.T.astype(bf16)
        spell_out(2)
        for j in range(FEEDFWD_TILES):
            at = slice(j * LANES, (j + 1) * LANES)
            to_matrix(flat, j * MODEL_WIDTH, slab, LANES // 2, 9)
            value = columns_of(slab, LANES, MODEL_WIDTH)
            wd[at] = value.astype(bf16)
            wd_t[:, at] = value.T.astype(bf16)
        dwg_t[...] = jnp.zeros_like(dwg_t)
        dwu_t[...] = jnp.zeros_like(dwu_t)
        dwd[...] = jnp.zeros_like(dwd)
        dgain[...] = jnp.zeros_like(dgain)

    @pl.when(live[b] == 0)
    def _():
        layer[...] = jnp.zeros_like(layer)
        hgrad[...] = jnp.zeros_like(hgrad)

    @pl.when(live[b] > 0)
    def _():
        x = hidden[0]
        inverse = inverse_rms(x)
        alive = st_row[0] < rows
        normed = (x * inverse * spread(gains[1], rows)).astype(bf16)
        n2_t[...] = normed
        n2[...] = normed.T
        grad = jnp.where(alive, cot[0].astype(f32), 0.0).astype(bf16)
        rl_t[...] = grad
        rl[...] = grad.T
        res[...] = jnp.zeros_like(res)
        n2g[...] = jnp.zeros_like(n2g)

        def chunk(k, carry):
            at = pl.ds(pl.multiple_of(k * CHUNK, CHUNK), CHUNK)
            pre = mm(wg_t[at, :], n2_t[...])
            up = mm(wu_t[at, :], n2_t[...])
            ag = mm(wd[at, :], rl_t[...])
            s = jax.nn.sigmoid(pre)
            silu = pre * s
            act = (silu * up).astype(bf16)
            gl = (ag * up * s * (1.0 + pre * (1.0 - s))).astype(bf16)
            ul = (ag * silu).astype(bf16)
            res[...] += mm(wd_t[:, at], act)
            n2g[...] += mm(wg[:, at], gl) + mm(wu[:, at], ul)
            dwd[at, :] += mm(act, rl[...])
            dwg_t[at, :] += mm(gl, n2[...])
            dwu_t[at, :] += mm(ul, n2[...])
            return carry

        lax.fori_loop(0, FEEDFWD_UNITS // CHUNK, chunk, 0)
        x = hidden[0]
        layer[0] = jnp.where(alive, x + res[...], 0.0).astype(bf16)
        ng = n2g[...]
        dgain[...] += fold(ng * x * inverse)
        hgrad[0] = rl_t[...].astype(f32) + norm_back(x, inverse, spread(gains[1], rows), ng)

    @pl.when(b == pl.num_programs(0) - 1)
    def _():
        for p in range(3):
            for j in range(FEEDFWD_TILES):
                at = slice(j * LANES, (j + 1) * LANES)
                if p < 2:
                    flat[pl.ds(j, MODEL_WIDTH, stride=FEEDFWD_TILES), :] = (dwg_t, dwu_t)[p][at].T
                else:
                    put_columns(slab, dwd[at])
                    to_flat(slab, flat, j * MODEL_WIDTH, LANES // 2, 9)
            for k in range(UNITS):
                place = k ^ own[0]

                @pl.when(place % 2 == 0)
                def _():
                    keep[place // 2, p] = flat[k * UNIT : (k + 1) * UNIT].astype(bf16)

                @pl.when(place % 2 == 1)
                def _():
                    send[place // 2, p] = flat[k * UNIT : (k + 1) * UNIT].astype(bf16)


def attention_backward(
    lo, final, live, own, hgrad, tok, qk_t, kv, mix_t, lse, st_row, cos, sin, w, wo, gains, *refs
):
    if final:
        dgain_two, dw_in, dwo_in, dgain_in, _, igrad, keep, send = refs[:8]
        bias, mg_t, mg, q, dq, dk, dv, low_t, flat, square, dw_t, dwo, dgain = refs[8:]
    else:
        igrad, dw_t, dwo, dgain = refs[:4]
        bias, mg_t, mg, q, dq, dk, dv, low_t = refs[4:]
    b = pl.program_id(0) + lo
    rows = tok.shape[2]
    tiles = rows // TILE
    scale = HEAD_SIZE ** (-0.5)

    @pl.when(b == lo)
    def _():
        if final:
            dw_t[...] = dw_in[...]
            dwo[...] = dwo_in[...]
            dgain[...] = dgain_in[...]
        else:
            dw_t[...] = jnp.zeros_like(dw_t)
            dwo[...] = jnp.zeros_like(dwo)
            dgain[...] = jnp.zeros_like(dgain)

    @pl.when(live[b] == 0)
    def _():
        igrad[...] = jnp.zeros_like(igrad)

    @pl.when(live[b] > 0)
    def _():
        hl_t = hgrad[0].astype(bf16)
        dwo[...] += mm(mix_t[0], hl_t.T)
        mg_t[0] = mm(wo[...], hl_t).astype(bf16)
        for h in range(QUERY_HEADS):
            at = slice(h * HEAD_SIZE, (h + 1) * HEAD_SIZE)
            mg[h] = mg_t[0, at].T
            q[h] = qk_t[0, at].T
        fill_bias(bias, st_row[0])
        dq[...] = jnp.zeros_like(dq)
        dk[...] = jnp.zeros_like(dk)
        dv[...] = jnp.zeros_like(dv)

        for i in range(tiles):

            @pl.when(i < live[b])
            def _():
                for g in range(KEY_VALUE_HEADS):
                    width = (i + 1) * TILE
                    cols = slice(i * TILE, width)
                    q_t = head_rows(qk_t, g, cols)
                    mask = bias[:width, cols]
                    scores = mm(kv[0, g, :width], q_t) + jnp.concatenate([mask] * GROUP, axis=1)
                    prob = jnp.exp(scores - lse[0, g * tiles + i])
                    dp = mm(kv[0, KEY_VALUE_HEADS + g, :width], head_rows(mg_t, g, cols))
                    delta = jnp.sum(prob * dp, axis=0, keepdims=True)
                    ds = (prob * (dp - delta)).astype(bf16)
                    low = prob.astype(bf16)
                    k_t = qk_t[0, pl.ds(MODEL_WIDTH + g * HEAD_SIZE, HEAD_SIZE), :width]
                    dq_i = mm(k_t, ds) * scale
                    for h in range(GROUP):
                        dq[pl.ds((g * GROUP + h) * HEAD_SIZE, HEAD_SIZE), cols] = dq_i[
                            :, h * TILE : (h + 1) * TILE
                        ]
                    q_i = jnp.concatenate([q[g * GROUP + h, cols] for h in range(GROUP)], axis=0)
                    mg_i = jnp.concatenate([mg[g * GROUP + h, cols] for h in range(GROUP)], axis=0)
                    dk[g, :width] += mm(ds, q_i)
                    dv[g, :width] += mm(low, mg_i)

        c, s = cos[0], sin[0]
        for h in range(QUERY_HEADS + KEY_VALUE_HEADS):
            at = h * HEAD_SIZE
            u = dq[at : at + HEAD_SIZE] if h < QUERY_HEADS else dk[h - QUERY_HEADS].T
            u1, u2 = u[:HALF], u[HALF:]
            r = jnp.concatenate([u1 * c + u2 * s, u2 * c - u1 * s], axis=0)
            low_t[at : at + HEAD_SIZE] = r.astype(bf16)
        for g in range(KEY_VALUE_HEADS):
            at = MODEL_WIDTH + KV_WIDTH + g * HEAD_SIZE
            low_t[at : at + HEAD_SIZE] = dv[g].T.astype(bf16)
        x = tok[0].astype(f32)
        inverse = inverse_rms(x)
        gain = spread(gains[0], rows)
        dw_t[...] += mm(low_t[...], (x * inverse * gain).astype(bf16).T)
        ng = mm(w[...], low_t[...])
        dgain[...] += fold(ng * x * inverse)
        igrad[0] = hgrad[0] + norm_back(x, inverse, gain, ng)

    if not final:
        return

    @pl.when(pl.program_id(0) == pl.num_programs(0) - 1)
    def _():
        pairs = MODEL_WIDTH // 2
        put_columns(square, dw_t[0:MODEL_WIDTH].T)
        to_flat(square, flat, 0, pairs, 9)
        for which in range(2):
            at = MODEL_WIDTH + which * KV_WIDTH
            put_columns(square, dw_t[at : at + KV_WIDTH].T)
            to_flat(square, flat, (3 + which) * UNIT, pairs, 3)
        put_columns(square, dwo[...])
        to_flat(square, flat, 5 * UNIT, pairs, 9)
        lines = [jnp.sum(d[...].T, axis=0, keepdims=True) for d in (dgain, dgain_two)]
        line = jnp.concatenate(lines, axis=1)
        tail = [line[:, j * LANES : (j + 1) * LANES] for j in range(9)]
        tail = jnp.concatenate(tail + [jnp.zeros((GAIN_ROWS - 9, LANES), f32)], axis=0).astype(bf16)
        for k in range(UNITS):
            place = k ^ own[0]
            ours = tail if k == UNITS - 1 else jnp.zeros_like(tail)

            @pl.when(place % 2 == 0)
            def _():
                keep[place // 2, 0:UNIT] = flat[k * UNIT : (k + 1) * UNIT].astype(bf16)
                keep[place // 2, UNIT : UNIT + GAIN_ROWS] = ours

            @pl.when(place % 2 == 1)
            def _():
                send[place // 2, 0:UNIT] = flat[k * UNIT : (k + 1) * UNIT].astype(bf16)
                send[place // 2, UNIT : UNIT + GAIN_ROWS] = ours


def by_buffer(*shape, lo=0):
    zeros = (0,) * len(shape)
    return pl.BlockSpec((1,) + shape, lambda b, live, own: (b + lo if lo else b,) + zeros)


def whole(*shape):
    zeros = (0,) * len(shape)
    return pl.BlockSpec(shape, lambda b, live, own: zeros, pipeline_mode=pl.Buffered(1))


def call(kernel, name, buffers, in_specs, out_specs, outs, scratch, flops, moved, args, aliases=None):
    return pl.pallas_call(
        kernel,
        name=name,
        out_shape=[jax.ShapeDtypeStruct(shape, dtype) for shape, dtype in outs],
        grid_spec=pltpu.PrefetchScalarGridSpec(
            num_scalar_prefetch=2,
            grid=(buffers,),
            in_specs=in_specs,
            out_specs=out_specs,
            scratch_shapes=[pltpu.VMEM(shape, dtype) for shape, dtype in scratch],
        ),
        input_output_aliases=aliases or {},
        compiler_params=pltpu.CompilerParams(
            dimension_semantics=("arbitrary",), vmem_limit_bytes=60 * 1024 * 1024
        ),
        cost_estimate=pl.CostEstimate(flops=flops, bytes_accessed=moved, transcendentals=0),
    )(*args)


def run_attention_forward(live, own, tokens, st_row, cos, sin, units):
    n, d, t = tokens.shape
    lines = KEY_VALUE_HEADS * (t // TILE)
    return call(
        attention_forward, "attention_forward", n,
        [by_buffer(d, t), by_buffer(1, t), by_buffer(HALF, t), by_buffer(HALF, t), whole(UNITS, UNIT + GAIN_ROWS, LANES)],
        [by_buffer(d + KV_WIDTH, t), by_buffer(2 * KEY_VALUE_HEADS, t, HEAD_SIZE), by_buffer(d, t), by_buffer(d, t),
         by_buffer(lines, 1, GROUP * TILE), whole(d, QKV_WIDTH), whole(d, d), whole(2, d, LANES)],
        [((n, d + KV_WIDTH, t), bf16), ((n, 2 * KEY_VALUE_HEADS, t, HEAD_SIZE), bf16), ((n, d, t), bf16), ((n, d, t), f32),
         ((n, lines, 1, GROUP * TILE), f32), ((d, QKV_WIDTH), bf16), ((d, d), bf16), ((2, d, LANES), f32)],
        [((QKV_WIDTH, d), bf16), ((d, d), bf16), ((KEY_VALUE_HEADS, HEAD_SIZE, t), bf16), ((t, t), f32),
         ((UNITS * UNIT, LANES), f32), ((5, d, LANES), f32), ((d, LANES), f32)],
        8 * 10**9, 20 * 10**6,
        (live, own, tokens, st_row, cos, sin, units),
    )


def run_mlp(live, own, hidden, cot, st_row, gains, units):
    n, d, t = hidden.shape
    f = FEEDFWD_UNITS
    half = (UNITS // 2, 3, UNIT, LANES)
    return call(
        mlp, "mlp", n,
        [by_buffer(d, t), by_buffer(d, t), by_buffer(1, t), whole(2, d, LANES)] + [whole(3, UNIT, LANES)] * UNITS,
        [by_buffer(d, t), by_buffer(d, t), whole(*half), whole(*half), whole(d, LANES)],
        [((n, d, t), bf16), ((n, d, t), f32), (half, bf16), (half, bf16), ((d, LANES), f32)],
        [((d, f), bf16), ((d, f), bf16), ((f, d), bf16), ((f, d), bf16), ((f, d), bf16), ((d, f), bf16),
         ((f, d), f32), ((f, d), f32), ((f, d), f32), ((t, d), bf16), ((d, t), bf16), ((t, d), bf16), ((d, t), bf16),
         ((d, t), f32), ((d, t), f32), ((UNITS * UNIT, LANES), f32), ((5, LANES, LANES), f32)],
        33 * 10**9, 30 * 10**6,
        (live, own, hidden, cot, st_row, gains, *units),
    )


def run_attention_backward(lo, hi, live, own, hgrad, tokens, qk_t, kv, mix_t, lse, st_row, cos, sin, w, wo, gains, so_far=None):
    n, d, t = tokens.shape
    lines = KEY_VALUE_HEADS * (t // TILE)
    final = so_far is not None
    sums = [((QKV_WIDTH, d), f32), ((d, d), f32), ((d, LANES), f32)]
    of = functools.partial(by_buffer, lo=lo)
    in_specs = [of(d, t), of(d, t), of(d + KV_WIDTH, t), of(2 * KEY_VALUE_HEADS, t, HEAD_SIZE), of(d, t), of(lines, 1, GROUP * TILE),
                of(1, t), of(HALF, t), of(HALF, t), whole(d, QKV_WIDTH), whole(d, d), whole(2, d, LANES)]
    args = [live, own, hgrad, tokens, qk_t, kv, mix_t, lse, st_row, cos, sin, w, wo, gains]
    out_specs, outs = [of(d, t)], [((n, d, t), f32)]
    scratch = [((t, t), f32), ((1, d, t), bf16), ((QUERY_HEADS, t, HEAD_SIZE), bf16), ((QUERY_HEADS, t, HEAD_SIZE), bf16),
               ((d, t), f32), ((KEY_VALUE_HEADS, t, HEAD_SIZE), f32), ((KEY_VALUE_HEADS, t, HEAD_SIZE), f32), ((QKV_WIDTH, t), bf16)]
    aliases = {}
    if final:
        half = (UNITS // 2, UNIT + GAIN_ROWS, LANES)
        in_specs += [whole(d, LANES)] + [whole(*shape) for shape, _ in sums] + [pl.BlockSpec(memory_space=pl.ANY)]
        args += list(so_far)
        aliases = {len(args) - 1: 0}
        out_specs += [whole(*half)] * 2
        outs += [(half, bf16)] * 2
        scratch += [((UNITS * UNIT, LANES), f32), ((5, d, LANES), f32)] + sums
    else:
        out_specs += [whole(*shape) for shape, _ in sums]
        outs += sums
    return call(
        functools.partial(attention_backward, lo, final), "attention_backward", hi - lo,
        in_specs, out_specs, outs, scratch, 8 * 10**9, 20 * 10**6, args, aliases,
    )


def swap(x, bits):
    size = lax.axis_size("dp")
    return lax.ppermute(x, "dp", [(i, i ^ bits) for i in range(size)])


def plane(i):
    return i // UNITS


def pick(pieces, index):
    chosen = pieces[0]
    for i, piece in enumerate(pieces[1:], 1):
        chosen = jnp.where(index == i, piece, chosen)
    return chosen


def with_partners(even):
    return [piece for mine in even for piece in (mine, swap(mine, 1))]


def core_sums(keep, send):
    other = swap(send, 1)
    sums = [keep[j].astype(f32) + other[j].astype(f32) for j in range(UNITS // 2)]
    return [sums[0]] + [s.astype(bf16) for s in sums[1:]]


def to_plane(two, four, six):
    return [swap(two, 2), swap(four, 4), swap(six, 6)]


def plane_sums(own, two, four, six):
    return (own + two.astype(f32)) + (four.astype(f32) + six.astype(f32))


def add_up(value):
    bits = 1
    while bits < lax.axis_size("dp"):
        value = value + swap(value, bits)
        bits *= 2
    return value


def local(tokens, doc_starts, cotangent, master, moment_one, moment_two):
    size = lax.axis_size("dp")
    me = lax.axis_index("dp")
    z = plane(me)
    buffers, rows = tokens.shape[:2]
    shard = master.shape[0] // LANES
    total = 4 * UNITS * UNIT
    by_units = size == 4 * UNITS and shard == UNIT + 1
    own_rows = master.reshape(shard, LANES)
    if by_units:
        own = me % UNITS
        before = lax.ppermute(own_rows[shard - size :], "dp", [(i, i + 1) for i in range(size - 1)])
        unit = lax.dynamic_slice_in_dim(jnp.concatenate([before, own_rows], axis=0), size - me, UNIT).astype(bf16)
        gain_at = total - (size - 1) * shard
        gain_rows = own_rows[gain_at : gain_at + GAIN_ROWS].astype(bf16)
        rows_here = jnp.concatenate([unit, jnp.where(me == size - 1, gain_rows, jnp.zeros_like(gain_rows))], axis=0)
        planes = [rows_here] + [swap(rows_here, far * UNITS) for far in (1, 2, 3)]
        head = jnp.concatenate([pick([r[:UNIT] for r in planes], z), pick([r[UNIT:] for r in planes], z ^ 3)], axis=0)
        rest = jnp.stack([pick([r[:UNIT] for r in planes], z ^ p) for p in (1, 2, 3)])
        around = [swap(head, bits) for bits in (2, 4, 6)]
        rest, *around = lax.optimization_barrier((rest, *around))
        units = jnp.stack(with_partners([head, *around]))
        rest_around = [swap(rest, bits) for bits in (2, 4, 6)]
    else:
        own = jnp.zeros_like(me)
        all_rows = lax.all_gather(own_rows.astype(bf16), "dp", axis=0, tiled=True)
        units = all_rows[: UNITS * UNIT].reshape(UNITS, UNIT, LANES)
        gain_rows = jnp.pad(all_rows[None, total : total + GAIN_ROWS], ((UNITS - 1, 0), (0, 0), (0, 0)))
        units = jnp.concatenate([units, gain_rows], axis=1)
        late_units = all_rows[UNITS * UNIT : total].reshape(3, UNITS, UNIT, LANES)
        late_units = [late_units[:, k] for k in range(UNITS)]
    own = own.astype(jnp.int32).reshape(1)

    is_live = doc_starts < rows
    live = jnp.sum(is_live.astype(jnp.int32), axis=1) // TILE
    positions = jnp.where(is_live, jnp.arange(rows) - doc_starts, 0).astype(f32)
    frequency = rope_base ** (-(jnp.arange(HALF, dtype=f32) * 2.0 / HEAD_SIZE))
    angles = frequency[None, :, None] * positions[:, None, :]
    cos, sin = jnp.cos(angles), jnp.sin(angles)
    st_row = doc_starts.astype(f32)[:, None, :]
    tok_t, cot_t = tokens.transpose(0, 2, 1), cotangent.transpose(0, 2, 1)

    qk_t, kv, mix_t, hidden, lse, w, wo, gains = run_attention_forward(live, own, tok_t, st_row, cos, sin, units)
    if by_units:
        hidden, *rest_around = lax.optimization_barrier((hidden, *rest_around))
        late_units = with_partners([rest, *rest_around])
    layer, hgrad, keep, send, dgain_two = run_mlp(live, own, hidden, cot_t, st_row, gains, late_units)
    shared = (live, own, hgrad, tok_t, qk_t, kv, mix_t, lse, st_row, cos, sin, w, wo, gains)
    igrad, dw_t, dwo, dgain = run_attention_backward(0, buffers // 2, *shared)
    if by_units:
        late = core_sums(keep, send)
        dgain, *late = lax.optimization_barrier((dgain, *late))
        arrived = to_plane(*late[1:])
    igrad, keep_early, send_early = run_attention_backward(
        buffers // 2, buffers, *shared, so_far=(dgain_two, dw_t, dwo, dgain, igrad)
    )
    if by_units:
        last = size // UNITS - 1
        keep_early, send_early, *arrived = lax.optimization_barrier((keep_early, send_early, *arrived))
        late_sum = plane_sums(late[0], *arrived)
        mine = lax.dynamic_index_in_dim(late_sum, jnp.maximum(z - 1, 0), 0, keepdims=False)
        sent = [
            lax.dynamic_index_in_dim(late_sum, jnp.maximum((z ^ far) - 1, 0), 0, keepdims=False).astype(bf16)
            for far in (1, 2, 3)
        ]
        send_early, *sent = lax.optimization_barrier((send_early, *sent))
        for far in (1, 2, 3):
            pairs = [(i, i ^ (far * UNITS)) for i in range(size) if plane(i ^ (far * UNITS)) > 0]
            sent[far - 1] = lax.ppermute(sent[far - 1], "dp", pairs)
        early = core_sums(keep_early, send_early)
        arrived = to_plane(*early[1:])
        sent_and_arrived = lax.optimization_barrier((*sent, *arrived))
        sent, arrived = sent_and_arrived[:3], sent_and_arrived[3:]
        for piece in sent:
            mine = mine + piece.astype(f32)
        early_sum = plane_sums(early[0], *arrived)
        early_low = early_sum.astype(bf16)
        for far in (1, 2, 3):
            pairs = [(far * UNITS + k, k) for k in range(UNITS)]
            pairs += [((last ^ far) * UNITS + UNITS - 1, size - 1)]
            early_sum = early_sum + lax.ppermute(early_low, "dp", pairs).astype(f32)
        unit_grad = jnp.where(z == 0, early_sum[:UNIT], mine)
        gain_grads = jnp.where(me == size - 1, early_sum[UNIT:], 0.0)
        square_sum = add_up((jnp.sum(unit_grad * unit_grad) + jnp.sum(gain_grads * gain_grads)).reshape(1, 1))[0, 0]
        after = lax.ppermute(unit_grad[:size], "dp", [(i + 1, i) for i in range(size - 1)])
        after = after + jnp.pad(gain_grads, ((0, size - GAIN_ROWS), (0, 0)))
        grad_shard = lax.dynamic_slice_in_dim(jnp.concatenate([unit_grad, after], axis=0), me, shard).reshape(-1)
    else:
        early = jnp.stack([keep_early, send_early], axis=1).reshape(UNITS, UNIT + GAIN_ROWS, LANES)
        late = jnp.stack([keep, send], axis=1).reshape(UNITS, 3, UNIT, LANES)
        pieces = [early[:, :UNIT].reshape(-1, LANES)] + [late[:, p].reshape(-1, LANES) for p in range(3)]
        grads = jnp.concatenate(pieces + [early[UNITS - 1, UNIT:]], axis=0).astype(f32)
        grads = jnp.pad(grads, ((0, size * shard - grads.shape[0]), (0, 0)))
        grad_shard = lax.psum_scatter(grads.reshape(-1), "dp", scatter_dimension=0, tiled=True)
        square_sum = lax.psum(jnp.sum(grad_shard * grad_shard), "dp")
    grad_norm = jnp.sqrt(square_sum)
    clipped = grad_shard * (clip_norm / jnp.maximum(grad_norm, clip_norm))
    new_one = decay_one * moment_one + (1.0 - decay_one) * clipped
    new_two = decay_two * moment_two + (1.0 - decay_two) * clipped * clipped
    corrected_one = new_one / (1.0 - decay_one**STEP)
    corrected_two = new_two / (1.0 - decay_two**STEP)
    new_master = master - learn_rate * (
        corrected_one / (jnp.sqrt(corrected_two) + adam_eps) + weight_decay * master
    )
    return (layer.transpose(0, 2, 1), igrad.transpose(0, 2, 1), grad_shard, grad_norm, new_master, new_one, new_two)


def solution(mesh):
    flat, cube = P("dp"), P("dp", None, None)
    return jax.shard_map(
        local,
        mesh=mesh,
        in_specs=(cube, P("dp", None), cube, flat, flat, flat),
        out_specs=(cube, cube, flat, P(), flat, flat, flat),
        check_vma=False,
    )
```

```python
import functools

import jax
import jax.numpy as jnp
from jax import lax
from jax.experimental import pallas as pl
from jax.experimental.pallas import tpu as pltpu
from jax.sharding import PartitionSpec as P

MODEL_WIDTH = 576
QUERY_HEADS = 9
KEY_VALUE_HEADS = 3
HEAD_SIZE = 64
FEEDFWD_UNITS = 1536
TILE = 128
STEP = 8
GROUP = QUERY_HEADS // KEY_VALUE_HEADS
HALF = HEAD_SIZE // 2
KV_WIDTH = KEY_VALUE_HEADS * HEAD_SIZE
QKV_WIDTH = MODEL_WIDTH + 2 * KV_WIDTH
CHUNK = 1536
LANES = 128
UNIT = MODEL_WIDTH * KV_WIDTH // LANES
GAIN_ROWS = 16
UNITS = 8
FEEDFWD_TILES = FEEDFWD_UNITS // LANES

rms_eps = 1e-05
rope_base = 100000.0
learn_rate = 0.02
decay_one = 0.9
decay_two = 0.999
adam_eps = 1e-08
weight_decay = 0.1
clip_norm = 1.0
mask_fill = -1000000000.0

bf16 = jnp.bfloat16
f32 = jnp.float32


def mm(a, b):
    return jnp.dot(a, b, preferred_element_type=f32)


def inverse_rms(x):
    return lax.rsqrt(jnp.mean(x * x, axis=0, keepdims=True) + rms_eps)


def spread(gain, tokens):
    return jnp.concatenate([gain] * (tokens // LANES), axis=1)


def fold(x):
    return sum(x[:, t : t + LANES] for t in range(0, x.shape[1], LANES))


def norm_back(x, inverse, gain, grad):
    e = grad * gain
    return inverse * e - x * (inverse * inverse * inverse) * jnp.mean(e * x, axis=0, keepdims=True)


def fill_bias(bias, starts_row):
    rows = starts_row.shape[1]
    starts_col = jnp.broadcast_to(starts_row, (TILE, rows)).T
    key_at = lax.broadcasted_iota(jnp.int32, (rows, TILE), 0)
    for i in range(rows // TILE):
        width = (i + 1) * TILE
        query_at = lax.broadcasted_iota(jnp.int32, (rows, TILE), 1) + i * TILE
        allowed = (starts_col == starts_row[:, i * TILE : width]) & (key_at <= query_at)
        bias[:, i * TILE : width] = jnp.where(allowed, 0.0, mask_fill)


def half_turn(x):
    return pltpu.roll(x, HEAD_SIZE, 1)


def to_matrix(flat, base, out, pairs, tiles):
    half = tiles // 2
    low = lax.broadcasted_iota(jnp.int32, (pairs, LANES), 1) < HEAD_SIZE
    for t in range(half + 1):
        out[t, pl.ds(0, pairs, stride=2), :] = flat[pl.ds(base + t, pairs, stride=tiles), :]
    turned = half_turn(flat[pl.ds(base + half, pairs, stride=tiles), :])
    for t in range(half):
        following = half_turn(flat[pl.ds(base + half + t + 1, pairs, stride=tiles), :])
        out[t, pl.ds(1, pairs, stride=2), :] = jnp.where(low, turned, following)
        turned = following
    out[half, pl.ds(1, pairs, stride=2), :] = turned


def to_flat(matrix, flat, base, pairs, tiles):
    half = tiles // 2
    low = lax.broadcasted_iota(jnp.int32, (pairs, LANES), 1) < HEAD_SIZE
    for t in range(half):
        flat[pl.ds(base + t, pairs, stride=tiles), :] = matrix[t, pl.ds(0, pairs, stride=2), :]
    before = matrix[half, pl.ds(0, pairs, stride=2), :]
    for t in range(half + 1):
        turned = half_turn(matrix[t, pl.ds(1, pairs, stride=2), :])
        flat[pl.ds(base + half + t, pairs, stride=tiles), :] = jnp.where(low, before, turned)
        before = turned


def columns_of(matrix, rows, width):
    full = width // LANES
    return jnp.concatenate([matrix[t, :rows] for t in range(full)] + [matrix[full, :rows, :HEAD_SIZE]], axis=1)


def put_columns(matrix, value):
    rows, width = value.shape
    full = width // LANES
    for t in range(full):
        matrix[t, :rows] = value[:, t * LANES : (t + 1) * LANES]
    matrix[full, :rows, :HEAD_SIZE] = value[:, full * LANES :]


def head_rows(ref, g, columns):
    return jnp.concatenate(
        [ref[0, pl.ds((g * GROUP + h) * HEAD_SIZE, HEAD_SIZE), columns] for h in range(GROUP)], axis=1
    )


def attention_forward(
    live, own, tok, st_row, cos, sin, units,
    qk_t, kv, mix_t, hidden, lse, w, wo, gains,
    w_t, wo_t, v_t, bias, flat, square, gain
):
    b = pl.program_id(0)
    rows = tok.shape[2]

    @pl.when(b == 0)
    def _():
        for k in range(UNITS):
            flat[k * UNIT : (k + 1) * UNIT] = units[k ^ own[0], 0:UNIT].astype(f32)
        pairs = MODEL_WIDTH // 2
        to_matrix(flat, 5 * UNIT, square, pairs, 9)
        value = columns_of(square, MODEL_WIDTH, MODEL_WIDTH)
        wo[...] = value.astype(bf16)
        wo_t[...] = value.T.astype(bf16)
        to_matrix(flat, 0, square, pairs, 9)
        value = columns_of(square, MODEL_WIDTH, MODEL_WIDTH)
        w[:, 0:MODEL_WIDTH] = value.astype(bf16)
        w_t[0:MODEL_WIDTH] = value.T.astype(bf16)
        for which in range(2):
            at = MODEL_WIDTH + which * KV_WIDTH
            to_matrix(flat, (3 + which) * UNIT, square, pairs, 3)
            value = columns_of(square, MODEL_WIDTH, KV_WIDTH)
            w[:, at : at + KV_WIDTH] = value.astype(bf16)
            w_t[at : at + KV_WIDTH] = value.T.astype(bf16)
        tail = units[(UNITS - 1) ^ own[0], UNIT : UNIT + GAIN_ROWS].astype(f32)
        line = jnp.concatenate([tail[j : j + 1] for j in range(9)], axis=1)
        for which in range(2):
            one = line[:, which * MODEL_WIDTH : (which + 1) * MODEL_WIDTH]
            gains[which] = jnp.broadcast_to(one, (LANES, MODEL_WIDTH)).T
        gain[...] = gains[0]

    @pl.when(live[b] > 0)
    def _():
        x = tok[0].astype(f32)
        n1_t = (x * inverse_rms(x) * spread(gain[...], rows)).astype(bf16)
        c, s = cos[0], sin[0]
        for h in range(QUERY_HEADS + KEY_VALUE_HEADS):
            at = h * HEAD_SIZE
            u = mm(w_t[at : at + HEAD_SIZE], n1_t)
            u1, u2 = u[:HALF], u[HALF:]
            r = jnp.concatenate([u1 * c - u2 * s, u2 * c + u1 * s], axis=0)
            if h < QUERY_HEADS:
                r = r * HEAD_SIZE ** (-0.5)
            r = r.astype(bf16)
            qk_t[0, at : at + HEAD_SIZE] = r
            if h >= QUERY_HEADS:
                kv[0, h - QUERY_HEADS] = r.T
        for g in range(KEY_VALUE_HEADS):
            at = MODEL_WIDTH + KV_WIDTH + g * HEAD_SIZE
            v = mm(w_t[at : at + HEAD_SIZE], n1_t).astype(bf16)
            v_t[g] = v
            kv[0, KEY_VALUE_HEADS + g] = v.T
        fill_bias(bias, st_row[0])
        mix_t[...] = jnp.zeros_like(mix_t)

        for i in range(rows // TILE):

            @pl.when(i < live[b])
            def _():
                for g in range(KEY_VALUE_HEADS):
                    width = (i + 1) * TILE
                    cols = slice(i * TILE, width)
                    q_t = head_rows(qk_t, g, cols)
                    mask = bias[:width, cols]
                    scores = mm(kv[0, g, :width], q_t) + jnp.concatenate([mask] * GROUP, axis=1)
                    peak = jnp.max(scores, axis=0, keepdims=True)
                    e = jnp.exp(scores - peak)
                    total = jnp.sum(e, axis=0, keepdims=True)
                    prob = (e * (1.0 / total)).astype(bf16)
                    lse[0, g * (rows // TILE) + i] = peak + jnp.log(total)
                    out = mm(v_t[g, :, :width], prob).astype(bf16)
                    for h in range(GROUP):
                        mix_t[0, pl.ds((g * GROUP + h) * HEAD_SIZE, HEAD_SIZE), cols] = out[
                            :, h * TILE : (h + 1) * TILE
                        ]

        hidden[0] = tok[0].astype(f32) + mm(wo_t[...], mix_t[0])


def mlp(
    live, own, hidden, cot, st_row, gains, *refs
):
    units, refs = refs[:UNITS], refs[UNITS:]
    layer, hgrad, keep, send, dgain, *refs = refs
    wg, wu, wd, wg_t, wu_t, wd_t, dwg_t, dwu_t, dwd, n2, n2_t, rl, rl_t, n2g, res, flat, slab = refs
    b = pl.program_id(0)
    rows = hidden.shape[2]

    @pl.when(b == 0)
    def _():
        def spell_out(which):
            half = UNIT // 2
            for m in range(UNITS):

                def place(part, carry):
                    to = pl.multiple_of((own[0] ^ m) * UNIT + part * half, 8)
                    at = pl.multiple_of(part * half, 16)
                    flat[pl.ds(to, half)] = units[m][which, pl.ds(at, half)].astype(f32)
                    return carry

                lax.fori_loop(0, 2, place, 0)

        for which, straight, turned in ((0, wg, wg_t), (1, wu, wu_t)):
            spell_out(which)
            for j in range(FEEDFWD_TILES):
                at = slice(j * LANES, (j + 1) * LANES)
                part = flat[pl.ds(j, MODEL_WIDTH, stride=FEEDFWD_TILES), :]
                straight[:, at] = part.astype(bf16)
                turned[at] = part.T.astype(bf16)
        spell_out(2)
        for j in range(FEEDFWD_TILES):
            at = slice(j * LANES, (j + 1) * LANES)
            to_matrix(flat, j * MODEL_WIDTH, slab, LANES // 2, 9)
            value = columns_of(slab, LANES, MODEL_WIDTH)
            wd[at] = value.astype(bf16)
            wd_t[:, at] = value.T.astype(bf16)
        dwg_t[...] = jnp.zeros_like(dwg_t)
        dwu_t[...] = jnp.zeros_like(dwu_t)
        dwd[...] = jnp.zeros_like(dwd)
        dgain[...] = jnp.zeros_like(dgain)

    @pl.when(live[b] == 0)
    def _():
        layer[...] = jnp.zeros_like(layer)
        hgrad[...] = jnp.zeros_like(hgrad)

    @pl.when(live[b] > 0)
    def _():
        x = hidden[0]
        inverse = inverse_rms(x)
        alive = st_row[0] < rows
        normed = (x * inverse * spread(gains[1], rows)).astype(bf16)
        n2_t[...] = normed
        n2[...] = normed.T
        grad = jnp.where(alive, cot[0].astype(f32), 0.0).astype(bf16)
        rl_t[...] = grad
        rl[...] = grad.T
        res[...] = jnp.zeros_like(res)
        n2g[...] = jnp.zeros_like(n2g)

        def chunk(k, carry):
            at = pl.ds(pl.multiple_of(k * CHUNK, CHUNK), CHUNK)
            pre = mm(wg_t[at, :], n2_t[...])
            up = mm(wu_t[at, :], n2_t[...])
            ag = mm(wd[at, :], rl_t[...])
            s = jax.nn.sigmoid(pre)
            silu = pre * s
            act = (silu * up).astype(bf16)
            gl = (ag * up * s * (1.0 + pre * (1.0 - s))).astype(bf16)
            ul = (ag * silu).astype(bf16)
            res[...] += mm(wd_t[:, at], act)
            n2g[...] += mm(wg[:, at], gl) + mm(wu[:, at], ul)
            dwd[at, :] += mm(act, rl[...])
            dwg_t[at, :] += mm(gl, n2[...])
            dwu_t[at, :] += mm(ul, n2[...])
            return carry

        lax.fori_loop(0, FEEDFWD_UNITS // CHUNK, chunk, 0)
        x = hidden[0]
        layer[0] = jnp.where(alive, x + res[...], 0.0).astype(bf16)
        ng = n2g[...]
        dgain[...] += fold(ng * x * inverse)
        hgrad[0] = rl_t[...].astype(f32) + norm_back(x, inverse, spread(gains[1], rows), ng)

    @pl.when(b == pl.num_programs(0) - 1)
    def _():
        for p in range(3):
            for j in range(FEEDFWD_TILES):
                at = slice(j * LANES, (j + 1) * LANES)
                if p < 2:
                    flat[pl.ds(j, MODEL_WIDTH, stride=FEEDFWD_TILES), :] = (dwg_t, dwu_t)[p][at].T
                else:
                    put_columns(slab, dwd[at])
                    to_flat(slab, flat, j * MODEL_WIDTH, LANES // 2, 9)
            for k in range(UNITS):
                place = k ^ own[0]

                @pl.when(place % 2 == 0)
                def _():
                    keep[place // 2, p] = flat[k * UNIT : (k + 1) * UNIT].astype(bf16)

                @pl.when(place % 2 == 1)
                def _():
                    send[place // 2, p] = flat[k * UNIT : (k + 1) * UNIT].astype(bf16)


def attention_backward(
    lo, final, live, own, hgrad, tok, qk_t, kv, mix_t, lse, st_row, cos, sin, w, wo, gains, *refs
):
    if final:
        dgain_two, dw_in, dwo_in, dgain_in, _, igrad, keep, send = refs[:8]
        bias, mg_t, mg, q, dq, dk, dv, low_t, flat, square, dw_t, dwo, dgain = refs[8:]
    else:
        igrad, dw_t, dwo, dgain = refs[:4]
        bias, mg_t, mg, q, dq, dk, dv, low_t = refs[4:]
    b = pl.program_id(0) + lo
    rows = tok.shape[2]
    tiles = rows // TILE
    scale = HEAD_SIZE ** (-0.5)

    @pl.when(b == lo)
    def _():
        if final:
            dw_t[...] = dw_in[...]
            dwo[...] = dwo_in[...]
            dgain[...] = dgain_in[...]
        else:
            dw_t[...] = jnp.zeros_like(dw_t)
            dwo[...] = jnp.zeros_like(dwo)
            dgain[...] = jnp.zeros_like(dgain)

    @pl.when(live[b] == 0)
    def _():
        igrad[...] = jnp.zeros_like(igrad)

    @pl.when(live[b] > 0)
    def _():
        hl_t = hgrad[0].astype(bf16)
        dwo[...] += mm(mix_t[0], hl_t.T)
        mg_t[0] = mm(wo[...], hl_t).astype(bf16)
        for h in range(QUERY_HEADS):
            at = slice(h * HEAD_SIZE, (h + 1) * HEAD_SIZE)
            mg[h] = mg_t[0, at].T
            q[h] = qk_t[0, at].T
        fill_bias(bias, st_row[0])
        dq[...] = jnp.zeros_like(dq)
        dk[...] = jnp.zeros_like(dk)
        dv[...] = jnp.zeros_like(dv)

        for i in range(tiles):

            @pl.when(i < live[b])
            def _():
                for g in range(KEY_VALUE_HEADS):
                    width = (i + 1) * TILE
                    cols = slice(i * TILE, width)
                    q_t = head_rows(qk_t, g, cols)
                    mask = bias[:width, cols]
                    scores = mm(kv[0, g, :width], q_t) + jnp.concatenate([mask] * GROUP, axis=1)
                    prob = jnp.exp(scores - lse[0, g * tiles + i])
                    dp = mm(kv[0, KEY_VALUE_HEADS + g, :width], head_rows(mg_t, g, cols))
                    delta = jnp.sum(prob * dp, axis=0, keepdims=True)
                    ds = (prob * (dp - delta)).astype(bf16)
                    low = prob.astype(bf16)
                    k_t = qk_t[0, pl.ds(MODEL_WIDTH + g * HEAD_SIZE, HEAD_SIZE), :width]
                    dq_i = mm(k_t, ds) * scale
                    for h in range(GROUP):
                        dq[pl.ds((g * GROUP + h) * HEAD_SIZE, HEAD_SIZE), cols] = dq_i[
                            :, h * TILE : (h + 1) * TILE
                        ]
                    q_i = jnp.concatenate([q[g * GROUP + h, cols] for h in range(GROUP)], axis=0)
                    mg_i = jnp.concatenate([mg[g * GROUP + h, cols] for h in range(GROUP)], axis=0)
                    dk[g, :width] += mm(ds, q_i)
                    dv[g, :width] += mm(low, mg_i)

        c, s = cos[0], sin[0]
        for h in range(QUERY_HEADS + KEY_VALUE_HEADS):
            at = h * HEAD_SIZE
            u = dq[at : at + HEAD_SIZE] if h < QUERY_HEADS else dk[h - QUERY_HEADS].T
            u1, u2 = u[:HALF], u[HALF:]
            r = jnp.concatenate([u1 * c + u2 * s, u2 * c - u1 * s], axis=0)
            low_t[at : at + HEAD_SIZE] = r.astype(bf16)
        for g in range(KEY_VALUE_HEADS):
            at = MODEL_WIDTH + KV_WIDTH + g * HEAD_SIZE
            low_t[at : at + HEAD_SIZE] = dv[g].T.astype(bf16)
        x = tok[0].astype(f32)
        inverse = inverse_rms(x)
        gain = spread(gains[0], rows)
        dw_t[...] += mm(low_t[...], (x * inverse * gain).astype(bf16).T)
        ng = mm(w[...], low_t[...])
        dgain[...] += fold(ng * x * inverse)
        igrad[0] = hgrad[0] + norm_back(x, inverse, gain, ng)

    if not final:
        return

    @pl.when(pl.program_id(0) == pl.num_programs(0) - 1)
    def _():
        pairs = MODEL_WIDTH // 2
        put_columns(square, dw_t[0:MODEL_WIDTH].T)
        to_flat(square, flat, 0, pairs, 9)
        for which in range(2):
            at = MODEL_WIDTH + which * KV_WIDTH
            put_columns(square, dw_t[at : at + KV_WIDTH].T)
            to_flat(square, flat, (3 + which) * UNIT, pairs, 3)
        put_columns(square, dwo[...])
        to_flat(square, flat, 5 * UNIT, pairs, 9)
        lines = [jnp.sum(d[...].T, axis=0, keepdims=True) for d in (dgain, dgain_two)]
        line = jnp.concatenate(lines, axis=1)
        tail = [line[:, j * LANES : (j + 1) * LANES] for j in range(9)]
        tail = jnp.concatenate(tail + [jnp.zeros((GAIN_ROWS - 9, LANES), f32)], axis=0).astype(bf16)
        for k in range(UNITS):
            place = k ^ own[0]
            ours = tail if k == UNITS - 1 else jnp.zeros_like(tail)

            @pl.when(place % 2 == 0)
            def _():
                keep[place // 2, 0:UNIT] = flat[k * UNIT : (k + 1) * UNIT].astype(bf16)
                keep[place // 2, UNIT : UNIT + GAIN_ROWS] = ours

            @pl.when(place % 2 == 1)
            def _():
                send[place // 2, 0:UNIT] = flat[k * UNIT : (k + 1) * UNIT].astype(bf16)
                send[place // 2, UNIT : UNIT + GAIN_ROWS] = ours


def by_buffer(*shape, lo=0):
    zeros = (0,) * len(shape)
    return pl.BlockSpec((1,) + shape, lambda b, live, own: (b + lo if lo else b,) + zeros)


def whole(*shape):
    zeros = (0,) * len(shape)
    return pl.BlockSpec(shape, lambda b, live, own: zeros, pipeline_mode=pl.Buffered(1))


def call(kernel, name, buffers, in_specs, out_specs, outs, scratch, flops, moved, args, aliases=None):
    return pl.pallas_call(
        kernel,
        name=name,
        out_shape=[jax.ShapeDtypeStruct(shape, dtype) for shape, dtype in outs],
        grid_spec=pltpu.PrefetchScalarGridSpec(
            num_scalar_prefetch=2,
            grid=(buffers,),
            in_specs=in_specs,
            out_specs=out_specs,
            scratch_shapes=[pltpu.VMEM(shape, dtype) for shape, dtype in scratch],
        ),
        input_output_aliases=aliases or {},
        compiler_params=pltpu.CompilerParams(
            dimension_semantics=("arbitrary",), vmem_limit_bytes=60 * 1024 * 1024
        ),
        cost_estimate=pl.CostEstimate(flops=flops, bytes_accessed=moved, transcendentals=0),
    )(*args)


def run_attention_forward(live, own, tokens, st_row, cos, sin, units):
    n, d, t = tokens.shape
    lines = KEY_VALUE_HEADS * (t // TILE)
    return call(
        attention_forward, "attention_forward", n,
        [by_buffer(d, t), by_buffer(1, t), by_buffer(HALF, t), by_buffer(HALF, t), whole(UNITS, UNIT + GAIN_ROWS, LANES)],
        [by_buffer(d + KV_WIDTH, t), by_buffer(2 * KEY_VALUE_HEADS, t, HEAD_SIZE), by_buffer(d, t), by_buffer(d, t),
         by_buffer(lines, 1, GROUP * TILE), whole(d, QKV_WIDTH), whole(d, d), whole(2, d, LANES)],
        [((n, d + KV_WIDTH, t), bf16), ((n, 2 * KEY_VALUE_HEADS, t, HEAD_SIZE), bf16), ((n, d, t), bf16), ((n, d, t), f32),
         ((n, lines, 1, GROUP * TILE), f32), ((d, QKV_WIDTH), bf16), ((d, d), bf16), ((2, d, LANES), f32)],
        [((QKV_WIDTH, d), bf16), ((d, d), bf16), ((KEY_VALUE_HEADS, HEAD_SIZE, t), bf16), ((t, t), f32),
         ((UNITS * UNIT, LANES), f32), ((5, d, LANES), f32), ((d, LANES), f32)],
        8 * 10**9, 20 * 10**6,
        (live, own, tokens, st_row, cos, sin, units),
    )


def run_mlp(live, own, hidden, cot, st_row, gains, units):
    n, d, t = hidden.shape
    f = FEEDFWD_UNITS
    half = (UNITS // 2, 3, UNIT, LANES)
    return call(
        mlp, "mlp", n,
        [by_buffer(d, t), by_buffer(d, t), by_buffer(1, t), whole(2, d, LANES)] + [whole(3, UNIT, LANES)] * UNITS,
        [by_buffer(d, t), by_buffer(d, t), whole(*half), whole(*half), whole(d, LANES)],
        [((n, d, t), bf16), ((n, d, t), f32), (half, bf16), (half, bf16), ((d, LANES), f32)],
        [((d, f), bf16), ((d, f), bf16), ((f, d), bf16), ((f, d), bf16), ((f, d), bf16), ((d, f), bf16),
         ((f, d), f32), ((f, d), f32), ((f, d), f32), ((t, d), bf16), ((d, t), bf16), ((t, d), bf16), ((d, t), bf16),
         ((d, t), f32), ((d, t), f32), ((UNITS * UNIT, LANES), f32), ((5, LANES, LANES), f32)],
        33 * 10**9, 30 * 10**6,
        (live, own, hidden, cot, st_row, gains, *units),
    )


def run_attention_backward(lo, hi, live, own, hgrad, tokens, qk_t, kv, mix_t, lse, st_row, cos, sin, w, wo, gains, so_far=None):
    n, d, t = tokens.shape
    lines = KEY_VALUE_HEADS * (t // TILE)
    final = so_far is not None
    sums = [((QKV_WIDTH, d), f32), ((d, d), f32), ((d, LANES), f32)]
    of = functools.partial(by_buffer, lo=lo)
    in_specs = [of(d, t), of(d, t), of(d + KV_WIDTH, t), of(2 * KEY_VALUE_HEADS, t, HEAD_SIZE), of(d, t), of(lines, 1, GROUP * TILE),
                of(1, t), of(HALF, t), of(HALF, t), whole(d, QKV_WIDTH), whole(d, d), whole(2, d, LANES)]
    args = [live, own, hgrad, tokens, qk_t, kv, mix_t, lse, st_row, cos, sin, w, wo, gains]
    out_specs, outs = [of(d, t)], [((n, d, t), f32)]
    scratch = [((t, t), f32), ((1, d, t), bf16), ((QUERY_HEADS, t, HEAD_SIZE), bf16), ((QUERY_HEADS, t, HEAD_SIZE), bf16),
               ((d, t), f32), ((KEY_VALUE_HEADS, t, HEAD_SIZE), f32), ((KEY_VALUE_HEADS, t, HEAD_SIZE), f32), ((QKV_WIDTH, t), bf16)]
    aliases = {}
    if final:
        half = (UNITS // 2, UNIT + GAIN_ROWS, LANES)
        in_specs += [whole(d, LANES)] + [whole(*shape) for shape, _ in sums] + [pl.BlockSpec(memory_space=pl.ANY)]
        args += list(so_far)
        aliases = {len(args) - 1: 0}
        out_specs += [whole(*half)] * 2
        outs += [(half, bf16)] * 2
        scratch += [((UNITS * UNIT, LANES), f32), ((5, d, LANES), f32)] + sums
    else:
        out_specs += [whole(*shape) for shape, _ in sums]
        outs += sums
    return call(
        functools.partial(attention_backward, lo, final), "attention_backward", hi - lo,
        in_specs, out_specs, outs, scratch, 8 * 10**9, 20 * 10**6, args, aliases,
    )


def swap(x, bits):
    size = lax.axis_size("dp")
    return lax.ppermute(x, "dp", [(i, i ^ bits) for i in range(size)])


def plane(i):
    return i // UNITS


def pick(pieces, index):
    chosen = pieces[0]
    for i, piece in enumerate(pieces[1:], 1):
        chosen = jnp.where(index == i, piece, chosen)
    return chosen


def with_partners(even):
    return [piece for mine in even for piece in (mine, swap(mine, 1))]


def core_sums(keep, send):
    other = swap(send, 1)
    sums = [keep[j].astype(f32) + other[j].astype(f32) for j in range(UNITS // 2)]
    return [sums[0]] + [s.astype(bf16) for s in sums[1:]]


def to_plane(two, four, six):
    return [swap(two, 2), swap(four, 4), swap(six, 6)]


def plane_sums(own, two, four, six):
    return (own + two.astype(f32)) + (four.astype(f32) + six.astype(f32))


def add_up(value):
    bits = 1
    while bits < lax.axis_size("dp"):
        value = value + swap(value, bits)
        bits *= 2
    return value


def document_tables(doc_starts):
    rows = doc_starts.shape[1]
    is_live = doc_starts < rows
    live = jnp.sum(is_live.astype(jnp.int32), axis=1) // TILE
    positions = jnp.where(is_live, jnp.arange(rows) - doc_starts, 0).astype(f32)
    frequency = rope_base ** (-(jnp.arange(HALF, dtype=f32) * 2.0 / HEAD_SIZE))
    angles = frequency[None, :, None] * positions[:, None, :]
    cos, sin = jnp.cos(angles), jnp.sin(angles)
    st_row = doc_starts.astype(f32)[:, None, :]
    return live, cos, sin, st_row


def local(tokens, doc_starts, cotangent, master, moment_one, moment_two):
    size = lax.axis_size("dp")
    me = lax.axis_index("dp")
    z = plane(me)
    buffers, rows = tokens.shape[:2]
    shard = master.shape[0] // LANES
    total = 4 * UNITS * UNIT
    by_units = size == 4 * UNITS and shard == UNIT + 1
    own_rows = master.reshape(shard, LANES)
    if by_units:
        own = me % UNITS
        before = lax.ppermute(own_rows[shard - size :], "dp", [(i, i + 1) for i in range(size - 1)])
        unit = lax.dynamic_slice_in_dim(jnp.concatenate([before, own_rows], axis=0), size - me, UNIT).astype(bf16)
        gain_at = total - (size - 1) * shard
        gain_rows = own_rows[gain_at : gain_at + GAIN_ROWS].astype(bf16)
        rows_here = jnp.concatenate([unit, jnp.where(me == size - 1, gain_rows, jnp.zeros_like(gain_rows))], axis=0)
        rows_here, unit, doc_starts = lax.optimization_barrier((rows_here, unit, doc_starts))
        live, cos, sin, st_row = document_tables(doc_starts)
        later, cos = lax.optimization_barrier((unit, cos))
        last = size // UNITS - 1
        head = jnp.concatenate([jnp.where(z == 0, rows_here[:UNIT], jnp.zeros_like(unit)), rows_here[UNIT:]], axis=0)
        arrived = []
        for far in (3, 2, 1):
            pairs = [(k, far * UNITS + k) for k in range(UNITS)] + [(size - 1, (last - far) * UNITS + UNITS - 1)]
            arrived.append(lax.ppermute(head, "dp", pairs))
        planes = [unit]
        for far in (1, 2, 3):
            pairs = [(i, i ^ (far * UNITS)) for i in range(size) if plane(i) > 0]
            planes.append(lax.ppermute(later, "dp", pairs))
        head = (head + arrived[0]) + (arrived[1] + arrived[2])
        rest = jnp.stack([pick(planes, z ^ p) for p in (1, 2, 3)])
        around = [swap(head, bits) for bits in (2, 4, 6)]
        rest, *around = lax.optimization_barrier((rest, *around))
        units = jnp.stack(with_partners([head, *around]))
        rest_around = [swap(rest, bits) for bits in (2, 4, 6)]
    else:
        live, cos, sin, st_row = document_tables(doc_starts)
        own = jnp.zeros_like(me)
        all_rows = lax.all_gather(own_rows.astype(bf16), "dp", axis=0, tiled=True)
        units = all_rows[: UNITS * UNIT].reshape(UNITS, UNIT, LANES)
        gain_rows = jnp.pad(all_rows[None, total : total + GAIN_ROWS], ((UNITS - 1, 0), (0, 0), (0, 0)))
        units = jnp.concatenate([units, gain_rows], axis=1)
        late_units = all_rows[UNITS * UNIT : total].reshape(3, UNITS, UNIT, LANES)
        late_units = [late_units[:, k] for k in range(UNITS)]
    own = own.astype(jnp.int32).reshape(1)

    tok_t, cot_t = tokens.transpose(0, 2, 1), cotangent.transpose(0, 2, 1)

    qk_t, kv, mix_t, hidden, lse, w, wo, gains = run_attention_forward(live, own, tok_t, st_row, cos, sin, units)
    if by_units:
        hidden, *rest_around = lax.optimization_barrier((hidden, *rest_around))
        late_units = with_partners([rest, *rest_around])
    layer, hgrad, keep, send, dgain_two = run_mlp(live, own, hidden, cot_t, st_row, gains, late_units)
    shared = (live, own, hgrad, tok_t, qk_t, kv, mix_t, lse, st_row, cos, sin, w, wo, gains)
    igrad, dw_t, dwo, dgain = run_attention_backward(0, buffers // 2, *shared)
    if by_units:
        late = core_sums(keep, send)
        dgain, *late = lax.optimization_barrier((dgain, *late))
        arrived = to_plane(*late[1:])
    igrad, keep_early, send_early = run_attention_backward(
        buffers // 2, buffers, *shared, so_far=(dgain_two, dw_t, dwo, dgain, igrad)
    )
    if by_units:
        keep_early, send_early, *arrived = lax.optimization_barrier((keep_early, send_early, *arrived))
        late_sum = plane_sums(late[0], *arrived)
        mine = lax.dynamic_index_in_dim(late_sum, jnp.maximum(z - 1, 0), 0, keepdims=False)
        sent = [
            lax.dynamic_index_in_dim(late_sum, jnp.maximum((z ^ far) - 1, 0), 0, keepdims=False).astype(bf16)
            for far in (1, 2, 3)
        ]
        send_early, *sent = lax.optimization_barrier((send_early, *sent))
        for far in (1, 2, 3):
            pairs = [(i, i ^ (far * UNITS)) for i in range(size) if plane(i ^ (far * UNITS)) > 0]
            sent[far - 1] = lax.ppermute(sent[far - 1], "dp", pairs)
        early = core_sums(keep_early, send_early)
        arrived = to_plane(*early[1:])
        sent_and_arrived = lax.optimization_barrier((*sent, *arrived))
        sent, arrived = sent_and_arrived[:3], sent_and_arrived[3:]
        for piece in sent:
            mine = mine + piece.astype(f32)
        early_sum = plane_sums(early[0], *arrived)
        early_low = early_sum.astype(bf16)
        for far in (1, 2, 3):
            pairs = [(far * UNITS + k, k) for k in range(UNITS)]
            pairs += [((last ^ far) * UNITS + UNITS - 1, size - 1)]
            early_sum = early_sum + lax.ppermute(early_low, "dp", pairs).astype(f32)
        unit_grad = jnp.where(z == 0, early_sum[:UNIT], mine)
        gain_grads = jnp.where(me == size - 1, early_sum[UNIT:], 0.0)
        square_sum = jnp.sum(unit_grad * unit_grad) + jnp.sum(gain_grads * gain_grads)
        square_sum = add_up(jnp.broadcast_to(square_sum, (8, LANES)))[0, 0]
        after = lax.ppermute(unit_grad[:size], "dp", [(i + 1, i) for i in range(size - 1)])
        after = after + jnp.pad(gain_grads, ((0, size - GAIN_ROWS), (0, 0)))
        grad_shard = lax.dynamic_slice_in_dim(jnp.concatenate([unit_grad, after], axis=0), me, shard).reshape(-1)
    else:
        early = jnp.stack([keep_early, send_early], axis=1).reshape(UNITS, UNIT + GAIN_ROWS, LANES)
        late = jnp.stack([keep, send], axis=1).reshape(UNITS, 3, UNIT, LANES)
        pieces = [early[:, :UNIT].reshape(-1, LANES)] + [late[:, p].reshape(-1, LANES) for p in range(3)]
        grads = jnp.concatenate(pieces + [early[UNITS - 1, UNIT:]], axis=0).astype(f32)
        grads = jnp.pad(grads, ((0, size * shard - grads.shape[0]), (0, 0)))
        grad_shard = lax.psum_scatter(grads.reshape(-1), "dp", scatter_dimension=0, tiled=True)
        square_sum = lax.psum(jnp.sum(grad_shard * grad_shard), "dp")
    grad_norm = jnp.sqrt(square_sum)
    clipped = grad_shard * (clip_norm / jnp.maximum(grad_norm, clip_norm))
    new_one = decay_one * moment_one + (1.0 - decay_one) * clipped
    new_two = decay_two * moment_two + (1.0 - decay_two) * clipped * clipped
    corrected_one = new_one / (1.0 - decay_one**STEP)
    corrected_two = new_two / (1.0 - decay_two**STEP)
    new_master = master - learn_rate * (
        corrected_one / (jnp.sqrt(corrected_two) + adam_eps) + weight_decay * master
    )
    return (layer.transpose(0, 2, 1), igrad.transpose(0, 2, 1), grad_shard, grad_norm, new_master, new_one, new_two)


def solution(mesh):
    flat, cube = P("dp"), P("dp", None, None)
    return jax.shard_map(
        local,
        mesh=mesh,
        in_specs=(cube, P("dp", None), cube, flat, flat, flat),
        out_specs=(cube, cube, flat, P(), flat, flat, flat),
        check_vma=False,
    )
```

```python
import functools

import jax
import jax.numpy as jnp
from jax import lax
from jax.experimental import pallas as pl
from jax.experimental.pallas import tpu as pltpu
from jax.sharding import PartitionSpec as P

MODEL_WIDTH = 576
QUERY_HEADS = 9
KEY_VALUE_HEADS = 3
HEAD_SIZE = 64
FEEDFWD_UNITS = 1536
TILE = 128
STEP = 8
GROUP = QUERY_HEADS // KEY_VALUE_HEADS
HALF = HEAD_SIZE // 2
KV_WIDTH = KEY_VALUE_HEADS * HEAD_SIZE
QKV_WIDTH = MODEL_WIDTH + 2 * KV_WIDTH
CHUNK = 1536
LANES = 128
UNIT = MODEL_WIDTH * KV_WIDTH // LANES
GAIN_ROWS = 16
UNITS = 8
FEEDFWD_TILES = FEEDFWD_UNITS // LANES

rms_eps = 1e-05
rope_base = 100000.0
learn_rate = 0.02
decay_one = 0.9
decay_two = 0.999
adam_eps = 1e-08
weight_decay = 0.1
clip_norm = 1.0
mask_fill = -1000000000.0

bf16 = jnp.bfloat16
f32 = jnp.float32


def mm(a, b):
    return jnp.dot(a, b, preferred_element_type=f32)


def inverse_rms(x):
    return lax.rsqrt(jnp.mean(x * x, axis=0, keepdims=True) + rms_eps)


def spread(gain, tokens):
    return jnp.concatenate([gain] * (tokens // LANES), axis=1)


def fold(x):
    return sum(x[:, t : t + LANES] for t in range(0, x.shape[1], LANES))


def norm_back(x, inverse, gain, grad):
    e = grad * gain
    return inverse * e - x * (inverse * inverse * inverse) * jnp.mean(e * x, axis=0, keepdims=True)


def fill_bias(bias, starts_row):
    rows = starts_row.shape[1]
    starts_col = jnp.broadcast_to(starts_row, (TILE, rows)).T
    key_at = lax.broadcasted_iota(jnp.int32, (rows, TILE), 0)
    for i in range(rows // TILE):
        width = (i + 1) * TILE
        query_at = lax.broadcasted_iota(jnp.int32, (rows, TILE), 1) + i * TILE
        allowed = (starts_col == starts_row[:, i * TILE : width]) & (key_at <= query_at)
        bias[:, i * TILE : width] = jnp.where(allowed, 0.0, mask_fill)


def half_turn(x):
    return pltpu.roll(x, HEAD_SIZE, 1)


def to_matrix(flat, base, out, pairs, tiles):
    half = tiles // 2
    low = lax.broadcasted_iota(jnp.int32, (pairs, LANES), 1) < HEAD_SIZE
    for t in range(half + 1):
        out[t, pl.ds(0, pairs, stride=2), :] = flat[pl.ds(base + t, pairs, stride=tiles), :]
    turned = half_turn(flat[pl.ds(base + half, pairs, stride=tiles), :])
    for t in range(half):
        following = half_turn(flat[pl.ds(base + half + t + 1, pairs, stride=tiles), :])
        out[t, pl.ds(1, pairs, stride=2), :] = jnp.where(low, turned, following)
        turned = following
    out[half, pl.ds(1, pairs, stride=2), :] = turned


def to_flat(matrix, flat, base, pairs, tiles):
    half = tiles // 2
    low = lax.broadcasted_iota(jnp.int32, (pairs, LANES), 1) < HEAD_SIZE
    for t in range(half):
        flat[pl.ds(base + t, pairs, stride=tiles), :] = matrix[t, pl.ds(0, pairs, stride=2), :]
    before = matrix[half, pl.ds(0, pairs, stride=2), :]
    for t in range(half + 1):
        turned = half_turn(matrix[t, pl.ds(1, pairs, stride=2), :])
        flat[pl.ds(base + half + t, pairs, stride=tiles), :] = jnp.where(low, before, turned)
        before = turned


def columns_of(matrix, rows, width):
    full = width // LANES
    return jnp.concatenate([matrix[t, :rows] for t in range(full)] + [matrix[full, :rows, :HEAD_SIZE]], axis=1)


def put_columns(matrix, value):
    rows, width = value.shape
    full = width // LANES
    for t in range(full):
        matrix[t, :rows] = value[:, t * LANES : (t + 1) * LANES]
    matrix[full, :rows, :HEAD_SIZE] = value[:, full * LANES :]


def head_rows(ref, g, columns):
    return jnp.concatenate(
        [ref[0, pl.ds((g * GROUP + h) * HEAD_SIZE, HEAD_SIZE), columns] for h in range(GROUP)], axis=1
    )


def attention_forward(
    live, own, tok, st_row, cos, sin, units,
    qk_t, kv, mix_t, hidden, lse, w, wo, gains,
    w_t, wo_t, v_t, bias, flat, square, gain
):
    b = pl.program_id(0)
    rows = tok.shape[2]

    @pl.when(b == 0)
    def _():
        for k in range(UNITS):
            flat[k * UNIT : (k + 1) * UNIT] = units[k ^ own[0], 0:UNIT].astype(f32)
        pairs = MODEL_WIDTH // 2
        to_matrix(flat, 5 * UNIT, square, pairs, 9)
        value = columns_of(square, MODEL_WIDTH, MODEL_WIDTH)
        wo[...] = value.astype(bf16)
        wo_t[...] = value.T.astype(bf16)
        to_matrix(flat, 0, square, pairs, 9)
        value = columns_of(square, MODEL_WIDTH, MODEL_WIDTH)
        w[:, 0:MODEL_WIDTH] = value.astype(bf16)
        w_t[0:MODEL_WIDTH] = value.T.astype(bf16)
        for which in range(2):
            at = MODEL_WIDTH + which * KV_WIDTH
            to_matrix(flat, (3 + which) * UNIT, square, pairs, 3)
            value = columns_of(square, MODEL_WIDTH, KV_WIDTH)
            w[:, at : at + KV_WIDTH] = value.astype(bf16)
            w_t[at : at + KV_WIDTH] = value.T.astype(bf16)
        tail = units[(UNITS - 1) ^ own[0], UNIT : UNIT + GAIN_ROWS].astype(f32)
        line = jnp.concatenate([tail[j : j + 1] for j in range(9)], axis=1)
        for which in range(2):
            one = line[:, which * MODEL_WIDTH : (which + 1) * MODEL_WIDTH]
            gains[which] = jnp.broadcast_to(one, (LANES, MODEL_WIDTH)).T
        gain[...] = gains[0]

    @pl.when(live[b] > 0)
    def _():
        x = tok[0].astype(f32)
        n1_t = (x * inverse_rms(x) * spread(gain[...], rows)).astype(bf16)
        c, s = cos[0], sin[0]
        for h in range(QUERY_HEADS + KEY_VALUE_HEADS):
            at = h * HEAD_SIZE
            u = mm(w_t[at : at + HEAD_SIZE], n1_t)
            u1, u2 = u[:HALF], u[HALF:]
            r = jnp.concatenate([u1 * c - u2 * s, u2 * c + u1 * s], axis=0)
            if h < QUERY_HEADS:
                r = r * HEAD_SIZE ** (-0.5)
            r = r.astype(bf16)
            qk_t[0, at : at + HEAD_SIZE] = r
            if h >= QUERY_HEADS:
                kv[0, h - QUERY_HEADS] = r.T
        for g in range(KEY_VALUE_HEADS):
            at = MODEL_WIDTH + KV_WIDTH + g * HEAD_SIZE
            v = mm(w_t[at : at + HEAD_SIZE], n1_t).astype(bf16)
            v_t[g] = v
            kv[0, KEY_VALUE_HEADS + g] = v.T
        fill_bias(bias, st_row[0])
        mix_t[...] = jnp.zeros_like(mix_t)

        for i in range(rows // TILE):

            @pl.when(i < live[b])
            def _():
                for g in range(KEY_VALUE_HEADS):
                    width = (i + 1) * TILE
                    cols = slice(i * TILE, width)
                    q_t = head_rows(qk_t, g, cols)
                    mask = bias[:width, cols]
                    scores = mm(kv[0, g, :width], q_t) + jnp.concatenate([mask] * GROUP, axis=1)
                    peak = jnp.max(scores, axis=0, keepdims=True)
                    e = jnp.exp(scores - peak)
                    total = jnp.sum(e, axis=0, keepdims=True)
                    prob = (e * (1.0 / total)).astype(bf16)
                    lse[0, g * (rows // TILE) + i] = peak + jnp.log(total)
                    out = mm(v_t[g, :, :width], prob).astype(bf16)
                    for h in range(GROUP):
                        mix_t[0, pl.ds((g * GROUP + h) * HEAD_SIZE, HEAD_SIZE), cols] = out[
                            :, h * TILE : (h + 1) * TILE
                        ]

        hidden[0] = tok[0].astype(f32) + mm(wo_t[...], mix_t[0])


def mlp(
    live, own, hidden, cot, st_row, gains, *refs
):
    units, refs = refs[:UNITS], refs[UNITS:]
    layer, hgrad, keep, send, dgain, *refs = refs
    wg, wu, wd, wg_t, wu_t, wd_t, dwg_t, dwu_t, dwd, n2, n2_t, rl, rl_t, n2g, res, flat, slab = refs
    b = pl.program_id(0)
    rows = hidden.shape[2]

    @pl.when(b == 0)
    def _():
        def spell_out(which):
            half = UNIT // 2
            for m in range(UNITS):

                def place(part, carry):
                    to = pl.multiple_of((own[0] ^ m) * UNIT + part * half, 8)
                    at = pl.multiple_of(part * half, 16)
                    flat[pl.ds(to, half)] = units[m][which, pl.ds(at, half)].astype(f32)
                    return carry

                lax.fori_loop(0, 2, place, 0)

        for which, straight, turned in ((0, wg, wg_t), (1, wu, wu_t)):
            spell_out(which)
            for j in range(FEEDFWD_TILES):
                at = slice(j * LANES, (j + 1) * LANES)
                part = flat[pl.ds(j, MODEL_WIDTH, stride=FEEDFWD_TILES), :]
                straight[:, at] = part.astype(bf16)
                turned[at] = part.T.astype(bf16)
        spell_out(2)
        for j in range(FEEDFWD_TILES):
            at = slice(j * LANES, (j + 1) * LANES)
            to_matrix(flat, j * MODEL_WIDTH, slab, LANES // 2, 9)
            value = columns_of(slab, LANES, MODEL_WIDTH)
            wd[at] = value.astype(bf16)
            wd_t[:, at] = value.T.astype(bf16)
        dwg_t[...] = jnp.zeros_like(dwg_t)
        dwu_t[...] = jnp.zeros_like(dwu_t)
        dwd[...] = jnp.zeros_like(dwd)
        dgain[...] = jnp.zeros_like(dgain)

    @pl.when(live[b] == 0)
    def _():
        layer[...] = jnp.zeros_like(layer)
        hgrad[...] = jnp.zeros_like(hgrad)

    @pl.when(live[b] > 0)
    def _():
        x = hidden[0]
        inverse = inverse_rms(x)
        alive = st_row[0] < rows
        normed = (x * inverse * spread(gains[1], rows)).astype(bf16)
        n2_t[...] = normed
        n2[...] = normed.T
        grad = jnp.where(alive, cot[0].astype(f32), 0.0).astype(bf16)
        rl_t[...] = grad
        rl[...] = grad.T
        res[...] = jnp.zeros_like(res)
        n2g[...] = jnp.zeros_like(n2g)

        def chunk(k, carry):
            at = pl.ds(pl.multiple_of(k * CHUNK, CHUNK), CHUNK)
            pre = mm(wg_t[at, :], n2_t[...])
            up = mm(wu_t[at, :], n2_t[...])
            ag = mm(wd[at, :], rl_t[...])
            s = jax.nn.sigmoid(pre)
            silu = pre * s
            act = (silu * up).astype(bf16)
            gl = (ag * up * s * (1.0 + pre * (1.0 - s))).astype(bf16)
            ul = (ag * silu).astype(bf16)
            res[...] += mm(wd_t[:, at], act)
            n2g[...] += mm(wg[:, at], gl) + mm(wu[:, at], ul)
            dwd[at, :] += mm(act, rl[...])
            dwg_t[at, :] += mm(gl, n2[...])
            dwu_t[at, :] += mm(ul, n2[...])
            return carry

        lax.fori_loop(0, FEEDFWD_UNITS // CHUNK, chunk, 0)
        x = hidden[0]
        layer[0] = jnp.where(alive, x + res[...], 0.0).astype(bf16)
        ng = n2g[...]
        dgain[...] += fold(ng * x * inverse)
        hgrad[0] = rl_t[...].astype(f32) + norm_back(x, inverse, spread(gains[1], rows), ng)

    @pl.when(b == pl.num_programs(0) - 1)
    def _():
        for p in range(3):
            for j in range(FEEDFWD_TILES):
                at = slice(j * LANES, (j + 1) * LANES)
                if p < 2:
                    flat[pl.ds(j, MODEL_WIDTH, stride=FEEDFWD_TILES), :] = (dwg_t, dwu_t)[p][at].T
                else:
                    put_columns(slab, dwd[at])
                    to_flat(slab, flat, j * MODEL_WIDTH, LANES // 2, 9)
            for k in range(UNITS):
                place = k ^ own[0]

                @pl.when(place % 2 == 0)
                def _():
                    keep[place // 2, p] = flat[k * UNIT : (k + 1) * UNIT].astype(bf16)

                @pl.when(place % 2 == 1)
                def _():
                    send[place // 2, p] = flat[k * UNIT : (k + 1) * UNIT].astype(bf16)


def attention_backward(
    lo, final, live, own, hgrad, tok, qk_t, kv, mix_t, lse, st_row, cos, sin, w, wo, gains, *refs
):
    if final:
        dgain_two, dw_in, dwo_in, dgain_in, _, igrad, keep, send = refs[:8]
        bias, mg_t, mg, q, dq, dk, dv, low_t, flat, square, dw_t, dwo, dgain = refs[8:]
    else:
        igrad, dw_t, dwo, dgain = refs[:4]
        bias, mg_t, mg, q, dq, dk, dv, low_t = refs[4:]
    b = pl.program_id(0) + lo
    rows = tok.shape[2]
    tiles = rows // TILE
    scale = HEAD_SIZE ** (-0.5)

    @pl.when(b == lo)
    def _():
        if final:
            dw_t[...] = dw_in[...]
            dwo[...] = dwo_in[...]
            dgain[...] = dgain_in[...]
        else:
            dw_t[...] = jnp.zeros_like(dw_t)
            dwo[...] = jnp.zeros_like(dwo)
            dgain[...] = jnp.zeros_like(dgain)

    @pl.when(live[b] == 0)
    def _():
        igrad[...] = jnp.zeros_like(igrad)

    @pl.when(live[b] > 0)
    def _():
        hl_t = hgrad[0].astype(bf16)
        dwo[...] += mm(mix_t[0], hl_t.T)
        mg_t[0] = mm(wo[...], hl_t).astype(bf16)
        for h in range(QUERY_HEADS):
            at = slice(h * HEAD_SIZE, (h + 1) * HEAD_SIZE)
            mg[h] = mg_t[0, at].T
            q[h] = qk_t[0, at].T
        fill_bias(bias, st_row[0])
        dq[...] = jnp.zeros_like(dq)
        dk[...] = jnp.zeros_like(dk)
        dv[...] = jnp.zeros_like(dv)

        for i in range(tiles):

            @pl.when(i < live[b])
            def _():
                for g in range(KEY_VALUE_HEADS):
                    width = (i + 1) * TILE
                    cols = slice(i * TILE, width)
                    q_t = head_rows(qk_t, g, cols)
                    mask = bias[:width, cols]
                    scores = mm(kv[0, g, :width], q_t) + jnp.concatenate([mask] * GROUP, axis=1)
                    prob = jnp.exp(scores - lse[0, g * tiles + i])
                    dp = mm(kv[0, KEY_VALUE_HEADS + g, :width], head_rows(mg_t, g, cols))
                    delta = jnp.sum(prob * dp, axis=0, keepdims=True)
                    ds = (prob * (dp - delta)).astype(bf16)
                    low = prob.astype(bf16)
                    k_t = qk_t[0, pl.ds(MODEL_WIDTH + g * HEAD_SIZE, HEAD_SIZE), :width]
                    dq_i = mm(k_t, ds) * scale
                    for h in range(GROUP):
                        dq[pl.ds((g * GROUP + h) * HEAD_SIZE, HEAD_SIZE), cols] = dq_i[
                            :, h * TILE : (h + 1) * TILE
                        ]
                    q_i = jnp.concatenate([q[g * GROUP + h, cols] for h in range(GROUP)], axis=0)
                    mg_i = jnp.concatenate([mg[g * GROUP + h, cols] for h in range(GROUP)], axis=0)
                    dk[g, :width] += mm(ds, q_i)
                    dv[g, :width] += mm(low, mg_i)

        c, s = cos[0], sin[0]
        for h in range(QUERY_HEADS + KEY_VALUE_HEADS):
            at = h * HEAD_SIZE
            u = dq[at : at + HEAD_SIZE] if h < QUERY_HEADS else dk[h - QUERY_HEADS].T
            u1, u2 = u[:HALF], u[HALF:]
            r = jnp.concatenate([u1 * c + u2 * s, u2 * c - u1 * s], axis=0)
            low_t[at : at + HEAD_SIZE] = r.astype(bf16)
        for g in range(KEY_VALUE_HEADS):
            at = MODEL_WIDTH + KV_WIDTH + g * HEAD_SIZE
            low_t[at : at + HEAD_SIZE] = dv[g].T.astype(bf16)
        x = tok[0].astype(f32)
        inverse = inverse_rms(x)
        gain = spread(gains[0], rows)
        dw_t[...] += mm(low_t[...], (x * inverse * gain).astype(bf16).T)
        ng = mm(w[...], low_t[...])
        dgain[...] += fold(ng * x * inverse)
        igrad[0] = hgrad[0] + norm_back(x, inverse, gain, ng)

    if not final:
        return

    @pl.when(pl.program_id(0) == pl.num_programs(0) - 1)
    def _():
        pairs = MODEL_WIDTH // 2
        put_columns(square, dw_t[0:MODEL_WIDTH].T)
        to_flat(square, flat, 0, pairs, 9)
        for which in range(2):
            at = MODEL_WIDTH + which * KV_WIDTH
            put_columns(square, dw_t[at : at + KV_WIDTH].T)
            to_flat(square, flat, (3 + which) * UNIT, pairs, 3)
        put_columns(square, dwo[...])
        to_flat(square, flat, 5 * UNIT, pairs, 9)
        lines = [jnp.sum(d[...].T, axis=0, keepdims=True) for d in (dgain, dgain_two)]
        line = jnp.concatenate(lines, axis=1)
        tail = [line[:, j * LANES : (j + 1) * LANES] for j in range(9)]
        tail = jnp.concatenate(tail + [jnp.zeros((GAIN_ROWS - 9, LANES), f32)], axis=0).astype(bf16)
        for k in range(UNITS):
            place = k ^ own[0]
            ours = tail if k == UNITS - 1 else jnp.zeros_like(tail)

            @pl.when(place % 2 == 0)
            def _():
                keep[place // 2, 0:UNIT] = flat[k * UNIT : (k + 1) * UNIT].astype(bf16)
                keep[place // 2, UNIT : UNIT + GAIN_ROWS] = ours

            @pl.when(place % 2 == 1)
            def _():
                send[place // 2, 0:UNIT] = flat[k * UNIT : (k + 1) * UNIT].astype(bf16)
                send[place // 2, UNIT : UNIT + GAIN_ROWS] = ours


def by_buffer(*shape, lo=0):
    zeros = (0,) * len(shape)
    return pl.BlockSpec((1,) + shape, lambda b, live, own: (b + lo if lo else b,) + zeros)


def whole(*shape):
    zeros = (0,) * len(shape)
    return pl.BlockSpec(shape, lambda b, live, own: zeros, pipeline_mode=pl.Buffered(1))


def call(kernel, name, buffers, in_specs, out_specs, outs, scratch, flops, moved, args, aliases=None):
    return pl.pallas_call(
        kernel,
        name=name,
        out_shape=[jax.ShapeDtypeStruct(shape, dtype) for shape, dtype in outs],
        grid_spec=pltpu.PrefetchScalarGridSpec(
            num_scalar_prefetch=2,
            grid=(buffers,),
            in_specs=in_specs,
            out_specs=out_specs,
            scratch_shapes=[pltpu.VMEM(shape, dtype) for shape, dtype in scratch],
        ),
        input_output_aliases=aliases or {},
        compiler_params=pltpu.CompilerParams(
            dimension_semantics=("arbitrary",), vmem_limit_bytes=60 * 1024 * 1024
        ),
        cost_estimate=pl.CostEstimate(flops=flops, bytes_accessed=moved, transcendentals=0),
    )(*args)


def run_attention_forward(live, own, tokens, st_row, cos, sin, units):
    n, d, t = tokens.shape
    lines = KEY_VALUE_HEADS * (t // TILE)
    return call(
        attention_forward, "attention_forward", n,
        [by_buffer(d, t), by_buffer(1, t), by_buffer(HALF, t), by_buffer(HALF, t), whole(UNITS, UNIT + GAIN_ROWS, LANES)],
        [by_buffer(d + KV_WIDTH, t), by_buffer(2 * KEY_VALUE_HEADS, t, HEAD_SIZE), by_buffer(d, t), by_buffer(d, t),
         by_buffer(lines, 1, GROUP * TILE), whole(d, QKV_WIDTH), whole(d, d), whole(2, d, LANES)],
        [((n, d + KV_WIDTH, t), bf16), ((n, 2 * KEY_VALUE_HEADS, t, HEAD_SIZE), bf16), ((n, d, t), bf16), ((n, d, t), f32),
         ((n, lines, 1, GROUP * TILE), f32), ((d, QKV_WIDTH), bf16), ((d, d), bf16), ((2, d, LANES), f32)],
        [((QKV_WIDTH, d), bf16), ((d, d), bf16), ((KEY_VALUE_HEADS, HEAD_SIZE, t), bf16), ((t, t), f32),
         ((UNITS * UNIT, LANES), f32), ((5, d, LANES), f32), ((d, LANES), f32)],
        8 * 10**9, 20 * 10**6,
        (live, own, tokens, st_row, cos, sin, units),
    )


def run_mlp(live, own, hidden, cot, st_row, gains, units):
    n, d, t = hidden.shape
    f = FEEDFWD_UNITS
    half = (UNITS // 2, 3, UNIT, LANES)
    return call(
        mlp, "mlp", n,
        [by_buffer(d, t), by_buffer(d, t), by_buffer(1, t), whole(2, d, LANES)] + [whole(3, UNIT, LANES)] * UNITS,
        [by_buffer(d, t), by_buffer(d, t), whole(*half), whole(*half), whole(d, LANES)],
        [((n, d, t), bf16), ((n, d, t), f32), (half, bf16), (half, bf16), ((d, LANES), f32)],
        [((d, f), bf16), ((d, f), bf16), ((f, d), bf16), ((f, d), bf16), ((f, d), bf16), ((d, f), bf16),
         ((f, d), f32), ((f, d), f32), ((f, d), f32), ((t, d), bf16), ((d, t), bf16), ((t, d), bf16), ((d, t), bf16),
         ((d, t), f32), ((d, t), f32), ((UNITS * UNIT, LANES), f32), ((5, LANES, LANES), f32)],
        33 * 10**9, 30 * 10**6,
        (live, own, hidden, cot, st_row, gains, *units),
    )


def run_attention_backward(lo, hi, live, own, hgrad, tokens, qk_t, kv, mix_t, lse, st_row, cos, sin, w, wo, gains, so_far=None):
    n, d, t = tokens.shape
    lines = KEY_VALUE_HEADS * (t // TILE)
    final = so_far is not None
    sums = [((QKV_WIDTH, d), f32), ((d, d), f32), ((d, LANES), f32)]
    of = functools.partial(by_buffer, lo=lo)
    in_specs = [of(d, t), of(d, t), of(d + KV_WIDTH, t), of(2 * KEY_VALUE_HEADS, t, HEAD_SIZE), of(d, t), of(lines, 1, GROUP * TILE),
                of(1, t), of(HALF, t), of(HALF, t), whole(d, QKV_WIDTH), whole(d, d), whole(2, d, LANES)]
    args = [live, own, hgrad, tokens, qk_t, kv, mix_t, lse, st_row, cos, sin, w, wo, gains]
    out_specs, outs = [of(d, t)], [((n, d, t), f32)]
    scratch = [((t, t), f32), ((1, d, t), bf16), ((QUERY_HEADS, t, HEAD_SIZE), bf16), ((QUERY_HEADS, t, HEAD_SIZE), bf16),
               ((d, t), f32), ((KEY_VALUE_HEADS, t, HEAD_SIZE), f32), ((KEY_VALUE_HEADS, t, HEAD_SIZE), f32), ((QKV_WIDTH, t), bf16)]
    aliases = {}
    if final:
        half = (UNITS // 2, UNIT + GAIN_ROWS, LANES)
        in_specs += [whole(d, LANES)] + [whole(*shape) for shape, _ in sums] + [pl.BlockSpec(memory_space=pl.ANY)]
        args += list(so_far)
        aliases = {len(args) - 1: 0}
        out_specs += [whole(*half)] * 2
        outs += [(half, bf16)] * 2
        scratch += [((UNITS * UNIT, LANES), f32), ((5, d, LANES), f32)] + sums
    else:
        out_specs += [whole(*shape) for shape, _ in sums]
        outs += sums
    return call(
        functools.partial(attention_backward, lo, final), "attention_backward", hi - lo,
        in_specs, out_specs, outs, scratch, 8 * 10**9, 20 * 10**6, args, aliases,
    )


def swap(x, bits):
    size = lax.axis_size("dp")
    return lax.ppermute(x, "dp", [(i, i ^ bits) for i in range(size)])


def plane(i):
    return i // UNITS


def pick(pieces, index):
    chosen = pieces[0]
    for i, piece in enumerate(pieces[1:], 1):
        chosen = jnp.where(index == i, piece, chosen)
    return chosen


def with_partners(even):
    return [piece for mine in even for piece in (mine, swap(mine, 1))]


def core_sums(keep, send):
    other = swap(send, 1)
    sums = [keep[j].astype(f32) + other[j].astype(f32) for j in range(UNITS // 2)]
    return [sums[0]] + [s.astype(bf16) for s in sums[1:]]


def to_plane(two, four, six):
    return [swap(two, 2), swap(four, 4), swap(six, 6)]


def plane_sums(own, two, four, six):
    return (own + two.astype(f32)) + (four.astype(f32) + six.astype(f32))


def add_up(value):
    bits = 1
    while bits < lax.axis_size("dp"):
        value = value + swap(value, bits)
        bits *= 2
    return value


def document_tables(doc_starts):
    rows = doc_starts.shape[1]
    is_live = doc_starts < rows
    live = jnp.sum(is_live.astype(jnp.int32), axis=1) // TILE
    positions = jnp.where(is_live, jnp.arange(rows) - doc_starts, 0).astype(f32)
    frequency = rope_base ** (-(jnp.arange(HALF, dtype=f32) * 2.0 / HEAD_SIZE))
    angles = frequency[None, :, None] * positions[:, None, :]
    cos, sin = jnp.cos(angles), jnp.sin(angles)
    st_row = doc_starts.astype(f32)[:, None, :]
    return live, cos, sin, st_row


def local(tokens, doc_starts, cotangent, master, moment_one, moment_two):
    size = lax.axis_size("dp")
    me = lax.axis_index("dp")
    z = plane(me)
    buffers, rows = tokens.shape[:2]
    shard = master.shape[0] // LANES
    total = 4 * UNITS * UNIT
    by_units = size == 4 * UNITS and shard == UNIT + 1
    own_rows = master.reshape(shard, LANES)
    if by_units:
        own = me % UNITS
        before = lax.ppermute(own_rows[shard - size :], "dp", [(i, i + 1) for i in range(size - 1)])
        unit = lax.dynamic_slice_in_dim(jnp.concatenate([before, own_rows], axis=0), size - me, UNIT).astype(bf16)
        gain_at = total - (size - 1) * shard
        gain_rows = own_rows[gain_at : gain_at + GAIN_ROWS].astype(bf16)
        rows_here = jnp.concatenate([unit, jnp.where(me == size - 1, gain_rows, jnp.zeros_like(gain_rows))], axis=0)
        rows_here, unit, doc_starts = lax.optimization_barrier((rows_here, unit, doc_starts))
        live, cos, sin, st_row = document_tables(doc_starts)
        later, live = lax.optimization_barrier((unit, live))
        last = size // UNITS - 1
        head = jnp.concatenate([jnp.where(z == 0, rows_here[:UNIT], jnp.zeros_like(unit)), rows_here[UNIT:]], axis=0)
        arrived = []
        for far in (3, 2, 1):
            pairs = [(k, far * UNITS + k) for k in range(UNITS)] + [(size - 1, (last - far) * UNITS + UNITS - 1)]
            arrived.append(lax.ppermute(head, "dp", pairs))
        planes = [unit]
        for far in (1, 2, 3):
            pairs = [(i, i ^ (far * UNITS)) for i in range(size) if plane(i) > 0]
            planes.append(lax.ppermute(later, "dp", pairs))
        head = (head + arrived[0]) + (arrived[1] + arrived[2])
        around = [swap(head, bits) for bits in (2, 4, 6)]
        units = jnp.stack(with_partners([head, *around]))
        units, *planes = lax.optimization_barrier((units, *planes))
        rest = jnp.stack([pick(planes, z ^ p) for p in (1, 2, 3)])
        rest_around = [swap(rest, bits) for bits in (2, 4, 6)]
    else:
        live, cos, sin, st_row = document_tables(doc_starts)
        own = jnp.zeros_like(me)
        all_rows = lax.all_gather(own_rows.astype(bf16), "dp", axis=0, tiled=True)
        units = all_rows[: UNITS * UNIT].reshape(UNITS, UNIT, LANES)
        gain_rows = jnp.pad(all_rows[None, total : total + GAIN_ROWS], ((UNITS - 1, 0), (0, 0), (0, 0)))
        units = jnp.concatenate([units, gain_rows], axis=1)
        late_units = all_rows[UNITS * UNIT : total].reshape(3, UNITS, UNIT, LANES)
        late_units = [late_units[:, k] for k in range(UNITS)]
    own = own.astype(jnp.int32).reshape(1)

    tok_t, cot_t = tokens.transpose(0, 2, 1), cotangent.transpose(0, 2, 1)

    qk_t, kv, mix_t, hidden, lse, w, wo, gains = run_attention_forward(live, own, tok_t, st_row, cos, sin, units)
    if by_units:
        hidden, *rest_around = lax.optimization_barrier((hidden, *rest_around))
        late_units = with_partners([rest, *rest_around])
    layer, hgrad, keep, send, dgain_two = run_mlp(live, own, hidden, cot_t, st_row, gains, late_units)
    shared = (live, own, hgrad, tok_t, qk_t, kv, mix_t, lse, st_row, cos, sin, w, wo, gains)
    igrad, dw_t, dwo, dgain = run_attention_backward(0, buffers // 2, *shared)
    if by_units:
        late = core_sums(keep, send)
        dgain, *late = lax.optimization_barrier((dgain, *late))
        arrived = to_plane(*late[1:])
    igrad, keep_early, send_early = run_attention_backward(
        buffers // 2, buffers, *shared, so_far=(dgain_two, dw_t, dwo, dgain, igrad)
    )
    if by_units:
        keep_early, send_early, *arrived = lax.optimization_barrier((keep_early, send_early, *arrived))
        late_sum = plane_sums(late[0], *arrived)
        mine = lax.dynamic_index_in_dim(late_sum, jnp.maximum(z - 1, 0), 0, keepdims=False)
        sent = [
            lax.dynamic_index_in_dim(late_sum, jnp.maximum((z ^ far) - 1, 0), 0, keepdims=False).astype(bf16)
            for far in (1, 2, 3)
        ]
        send_early, *sent = lax.optimization_barrier((send_early, *sent))
        for far in (1, 2, 3):
            pairs = [(i, i ^ (far * UNITS)) for i in range(size) if plane(i ^ (far * UNITS)) > 0]
            sent[far - 1] = lax.ppermute(sent[far - 1], "dp", pairs)
        early = core_sums(keep_early, send_early)
        arrived = to_plane(*early[1:])
        sent_and_arrived = lax.optimization_barrier((*sent, *arrived))
        sent, arrived = sent_and_arrived[:3], sent_and_arrived[3:]
        for piece in sent:
            mine = mine + piece.astype(f32)
        early_sum = plane_sums(early[0], *arrived)
        early_low = early_sum.astype(bf16)
        for far in (1, 2, 3):
            pairs = [(far * UNITS + k, k) for k in range(UNITS)]
            pairs += [((last ^ far) * UNITS + UNITS - 1, size - 1)]
            early_sum = early_sum + lax.ppermute(early_low, "dp", pairs).astype(f32)
        unit_grad = jnp.where(z == 0, early_sum[:UNIT], mine)
        gain_grads = jnp.where(me == size - 1, early_sum[UNIT:], 0.0)
        square_sum = jnp.sum(unit_grad * unit_grad) + jnp.sum(gain_grads * gain_grads)
        square_sum = add_up(jnp.broadcast_to(square_sum, (8, LANES)))[0, 0]
        after = lax.ppermute(unit_grad[:size], "dp", [(i + 1, i) for i in range(size - 1)])
        after = after + jnp.pad(gain_grads, ((0, size - GAIN_ROWS), (0, 0)))
        grad_shard = lax.dynamic_slice_in_dim(jnp.concatenate([unit_grad, after], axis=0), me, shard).reshape(-1)
    else:
        early = jnp.stack([keep_early, send_early], axis=1).reshape(UNITS, UNIT + GAIN_ROWS, LANES)
        late = jnp.stack([keep, send], axis=1).reshape(UNITS, 3, UNIT, LANES)
        pieces = [early[:, :UNIT].reshape(-1, LANES)] + [late[:, p].reshape(-1, LANES) for p in range(3)]
        grads = jnp.concatenate(pieces + [early[UNITS - 1, UNIT:]], axis=0).astype(f32)
        grads = jnp.pad(grads, ((0, size * shard - grads.shape[0]), (0, 0)))
        grad_shard = lax.psum_scatter(grads.reshape(-1), "dp", scatter_dimension=0, tiled=True)
        square_sum = lax.psum(jnp.sum(grad_shard * grad_shard), "dp")
    grad_norm = jnp.sqrt(square_sum)
    clipped = grad_shard * (clip_norm / jnp.maximum(grad_norm, clip_norm))
    new_one = decay_one * moment_one + (1.0 - decay_one) * clipped
    new_two = decay_two * moment_two + (1.0 - decay_two) * clipped * clipped
    corrected_one = new_one / (1.0 - decay_one**STEP)
    corrected_two = new_two / (1.0 - decay_two**STEP)
    new_master = master - learn_rate * (
        corrected_one / (jnp.sqrt(corrected_two) + adam_eps) + weight_decay * master
    )
    return (layer.transpose(0, 2, 1), igrad.transpose(0, 2, 1), grad_shard, grad_norm, new_master, new_one, new_two)


def solution(mesh):
    flat, cube = P("dp"), P("dp", None, None)
    return jax.shard_map(
        local,
        mesh=mesh,
        in_specs=(cube, P("dp", None), cube, flat, flat, flat),
        out_specs=(cube, cube, flat, P(), flat, flat, flat),
        check_vma=False,
    )
```
